128 devices in a mesh: row: 8 (over y_lo, z), col: 16 (over y_hi, x, core).
Axes of the slice: x: 4, y: 4 (y_hi: 2, y_lo: 2; y = y_hi * 2 + y_lo), z: 4, core: 2. Of those that a mesh axis runs over, the one named last changes fastest.
Arguments:
- species: float32 [53, 64, 128, 256], P(None, 'row', 'col'), may hold values from 0.05 to 2
- velocity: float32 [3, 64, 128, 256], P(None, 'row', 'col'), may hold values from -1 to 1
- diffusivity: float32 [53], replicated, may hold values from 0.02 to 0.1
- divergence: float32 [64, 128, 256], P('row', 'col'), may hold values from -6 to 6
- log_rates: float32 [325], replicated, may hold values from -3 to 1
- reactants: int32 [325, 53], replicated, may hold values from 0 to 3, as said below
- products: int32 [325, 53], replicated, may hold values from 0 to 3, as said below
- heat_weights: float32 [53], replicated, may hold values from -0.875 to 0.875
- substeps: int32 [64, 128, 2], P('row', 'col'), may hold values from 1 to 6
Outputs:
- reacted: float32 [53, 64, 128, 256], P(None, 'row', 'col')
- pressure: float32 [64, 128, 256], P('row', 'col')
The draws below stay inside these ranges and needn't reach their ends.
Inputs may be any that keep to these rules, and one draw needn't show every extreme that they name: `reactants`: each reaction has one or two reactant species. `products`: each reaction has one or two product species.
All inputs are finite; a program needn't handle non-finite values.
Results may differ from the reference program's by a relative error of at most 0.0003.
Values sent between devices are 32-bit elements; how exact they have to be, the bound alone decides.
A program may use at most 128 MiB of HBM per device.

```python
import math
import jax
import jax.numpy as jnp
from jax import lax

NS = 53
NR = 325
NZ = 256
BLOCK = 128
MAXSUB = 6
NX = 64
NY = 128


def stoich_matrix(key):
    key_first, key_second, key_lead, key_extra = jax.random.split(key, 4)
    first = jax.random.randint(key_first, (NR,), 0, NS)
    second = jax.random.randint(key_second, (NR,), 0, NS)
    lead_coef = jax.random.randint(key_lead, (NR,), 1, 3)
    extra_coef = jax.random.randint(key_extra, (NR,), 0, 2)
    columns = jnp.arange(NS, dtype=jnp.int32)
    matrix = lead_coef[:, None] * (columns[None, :] == first[:, None]).astype(jnp.int32)
    matrix = matrix + extra_coef[:, None] * (columns[None, :] == second[:, None]).astype(jnp.int32)
    return matrix.astype(jnp.int32)


def draw_reactants(key, part):
    return stoich_matrix(jax.random.fold_in(key, 11))


def draw_products(key, part):
    return stoich_matrix(jax.random.fold_in(key, 23))


def draw_substeps(key, part):
    own_key = jax.random.fold_in(key, 37)
    key_front, key_heavy, key_light = jax.random.split(own_key, 3)
    front_start = jax.random.randint(key_front, (), 0, NX)
    position = jnp.arange(NX, dtype=jnp.int32)
    distance = jnp.mod(position - front_start, NX)
    inside = (distance < NX // 4)[:, None, None]
    heavy = jax.random.randint(key_heavy, (NX, NY, NZ // BLOCK), 4, 7)
    light = jax.random.randint(key_light, (NX, NY, NZ // BLOCK), 1, 3)
    return jnp.where(inside, heavy, light).astype(jnp.int32)


def block_scale(key, dims, cuts, least, high):
    def one(dim, shards_of):
        heights = jax.random.uniform(jax.random.fold_in(jax.random.fold_in(key, 6), dim), (shards_of,), jnp.float32, least / len(cuts), high / len(cuts))
        return jnp.repeat(jnp.exp(heights), dims[dim] // shards_of).reshape((-1,) + (1,) * (len(dims) - dim - 1))

    level = one(*cuts[0])
    for cut in cuts[1:]:
        level = level * one(*cut)
    return level


def scatter_about(stream_key, shape, width, reach, cuts=(), held_as=jnp.bfloat16):
    drawn = jax.random.normal(stream_key, shape, jnp.float32) * width
    if len(cuts) > 0:
        drawn = block_scale(stream_key, shape, cuts, -0.22, 0.18) * drawn
    return jnp.clip(drawn, min=-reach, max=reach).astype(held_as)


def setup_inputs(seed: int = 0) -> dict:
    key_of = jax.random.split(jax.random.key(seed), 10)
    return {
        "species": jnp.clip(jnp.exp(math.log(2.0) - 3.6888794 * jax.random.uniform(key_of[0], (NS, NX, NY, NZ), jnp.float32) ** block_scale(key_of[0], (NS, NX, NY, NZ), ((1, 8), (2, 16)), -0.2, 0.2)), 0.05, 2.0),
        "velocity": jnp.clip(jax.random.uniform(key_of[1], (3, NX, NY, NZ), jnp.float32, -1.0, 1.0) * block_scale(key_of[1], (3, NX, NY, NZ), ((1, 8), (2, 16)), -0.4, 0.0), -1.0, 1.0),
        "diffusivity": jnp.clip(jnp.exp(jax.random.uniform(key_of[2], (NS,), jnp.float32, math.log(0.02), math.log(0.1))), 0.02, 0.1),
        "divergence": scatter_about(key_of[3], (NX, NY, NZ), 1.0, 6.0, ((0, 8), (1, 16)), jnp.float32),
        "log_rates": jnp.clip(jax.random.uniform(key_of[4], (NR,), jnp.float32, -3.0, 1.0), -3.0, 1.0),
        "reactants": draw_reactants(jax.random.fold_in(key_of[9], 71), 0),
        "products": draw_products(jax.random.fold_in(key_of[9], 71), 0),
        "heat_weights": scatter_about(key_of[7], (NS,), NS ** -0.5, 0.875, (), jnp.float32),
        "substeps": draw_substeps(jax.random.fold_in(key_of[9], 71), 0),
    }


time_step = 0.2
screen = 0.004
highest = lax.Precision.HIGHEST

def cosine_table(length):
    wave = jnp.arange(length, dtype=jnp.float32)
    sample = jnp.arange(length, dtype=jnp.float32) + 0.5
    weight = jnp.where(wave == 0, jnp.sqrt(1.0 / length), jnp.sqrt(2.0 / length)).astype(jnp.float32)
    return weight[:, None] * jnp.cos(jnp.pi * wave[:, None] * sample[None, :] / length)

def mode_values(length):
    wave = jnp.arange(length, dtype=jnp.float32)
    return 2.0 - 2.0 * jnp.cos(jnp.pi * wave / length)

def transport(centre, padded, velocity, diffusivity):
    x_minus = padded[:, :-2, 1:-1, 1:-1]
    x_plus = padded[:, 2:, 1:-1, 1:-1]
    y_minus = padded[:, 1:-1, :-2, 1:-1]
    y_plus = padded[:, 1:-1, 2:, 1:-1]
    z_minus = padded[:, 1:-1, 1:-1, :-2]
    z_plus = padded[:, 1:-1, 1:-1, 2:]
    lateral = x_minus + x_plus + (y_minus + y_plus) + (z_minus + z_plus) - 6.0 * centre
    upwind = jnp.maximum(velocity, 0.0)[:, None]
    downwind = jnp.minimum(velocity, 0.0)[:, None]
    carried = upwind[0] * (centre - x_minus) + downwind[0] * (x_plus - centre)
    carried = carried + upwind[1] * (centre - y_minus) + downwind[1] * (y_plus - centre)
    carried = carried + upwind[2] * (centre - z_minus) + downwind[2] * (z_plus - centre)
    return centre + time_step * (diffusivity[:, None, None, None] * lateral - carried)

def react_step(conc, step_size, log_rates, react_float, prod_float):
    rates = jnp.exp(log_rates[:, None] + jnp.dot(react_float, jnp.log(conc), precision=highest, preferred_element_type=jnp.float32))
    gained = jnp.dot(prod_float.T, rates, precision=highest, preferred_element_type=jnp.float32)
    lost = jnp.dot(react_float.T, rates, precision=highest, preferred_element_type=jnp.float32)
    return conc * (conc + step_size * gained) / (conc + step_size * lost)

def reference(species, velocity, diffusivity, divergence, log_rates, reactants, products, heat_weights, substeps):
    padded = jnp.pad(species, ((0, 0), (1, 1), (1, 1), (1, 1)), mode='edge')
    moved = transport(species, padded, velocity, diffusivity)
    react_float = reactants.astype(jnp.float32)
    prod_float = products.astype(jnp.float32)
    per_cell = jnp.broadcast_to(substeps[:, :, :, None], (NX, NY, NZ // BLOCK, BLOCK)).reshape(NX, NY * NZ)
    step_cells = time_step / per_cell.astype(jnp.float32)
    stacked = jnp.transpose(moved.reshape(NS, NX, NY * NZ), (1, 0, 2))

    def one_slice(packed):
        conc, counts, sizes = packed
        for level in range(MAXSUB):
            fresh = react_step(conc, sizes[None, :], log_rates, react_float, prod_float)
            conc = jnp.where(counts[None, :] > level, fresh, conc)
        return conc
    result = lax.map(one_slice, (stacked, per_cell, step_cells))
    reacted = jnp.transpose(result, (1, 0, 2)).reshape(NS, NX, NY, NZ)
    heat = jnp.einsum('s,sxyz->xyz', heat_weights, reacted - moved, precision=highest) / time_step
    source = divergence - heat
    table_x = cosine_table(NX)
    table_y = cosine_table(NY)
    table_z = cosine_table(NZ)
    spectrum = jnp.einsum('cz,xyz->xyc', table_z, source, precision=highest)
    spectrum = jnp.einsum('ax,xyc->ayc', table_x, spectrum, precision=highest)
    spectrum = jnp.einsum('by,ayc->abc', table_y, spectrum, precision=highest)
    denominator = screen + mode_values(NX)[:, None, None] + mode_values(NY)[None, :, None] + mode_values(NZ)[None, None, :]
    spectrum = spectrum / denominator
    spectrum = jnp.einsum('by,abc->ayc', table_y, spectrum, precision=highest)
    spectrum = jnp.einsum('ax,ayc->xyc', table_x, spectrum, precision=highest)
    pressure = jnp.einsum('cz,xyc->xyz', table_z, spectrum, precision=highest)
    return (reacted, pressure)
```

```python
import functools
import math

import jax
import jax.numpy as jnp
from jax import lax
from jax.experimental import pallas as pl
from jax.experimental.pallas import tpu as pltpu
from jax.sharding import Mesh
from jax.sharding import PartitionSpec as P

BLOCK = 128
ROW = ("row_0", "row_1")
COL = ("col_0", "col_1", "col_2")
ROW_COL = ("row_0", "row_1", "col_0", "col_1", "col_2")
time_step = 0.2
screen = 0.004
highest = lax.Precision.HIGHEST

NS, NR = 53, 325
SP, RP = 56, 336
LOG2E = 1.4426950408889634
f32, bf16 = jnp.float32, jnp.bfloat16

def split3(x):
    hi = lax.reduce_precision(x, 8, 7)
    mid = lax.reduce_precision(x - hi, 8, 7)
    return hi, mid, x - hi - mid

def matrices(log_rates, reactants, products):
    rf = reactants.astype(f32)
    pf = products.astype(f32)
    bias = jnp.stack(split3(log_rates * LOG2E), axis=1)
    first = jnp.concatenate([rf, bias, rf, jnp.zeros((NR, 3), f32)], axis=1)
    first = jnp.pad(first, ((0, RP - NR), (0, 0))).astype(bf16)
    half = jnp.concatenate([jnp.pad(pf, ((0, RP - NR), (0, 3))), jnp.pad(rf, ((0, RP - NR), (0, 3)))], axis=1).T
    second = jnp.concatenate([half, half], axis=1).astype(bf16)
    return first, second

def kernel(G, first_flag_ref, counts_ref, sp_ref, xlo_ref, xhi_ref, ylo_ref, yhi_ref, vel_ref, diff_ref, heat_ref, div_ref, hrow_ref, nrow_ref,
           s1_ref, s2_ref, out_ref, src_ref, sp, hx, ext, mov, cur, outs, order_ref, hist_ref, sem):
    copies = []
    for z in range(2):
        c = pltpu.make_async_copy(sp_ref.at[:, pl.ds(z * 128, 128)], sp.at[z], sem.at[z])
        c.start(); copies.append(c)
    for k, r in enumerate((xlo_ref, xhi_ref, ylo_ref, yhi_ref)):
        for z in range(2):
            c = pltpu.make_async_copy(r.at[:, pl.ds(z * 128, 128)], hx.at[k, z], sem.at[2 + 2 * k + z])
            c.start(); copies.append(c)
    for k in range(8):
        hist_ref[k] = 0
    def count(i, _):
        n = counts_ref[i]
        hist_ref[n] = hist_ref[n] + 1
        return 0
    lax.fori_loop(0, 128, count, 0)
    base = jnp.int32(0)
    for n in range(6, 0, -1):
        here = hist_ref[n]
        hist_ref[n] = base
        base = base + here
    def place(i, _):
        n = counts_ref[i]
        at = hist_ref[n]
        order_ref[at] = i
        hist_ref[n] = at + 1
        return 0
    lax.fori_loop(0, 128, place, 0)
    for c in copies:
        c.wait()

    pad = jnp.full((SP - NS, 128), 2.0, f32)
    def lay(c, _):
        x = c // 8
        y = c % 8
        for z in range(2):
            ext[(x + 1) * 10 + y + 1, :NS, z * 128:(z + 1) * 128] = sp[z, pl.ds(c, NS, stride=64), :]
        return 0
    lax.fori_loop(0, 64, lay, 0)
    def edge(c, _):
        for k, at, own in ((0, c + 1, 10 + c + 1), (1, 90 + c + 1, 80 + c + 1), (2, (c + 1) * 10, (c + 1) * 10 + 1), (3, (c + 1) * 10 + 9, (c + 1) * 10 + 8)):
            flag = first_flag_ref[k]
            for z in range(2):
                zs = slice(z * 128, (z + 1) * 128)
                @pl.when(flag == 0)
                def _():
                    ext[at, :NS, zs] = hx[k, z, pl.ds(c, NS, stride=8), :]
                @pl.when(flag != 0)
                def _():
                    ext[at, :NS, zs] = ext[own, :NS, zs]
        return 0
    lax.fori_loop(0, 8, edge, 0)

    diff = jnp.broadcast_to(diff_ref[...], (SP, 256))
    lane = lax.broadcasted_iota(jnp.int32, (SP, 256), 1)
    row = lax.broadcasted_iota(jnp.int32, (SP, 256), 0)
    def move(c, _):
        x = c // 8
        y = c % 8
        e = (x + 1) * 10 + y + 1
        centre = ext[e]
        xm, xp, ym, yp = ext[e - 10], ext[e + 10], ext[e - 1], ext[e + 1]
        zm = jnp.where(lane == 0, centre, pltpu.roll(centre, 1, 1))
        zp = jnp.where(lane == 255, centre, pltpu.roll(centre, 255, 1))
        lateral = xm + xp + (ym + yp) + (zm + zp) - 6.0 * centre
        carried = None
        for d, (m, p) in enumerate(((xm, xp), (ym, yp), (zm, zp))):
            v = jnp.broadcast_to(vel_ref[d, pl.ds(c, 1), :], (SP, 256))
            t = jnp.maximum(v, 0.0) * (centre - m) + jnp.minimum(v, 0.0) * (p - centre)
            carried = t if carried is None else carried + t
        moved = centre + 0.2 * (diff * lateral - carried)
        moved = jnp.where(row < NS, moved, 2.0)
        mov[2 * c] = moved[:, :128]
        mov[2 * c + 1] = moved[:, 128:]
        return 0
    lax.fori_loop(0, 64, move, 0)

    W = G * 128
    heat = jnp.broadcast_to(heat_ref[...], (SP, 128))
    def turn(t, _):
        ids = [order_ref[t * G + j] for j in range(G)]
        top = counts_ref[ids[0]]
        for j in range(G):
            cur[:, j * 128:(j + 1) * 128] = mov[ids[j]]
        h = jnp.concatenate([hrow_ref[pl.ds(ids[j], 1), :] for j in range(G)], axis=1)
        n = jnp.concatenate([nrow_ref[pl.ds(ids[j], 1), :] for j in range(G)], axis=1)
        hb = jnp.broadcast_to(h, (SP, W))
        nb = jnp.broadcast_to(n, (SP, W))
        def level(k, _):
            conc = cur[...]
            lg = jnp.log2(conc)
            hi = lg.astype(bf16).astype(f32)
            xin = jnp.concatenate([hi, lg - hi], axis=0).astype(bf16)
            rates = jnp.exp2(jnp.dot(s1_ref[...], xin, preferred_element_type=f32))
            rhi = rates.astype(bf16)
            rlo = (rates - rhi.astype(f32)).astype(bf16)
            both = jnp.dot(s2_ref[...], jnp.concatenate([rhi, rlo], axis=0), preferred_element_type=f32)
            gained, lost = both[:SP], both[SP:]
            fresh = conc * (conc + hb * gained) / (conc + hb * lost)
            cur[...] = jnp.where(nb > k, fresh, conc)
            return 0
        lax.fori_loop(0, top, level, 0)
        for j in range(G):
            c = ids[j] // 2
            z = ids[j] % 2
            res = cur[:, j * 128:(j + 1) * 128]
            outs[z, pl.ds(c, NS, stride=64), :] = res[:NS]
            gain = jnp.sum(heat * (res - mov[ids[j]]), axis=0, keepdims=True)
            src_ref[pl.ds(ids[j], 1), :] = div_ref[pl.ds(ids[j], 1), :] - gain / 0.2
        return 0
    lax.fori_loop(0, 128 // G, turn, 0)
    copies = []
    for z in range(2):
        c = pltpu.make_async_copy(outs.at[z], out_ref.at[:, pl.ds(z * 128, 128)], sem.at[z])
        c.start(); copies.append(c)
    for c in copies:
        c.wait()

def call(G, flags, counts, species, faces, velocity, diffusivity, heat_weights, divergence, first, second):
    hrow = jnp.broadcast_to((0.2 / counts.astype(f32))[:, None], (128, 128))
    nrow = jnp.broadcast_to(counts[:, None], (128, 128))
    vm = pl.BlockSpec(memory_space=pltpu.VMEM)
    sm = pl.BlockSpec(memory_space=pltpu.SMEM)
    hb = pl.BlockSpec(memory_space=pl.ANY)
    out, src = pl.pallas_call(
        functools.partial(kernel, G),
        out_shape=(jax.ShapeDtypeStruct((NS * 64, 256), f32), jax.ShapeDtypeStruct((128, 128), f32)),
        in_specs=[sm, sm, hb, hb, hb, hb, hb] + [vm] * 8,
        out_specs=(hb, vm),
        scratch_shapes=[
            pltpu.VMEM((2, NS * 64, 128), f32), pltpu.VMEM((4, 2, NS * 8, 128), f32), pltpu.VMEM((100, SP, 256), f32), pltpu.VMEM((128, SP, 128), f32),
            pltpu.VMEM((SP, G * 128), f32), pltpu.VMEM((2, NS * 64, 128), f32), pltpu.SMEM((128,), jnp.int32), pltpu.SMEM((8,), jnp.int32), pltpu.SemaphoreType.DMA((10,))],
        compiler_params=pltpu.CompilerParams(vmem_limit_bytes=50 << 20),
        name="transport_kinetics",
    )(flags, counts, species.reshape(NS * 64, 256), *[f.reshape(NS * 8, 256) for f in faces], velocity.reshape(3, 64, 256),
      jnp.pad(diffusivity, (0, SP - NS))[:, None], jnp.pad(heat_weights, (0, SP - NS))[:, None], divergence.reshape(128, 128), hrow, nrow, first, second)
    return out.reshape(NS, 8, 8, 256), src.reshape(64, 256)


def split_up(x, dim, size):
    before, after = (x.shape[:dim], x.shape[dim + 1 :])
    return jnp.moveaxis(x.reshape(*before, size, -1, *after), dim, 0)


def joined_along(parts, dim):
    shape = list(parts.shape[1:])
    shape[dim] *= parts.shape[0]
    return jnp.moveaxis(parts, 0, dim).reshape(shape)


def turned_blocks(parts, axes, turns):
    inside = parts.shape[1:]
    result = parts.reshape(*(lax.axis_size(a) for a in axes), *inside)
    for k in turns:
        result = lax.all_to_all(result, axes[k], k, k, tiled=True)
    return result.reshape(-1, *inside)


def core_and_chips(x, groups, turns, split_dim, concat_dim):
    size = lax.axis_size(groups[0]) * lax.axis_size(groups[1])
    parts = split_up(x, split_dim, size)
    return joined_along(turned_blocks(parts, groups, turns), concat_dim)


def cosine_table(length):
    wave = jnp.arange(length, dtype=jnp.float32)
    sample = jnp.arange(length, dtype=jnp.float32) + 0.5
    weight = jnp.where(wave == 0, jnp.sqrt(1.0 / length), jnp.sqrt(2.0 / length)).astype(
        jnp.float32
    )
    return weight[:, None] * jnp.cos(jnp.pi * wave[:, None] * sample[None, :] / length)


def mode_values(length):
    wave = jnp.arange(length, dtype=jnp.float32)
    return 2.0 - 2.0 * jnp.cos(jnp.pi * wave / length)


def faces_of(x, axis, dim):
    size = lax.axis_size(axis)
    up = [(i, (i + 1) % size) for i in range(size - 1)]
    last = lax.index_in_dim(x, x.shape[dim] - 1, dim, keepdims=False)
    leading = lax.index_in_dim(x, 0, dim, keepdims=False)
    return lax.ppermute(last, axis, up), lax.ppermute(leading, axis, [(b, a) for a, b in up])


def local(species, velocity, diffusivity, divergence, log_rates, reactants, products, heat_weights, substeps):
    species_count, cells_x, cells_y, cells_z = species.shape
    rows_count = lax.axis_size(ROW)
    cols_count = lax.axis_size(COL)
    device_count = rows_count * cols_count
    x_low, x_high = faces_of(species, ROW, 1)
    y_low, y_high = faces_of(species, COL, 2)
    at_row, at_col = lax.axis_index(ROW), lax.axis_index(COL)
    flags = jnp.stack([at_row == 0, at_row == rows_count - 1, at_col == 0, at_col == cols_count - 1]).astype(jnp.int32)
    first, second = matrices(log_rates, reactants, products)
    reacted, source = call(8, flags, substeps.reshape(-1), species, (x_low, x_high, y_low, y_high), velocity, diffusivity, heat_weights, divergence, first, second)
    source = source.reshape(cells_x, cells_y, cells_z)
    table_z = cosine_table(cells_z)
    forward = jnp.einsum("kz,xyz->kxy", table_z, source, precision=highest).reshape(
        cells_z, cells_x * cells_y
    )
    planes = core_and_chips(forward, (("row_0", "row_1", "col_0", "col_1"), "col_2"), (0, 1), 0, 1)
    depth = cells_z // device_count
    planes = planes.reshape(depth, rows_count, cols_count, cells_x, cells_y)
    table_x = cosine_table(rows_count * cells_x).reshape(rows_count * cells_x, rows_count, cells_x)
    table_y = cosine_table(cols_count * cells_y).reshape(cols_count * cells_y, cols_count, cells_y)
    spectrum = jnp.einsum("ari,zrcij->zacj", table_x, planes, precision=highest)
    spectrum = jnp.einsum("bcj,zacj->zab", table_y, spectrum, precision=highest)
    device_index = lax.axis_index(ROW) * cols_count + lax.axis_index(COL)
    z_values = lax.dynamic_slice_in_dim(mode_values(cells_z), device_index * depth, depth, 0)
    denominator = (
        screen
        + z_values[:, None, None]
        + mode_values(rows_count * cells_x)[None, :, None]
        + mode_values(cols_count * cells_y)[None, None, :]
    )
    spectrum = spectrum / denominator
    spectrum = jnp.einsum("bcj,zab->zacj", table_y, spectrum, precision=highest)
    spectrum = jnp.einsum("ari,zacj->zrcij", table_x, spectrum, precision=highest)
    outgoing = spectrum.reshape(depth, device_count * cells_x * cells_y)
    columns = lax.all_to_all(outgoing, ROW_COL, split_axis=1, concat_axis=0, tiled=True)
    columns = columns.reshape(cells_z, cells_x, cells_y)
    pressure = jnp.einsum("kz,kxy->xyz", table_z, columns, precision=highest)
    return (reacted, pressure)


def solution(mesh):
    finer = Mesh(mesh.devices.reshape(2, 4, 2, 4, 2), ("row_0", "row_1", "col_0", "col_1", "col_2"))
    in_specs = (
        P(None, ROW, COL, None),
        P(None, ROW, COL, None),
        P(),
        P(ROW, COL, None),
        P(),
        P(),
        P(),
        P(),
        P(ROW, COL, None),
    )
    out_specs = (P(None, ROW, COL, None), P(ROW, COL, None))
    return jax.shard_map(local, mesh=finer, in_specs=in_specs, out_specs=out_specs, check_vma=False)
```

```python
import functools

import jax
import jax.numpy as jnp
import numpy as np
from jax import lax
from jax.experimental import pallas as pl
from jax.experimental.pallas import tpu as pltpu
from jax.sharding import PartitionSpec as P

f32, bf16 = jnp.float32, jnp.bfloat16
MESH = pl.DeviceIdType.MESH
NS, SP = 53, 56
NR, RP = 325, 336
LOG2E = 1.4426950408889634
time_step = 0.2
screen = 0.004
highest = lax.Precision.HIGHEST

def advance_kernel(species, vel_hbm, diff_hbm, mov_ref, sp, hx, ext, mv, vel_ref, diff_ref, sem_in, ss, rs, sem_out):
    rows, cols = lax.axis_size("row"), lax.axis_size("col")
    me_r, me_c = lax.axis_index("row"), lax.axis_index("col")
    above = {"row": lax.rem(me_r + 1, rows), "col": me_c}
    below = {"row": lax.rem(me_r + rows - 1, rows), "col": me_c}
    right = {"row": me_r, "col": lax.rem(me_c + 1, cols)}
    left = {"row": me_r, "col": lax.rem(me_c + cols - 1, cols)}
    barrier = pltpu.get_barrier_semaphore()
    for peer in (above, below, right, left):
        pl.semaphore_signal(barrier, inc=1, device_id=peer, device_id_type=MESH)
    loads = [pltpu.make_async_copy(species.at[:, :, pl.ds(z * 128, 128)], sp.at[z], sem_in.at[z]) for z in range(2)]
    loads += [pltpu.make_async_copy(vel_hbm, vel_ref, sem_in.at[2]), pltpu.make_async_copy(diff_hbm, diff_ref, sem_in.at[3])]
    for c in loads:
        c.start()
    pl.semaphore_wait(barrier, 4)
    x_copies = []
    for z in range(2):
        zs = pl.ds(z * 128, 128)
        x_copies.append(pltpu.make_async_remote_copy(src_ref=species.at[:, pl.ds(56, 8), zs], dst_ref=hx.at[0, z], send_sem=ss.at[2 + z], recv_sem=rs.at[2 + z], device_id=above, device_id_type=MESH))
        x_copies.append(pltpu.make_async_remote_copy(src_ref=species.at[:, pl.ds(0, 8), zs], dst_ref=hx.at[1, z], send_sem=ss.at[4 + z], recv_sem=rs.at[4 + z], device_id=below, device_id_type=MESH))
    for c in x_copies:
        c.start()
    for c in loads:
        c.wait()

    def lay(x, y):
        c = x * 8 + y
        for z in range(2):
            ext[x + 1, y + 1, :NS, z * 128:(z + 1) * 128] = sp_rows(z, c)

    def sp_rows(z, c):
        return sp.at[z].reshape(NS * 64, 128)[pl.ds(c, NS, stride=64), :]

    def lay_edge(x, _):
        lay(x, 0)
        lay(x, 7)
        return 0
    lax.fori_loop(0, 8, lay_edge, 0)
    y_up = pltpu.make_async_remote_copy(src_ref=ext.at[pl.ds(1, 8), 8], dst_ref=ext.at[pl.ds(1, 8), 0], send_sem=ss.at[0], recv_sem=rs.at[0], device_id=right, device_id_type=MESH)
    y_down = pltpu.make_async_remote_copy(src_ref=ext.at[pl.ds(1, 8), 1], dst_ref=ext.at[pl.ds(1, 8), 9], send_sem=ss.at[1], recv_sem=rs.at[1], device_id=left, device_id_type=MESH)
    y_up.start()
    y_down.start()

    def lay_inner(x, _):
        for y in range(1, 7):
            lay(x, y)
        return 0
    lax.fori_loop(0, 8, lay_inner, 0)

    own = lax.broadcasted_iota(jnp.int32, (SP, NS), 0) == lax.broadcasted_iota(jnp.int32, (SP, NS), 1)
    fifth = jnp.broadcast_to(0.2 * jnp.sum(jnp.where(own, diff_ref[...], 0.0), axis=1, keepdims=True), (SP, 256))
    lane = lax.broadcasted_iota(jnp.int32, (SP, 256), 1)
    row = lax.broadcasted_iota(jnp.int32, (SP, 256), 0)

    def move(x, y):
        c = x * 8 + y
        centre = ext[x + 1, y + 1]
        near = (ext[x, y + 1], ext[x + 2, y + 1], ext[x + 1, y], ext[x + 1, y + 2],
                jnp.where(lane == 0, centre, pltpu.roll(centre, 1, 1)), jnp.where(lane == 255, centre, pltpu.roll(centre, 255, 1)))
        speeds = [0.2 * vel_ref[d, pl.ds(c, 1), :] for d in range(3)]
        still = 1.0 - (jnp.abs(speeds[0]) + jnp.abs(speeds[1]) + jnp.abs(speeds[2]))
        total = centre * (still - 6.0 * fifth)
        for d in range(3):
            total = total + near[2 * d] * (fifth + jnp.maximum(speeds[d], 0.0))
            total = total + near[2 * d + 1] * (fifth - jnp.minimum(speeds[d], 0.0))
        total = jnp.where(row < NS, total, 2.0)
        mv[2 * c] = total[:, :128]
        mv[2 * c + 1] = total[:, 128:]

    def inner(x, _):
        def go(y, _):
            move(x, y)
            return 0
        return lax.fori_loop(1, 7, go, 0)
    lax.fori_loop(1, 7, inner, 0)
    y_up.wait()
    y_down.wait()

    @pl.when(me_c == 0)
    def _():
        ext[pl.ds(1, 8), 0] = ext[pl.ds(1, 8), 1]

    @pl.when(me_c == cols - 1)
    def _():
        ext[pl.ds(1, 8), 9] = ext[pl.ds(1, 8), 8]

    def sides(x, _):
        move(x, 0)
        move(x, 7)
        return 0
    lax.fori_loop(1, 7, sides, 0)
    middle = pltpu.make_async_copy(mv.at[pl.ds(16, 96)], mov_ref.at[pl.ds(16, 96)], sem_out.at[0])
    middle.start()
    for c in x_copies:
        c.wait()

    def lay_halo(y, _):
        for k, at in ((0, 0), (1, 9)):
            for z in range(2):
                ext[at, y + 1, :NS, z * 128:(z + 1) * 128] = hx_rows(k, z, y)
        return 0

    def hx_rows(k, z, y):
        return hx.at[k, z].reshape(NS * 8, 128)[pl.ds(y, NS, stride=8), :]
    lax.fori_loop(0, 8, lay_halo, 0)

    @pl.when(me_r == 0)
    def _():
        ext[0, pl.ds(1, 8)] = ext[1, pl.ds(1, 8)]

    @pl.when(me_r == rows - 1)
    def _():
        ext[9, pl.ds(1, 8)] = ext[8, pl.ds(1, 8)]

    def ends(y, _):
        move(0, y)
        move(7, y)
        return 0
    lax.fori_loop(0, 8, ends, 0)
    low = pltpu.make_async_copy(mv.at[pl.ds(0, 16)], mov_ref.at[pl.ds(0, 16)], sem_out.at[1])
    high = pltpu.make_async_copy(mv.at[pl.ds(112, 16)], mov_ref.at[pl.ds(112, 16)], sem_out.at[2])
    low.start()
    high.start()
    middle.wait()
    low.wait()
    high.wait()


def advance(species, velocity, diffusivity):
    hb = pl.BlockSpec(memory_space=pl.ANY)
    dma = pltpu.SemaphoreType.DMA
    return pl.pallas_call(
        advance_kernel,
        out_shape=jax.ShapeDtypeStruct((128, SP, 128), f32),
        in_specs=[hb, hb, hb],
        out_specs=hb,
        scratch_shapes=[pltpu.VMEM((2, NS, 64, 128), f32), pltpu.VMEM((2, 2, NS, 8, 128), f32), pltpu.VMEM((10, 10, SP, 256), f32), pltpu.VMEM((128, SP, 128), f32), pltpu.VMEM((3, 64, 256), f32), pltpu.VMEM((1, NS), f32),
                        dma((4,)), dma((6,)), dma((6,)), dma((3,))],
        compiler_params=pltpu.CompilerParams(collective_id=0, has_side_effects=True, vmem_limit_bytes=28 << 20),
        name="advance",
    )(species.reshape(NS, 64, 256), velocity.reshape(3, 64, 256), diffusivity[None, :])


def split3(x):
    hi = lax.reduce_precision(x, 8, 7)
    mid = lax.reduce_precision(x - hi, 8, 7)
    return hi, mid, x - hi - mid


def matrices(log_rates, reactants, products):
    rf = reactants.astype(f32)
    pf = products.astype(f32)
    bias = jnp.stack(split3(log_rates * LOG2E), axis=1)
    first = jnp.concatenate([rf, bias, rf, jnp.zeros((NR, 3), f32)], axis=1)
    first = jnp.pad(first, ((0, RP - NR), (0, 0))).astype(bf16)
    half = jnp.concatenate([jnp.pad(pf, ((0, RP - NR), (0, 3))), jnp.pad(rf, ((0, RP - NR), (0, 3)))], axis=1).T
    second = jnp.concatenate([half, half], axis=1).astype(bf16)
    return first, second


def kinetics_kernel(G, counts_ref, size_ref, mov_hbm, weight_ref, s1_ref, s2_ref, out_ref, heat_ref, mov, cur, outs, order_ref, tally_ref, sem):
    load = pltpu.make_async_copy(mov_hbm, mov, sem.at[0])
    load.start()
    for k in range(8):
        tally_ref[k] = 0

    def count(i, _):
        n = counts_ref[i]
        tally_ref[n] = tally_ref[n] + 1
        return 0
    lax.fori_loop(0, 128, count, 0)
    base = jnp.int32(0)
    for n in range(6, 0, -1):
        here = tally_ref[n]
        tally_ref[n] = base
        base = base + here

    def place(i, _):
        n = counts_ref[i]
        at = tally_ref[n]
        order_ref[at] = i
        tally_ref[n] = at + 1
        return 0
    lax.fori_loop(0, 128, place, 0)
    own = lax.broadcasted_iota(jnp.int32, (SP, NS), 0) == lax.broadcasted_iota(jnp.int32, (SP, NS), 1)
    weight = jnp.broadcast_to(jnp.sum(jnp.where(own, weight_ref[...], 0.0), axis=1, keepdims=True) / time_step, (SP, 128))
    load.wait()
    W = G * 128

    def turn(t, _):
        ids = [order_ref[t * G + j] for j in range(G)]
        ns = [counts_ref[i] for i in ids]
        for j in range(G):
            cur[:, j * 128:(j + 1) * 128] = mov[ids[j]]
        h = jnp.concatenate([jnp.full((SP, 128), size_ref[n], f32) for n in ns], axis=1)
        nb = jnp.concatenate([jnp.full((SP, 128), n, jnp.int32) for n in ns], axis=1)

        def level(k, _):
            conc = cur[...]
            lg = jnp.log2(conc)
            hi = lg.astype(bf16).astype(f32)
            xin = jnp.concatenate([hi, lg - hi], axis=0).astype(bf16)
            rates = jnp.exp2(jnp.dot(s1_ref[...], xin, preferred_element_type=f32))
            rhi = rates.astype(bf16)
            rlo = (rates - rhi.astype(f32)).astype(bf16)
            both = jnp.dot(s2_ref[...], jnp.concatenate([rhi, rlo], axis=0), preferred_element_type=f32)
            fresh = conc * (conc + h * both[:SP]) / (conc + h * both[SP:])
            cur[...] = jnp.where(nb > k, fresh, conc)
            return 0
        lax.fori_loop(0, ns[0], level, 0)
        for j in range(G):
            c, z = ids[j] // 2, ids[j] % 2
            res = cur[:, j * 128:(j + 1) * 128]
            outs[z, pl.ds(c, NS, stride=64), :] = res[:NS]
            heat_ref[z, pl.ds(c, 1), :] = jnp.sum(weight * (res - mov[ids[j]]), axis=0, keepdims=True)
        return 0
    lax.fori_loop(0, 128 // G, turn, 0)
    stores = [pltpu.make_async_copy(outs.at[z], out_ref.at[:, pl.ds(z * 128, 128)], sem.at[z]) for z in range(2)]
    for c in stores:
        c.start()
    for c in stores:
        c.wait()


def kinetics(G, moved, counts, heat_weights, first, second):
    vm = pl.BlockSpec(memory_space=pltpu.VMEM)
    sm = pl.BlockSpec(memory_space=pltpu.SMEM)
    hb = pl.BlockSpec(memory_space=pl.ANY)
    sizes = np.array([0.0] + [time_step / n for n in range(1, 8)], np.float32)
    return pl.pallas_call(
        functools.partial(kinetics_kernel, G),
        out_shape=(jax.ShapeDtypeStruct((NS * 64, 256), f32), jax.ShapeDtypeStruct((2, 64, 128), f32)),
        in_specs=[sm, sm, hb, vm, vm, vm],
        out_specs=(hb, vm),
        scratch_shapes=[
            pltpu.VMEM((128, SP, 128), f32), pltpu.VMEM((SP, G * 128), f32), pltpu.VMEM((2, NS * 64, 128), f32),
            pltpu.SMEM((128,), jnp.int32), pltpu.SMEM((8,), jnp.int32), pltpu.SemaphoreType.DMA((2,))],
        compiler_params=pltpu.CompilerParams(vmem_limit_bytes=32 << 20),
        name="kinetics",
    )(counts, jnp.asarray(sizes), moved, heat_weights[None, :], first, second)


def cosine_table(length):
    wave = np.arange(length)[:, None]
    sample = np.arange(length)[None, :] + 0.5
    weight = np.sqrt(np.where(wave == 0, 1.0, 2.0) / length)
    return (weight * np.cos(np.pi * wave * sample / length)).astype(np.float32)


def mode_values(length):
    return 2.0 - 2.0 * np.cos(np.pi * np.arange(length) / length)


def exact_dot(a, b, dims):
    return lax.dot_general(a, b, (dims, ((), ())), precision=highest, preferred_element_type=f32)


def solve_kernel(heat_ref, div_ref, tz_ref, tx_ref, ty_ref, shift_ref, ly_ref, out_ref,
                 f1, send1, recv1, yv, send2, recv2, recv3, yb, send4, recv4, fp,
                 ss1, rs1, ss2, rs2, ss3, rs3, ss4, rs4):
    rows, cols = 8, 16
    me_r, me_c = lax.axis_index("row"), lax.axis_index("col")
    barrier = pltpu.get_barrier_semaphore()
    for d in range(1, rows):
        pl.semaphore_signal(barrier, inc=1, device_id={"row": lax.rem(me_r + d, rows), "col": me_c}, device_id_type=pl.DeviceIdType.MESH)
    for d in range(1, cols):
        pl.semaphore_signal(barrier, inc=1, device_id={"row": me_r, "col": lax.rem(me_c + d, cols)}, device_id_type=pl.DeviceIdType.MESH)

    def row_copy(send, recv, ss, rs, d):
        to = lax.rem(me_r + d, rows)
        return pltpu.make_async_remote_copy(src_ref=send.at[to], dst_ref=recv.at[me_r], send_sem=ss.at[d], recv_sem=rs.at[me_r],
                                            device_id={"row": to, "col": me_c}, device_id_type=pl.DeviceIdType.MESH)

    def col_copy(send, recv, ss, rs, d):
        to = lax.rem(me_c + d, cols)
        return pltpu.make_async_remote_copy(src_ref=send.at[to], dst_ref=recv.at[me_c], send_sem=ss.at[d], recv_sem=rs.at[me_c],
                                            device_id={"row": me_r, "col": to}, device_id_type=pl.DeviceIdType.MESH)

    def row_arrival(send, recv, ss, rs, d):
        come = lax.rem(me_r + d, rows)
        return pltpu.make_async_remote_copy(src_ref=send.at[come], dst_ref=recv.at[come], send_sem=ss.at[d], recv_sem=rs.at[come],
                                            device_id={"row": come, "col": me_c}, device_id_type=pl.DeviceIdType.MESH)

    def col_arrival(send, recv, ss, rs, d):
        come = lax.rem(me_c + d, cols)
        return pltpu.make_async_remote_copy(src_ref=send.at[come], dst_ref=recv.at[come], send_sem=ss.at[d], recv_sem=rs.at[come],
                                            device_id={"row": me_r, "col": come}, device_id_type=pl.DeviceIdType.MESH)

    lane = lax.broadcasted_iota(jnp.int32, (8, 128), 1)
    part = lane // 32
    source = div_ref[...] - jnp.concatenate([heat_ref[0], heat_ref[1]], axis=1)
    forward = exact_dot(source, tz_ref[...], ((1,), (1,)))
    f1[0] = forward[:, :128]
    f1[1] = forward[:, 128:]
    for kh in range(2):
        for h in range(2):
            v = [f1[kh, pl.ds(4 * h + p, 8, stride=8), :] for p in range(4)]
            for q in range(4):
                tile = jnp.zeros((8, 128), f32)
                for p in range(4):
                    s = (p - q) * 32 % 128
                    tile = jnp.where(part == p, pltpu.roll(v[p], s, 1) if s else v[p], tile)
                send1[kh * 4 + q, :, h * 128:(h + 1) * 128] = tile
    pl.semaphore_wait(barrier, rows - 1 + cols - 1)
    sent = [row_copy(send1, recv1, ss1, rs1, d) for d in range(1, rows)]
    for c in sent:
        c.start()
    recv1[me_r] = send1[me_r]
    for d in range(1, rows):
        row_arrival(send1, recv1, ss1, rs1, d).wait_recv()
    for c in sent:
        c.wait_send()
    block = recv1[...].reshape(64, 256)
    tx = tx_ref[...]
    yv[...] = exact_dot(jnp.transpose(block), jnp.concatenate([tx, tx], axis=0), ((1,), (1,)))
    for c in range(cols):
        send2[c] = jnp.where(lane < 64, yv[pl.ds(2 * c, 8, stride=32), :], yv[pl.ds(2 * c + 1, 8, stride=32), :])
    sent = [col_copy(send2, recv2, ss2, rs2, d) for d in range(1, cols)]
    for c in sent:
        c.start()
    recv2[me_c] = send2[me_c]
    for d in range(1, cols):
        col_arrival(send2, recv2, ss2, rs2, d).wait_recv()
    for c in sent:
        c.wait_send()
    ty = ty_ref[...]
    spectrum = exact_dot(ty, recv2[...].reshape(128, 128), ((1,), (0,)))
    shift = shift_ref[pl.ds(me_r * cols + me_c, 1), :]
    spectrum = spectrum / (ly_ref[...] + shift)
    send2[...] = exact_dot(ty, spectrum, ((0,), (0,))).reshape(cols, 8, 128)
    sent = [col_copy(send2, recv3, ss3, rs3, d) for d in range(1, cols)]
    for c in sent:
        c.start()
    recv3[me_c] = send2[me_c]
    for d in range(1, cols):
        col_arrival(send2, recv3, ss3, rs3, d).wait_recv()
    for c in sent:
        c.wait_send()
    for c in range(cols):
        tile = recv3[c]
        yb[pl.ds(2 * c, 8, stride=32), :] = jnp.where(lane < 64, tile, 0.0)
        yb[pl.ds(2 * c + 1, 8, stride=32), :] = jnp.where(lane < 64, 0.0, tile)
    txt = jnp.transpose(tx)
    send4[...] = exact_dot(jnp.concatenate([txt, txt], axis=1), yb[...], ((1,), (1,))).reshape(8, 8, 256)
    sent = [row_copy(send4, recv4, ss4, rs4, d) for d in range(1, rows)]
    for c in sent:
        c.start()
    recv4[me_r] = send4[me_r]
    for d in range(1, rows):
        row_arrival(send4, recv4, ss4, rs4, d).wait_recv()
    for c in sent:
        c.wait_send()
    for kh in range(2):
        for h in range(2):
            v = [recv4[kh * 4 + q, :, h * 128:(h + 1) * 128] for q in range(4)]
            for p in range(4):
                tile = jnp.zeros((8, 128), f32)
                for q in range(4):
                    s = (q - p) * 32 % 128
                    tile = jnp.where(part == q, pltpu.roll(v[q], s, 1) if s else v[q], tile)
                fp[kh, pl.ds(4 * h + p, 8, stride=8), :] = tile
    out_ref[...] = exact_dot(jnp.concatenate([fp[0], fp[1]], axis=1), tz_ref[...], ((1,), (0,)))


def solve(heat, divergence):
    lx, ly, lz = mode_values(64), mode_values(128), mode_values(256)
    device = np.arange(128)
    lanes = np.arange(128)
    shift = screen + lx[lanes % 64][None, :] + lz[(device // 16 * 32 + device % 16 * 2)[:, None] + (lanes // 64)[None, :]]
    vm = pl.BlockSpec(memory_space=pltpu.VMEM)
    dma = pltpu.SemaphoreType.DMA
    out = pl.pallas_call(
        solve_kernel,
        out_shape=jax.ShapeDtypeStruct((64, 256), f32),
        in_specs=[vm] * 7,
        out_specs=vm,
        scratch_shapes=[
            pltpu.VMEM((2, 64, 128), f32), pltpu.VMEM((8, 8, 256), f32), pltpu.VMEM((8, 8, 256), f32), pltpu.VMEM((256, 128), f32),
            pltpu.VMEM((16, 8, 128), f32), pltpu.VMEM((16, 8, 128), f32), pltpu.VMEM((16, 8, 128), f32), pltpu.VMEM((256, 128), f32),
            pltpu.VMEM((8, 8, 256), f32), pltpu.VMEM((8, 8, 256), f32), pltpu.VMEM((2, 64, 128), f32),
            dma((8,)), dma((8,)), dma((16,)), dma((16,)), dma((16,)), dma((16,)), dma((8,)), dma((8,))],
        compiler_params=pltpu.CompilerParams(collective_id=1, has_side_effects=True, vmem_limit_bytes=16 << 20),
        name="screened_solve",
    )(heat, divergence.reshape(64, 256), jnp.asarray(cosine_table(256)), jnp.asarray(cosine_table(64)), jnp.asarray(cosine_table(128)),
      jnp.asarray(shift.astype(np.float32)), jnp.asarray(np.broadcast_to(ly[:, None], (128, 128)).astype(np.float32)))
    return out.reshape(8, 8, 256)


def local(species, velocity, diffusivity, divergence, log_rates, reactants, products, heat_weights, substeps):
    first, second = matrices(log_rates, reactants, products)
    moved = advance(species, velocity, diffusivity)
    reacted, heat = kinetics(16, moved, substeps.reshape(-1), heat_weights, first, second)
    pressure = solve(heat, divergence)
    return reacted.reshape(species.shape), pressure


def solution(mesh):
    cells = P("row", "col", None)
    fields = P(None, "row", "col", None)
    in_specs = (fields, fields, P(), cells, P(), P(), P(), P(), cells)
    return jax.shard_map(local, mesh=mesh, in_specs=in_specs, out_specs=(fields, cells), check_vma=False)
```

```python
import functools

import jax
import jax.numpy as jnp
import numpy as np
from jax import lax
from jax.experimental import pallas as pl
from jax.experimental.pallas import tpu as pltpu
from jax.sharding import PartitionSpec as P

f32, bf16 = jnp.float32, jnp.bfloat16
MESH = pl.DeviceIdType.MESH
NS, SP = 53, 56
NR, RP = 325, 336
LOG2E = 1.4426950408889634
time_step = 0.2
screen = 0.004
highest = lax.Precision.HIGHEST

def split3(x):
    hi = x.astype(bf16).astype(f32)
    mid = (x - hi).astype(bf16).astype(f32)
    return hi, mid, x - hi - mid


def build_matrices(log_rates, react_ref, prod_ref, react, prod, first_ref, second_ref):
    react[...] = jnp.zeros_like(react)
    prod[...] = jnp.zeros_like(prod)
    react[:NR, :NS] = react_ref[...].astype(f32)
    prod[:NR, :NS] = prod_ref[...].astype(f32)
    rp = react[...]
    own = lax.broadcasted_iota(jnp.int32, (RP, NR), 0) == lax.broadcasted_iota(jnp.int32, (RP, NR), 1)
    hi, mid, low = split3(jnp.sum(jnp.where(own, log_rates[...], 0.0), axis=1, keepdims=True) * LOG2E)
    lane = lax.broadcasted_iota(jnp.int32, (RP, 128), 1)
    later = pltpu.roll(rp, SP, 1)
    both = jnp.where(lane == NS, hi, jnp.where(lane == NS + 1, mid, jnp.where(lane == NS + 2, low, rp + later)))
    first_ref[...] = both[:, :2 * SP].astype(bf16)
    outcome = prod[...] + later
    second_ref[...] = jnp.transpose(jnp.concatenate([outcome, outcome], axis=0))[:2 * SP].astype(bf16)


def build_order(counts, order_ref):
    n = counts[...].astype(f32)
    row = lax.broadcasted_iota(jnp.int32, (128, 128), 0)
    lane = lax.broadcasted_iota(jnp.int32, (128, 128), 1)
    column = jnp.sum(jnp.where(row == lane, n, 0.0), axis=1, keepdims=True)
    ahead = jnp.where(n > column, 1.0, jnp.where(n == column, jnp.where(lane < row, 1.0, 0.0), 0.0))
    rank = jnp.sum(ahead, axis=1, keepdims=True).astype(jnp.int32)
    here = rank == lane
    order_ref[0:1, :] = jnp.sum(jnp.where(here, row.astype(f32), 0.0), axis=0, keepdims=True).astype(jnp.int32)
    order_ref[1:2, :] = jnp.sum(jnp.where(here, jnp.broadcast_to(column, (128, 128)), 0.0), axis=0, keepdims=True).astype(jnp.int32)


def advance_kernel(species, vel_hbm, diff_hbm, rates_hbm, react_hbm, prod_hbm, counts_hbm, mov_ref, first_ref, second_ref, order_ref,
                   sp, hx, ext, mv, vel_ref, diff_ref, rates_ref, react_ref, prod_ref, counts_ref, react, prod, sem_in, ss, rs, sem_out):
    rows, cols = lax.axis_size("row"), lax.axis_size("col")
    me_r, me_c = lax.axis_index("row"), lax.axis_index("col")
    above = {"row": lax.rem(me_r + 1, rows), "col": me_c}
    below = {"row": lax.rem(me_r + rows - 1, rows), "col": me_c}
    right = {"row": me_r, "col": lax.rem(me_c + 1, cols)}
    left = {"row": me_r, "col": lax.rem(me_c + cols - 1, cols)}
    barrier = pltpu.get_barrier_semaphore()
    for peer in (above, below, right, left):
        pl.semaphore_signal(barrier, inc=1, device_id=peer, device_id_type=MESH)
    loads = [pltpu.make_async_copy(species.at[:, :, pl.ds(z * 128, 128)], sp.at[z], sem_in.at[z]) for z in range(2)]
    loads += [pltpu.make_async_copy(vel_hbm, vel_ref, sem_in.at[2]), pltpu.make_async_copy(diff_hbm, diff_ref, sem_in.at[3])]
    extra = [pltpu.make_async_copy(a, b, sem_in.at[4 + k]) for k, (a, b) in enumerate(((rates_hbm, rates_ref), (react_hbm, react_ref), (prod_hbm, prod_ref), (counts_hbm, counts_ref)))]
    for c in loads + extra:
        c.start()
    pl.semaphore_wait(barrier, 4)
    x_copies = []
    for z in range(2):
        zs = pl.ds(z * 128, 128)
        x_copies.append(pltpu.make_async_remote_copy(src_ref=species.at[:, pl.ds(56, 8), zs], dst_ref=hx.at[0, z], send_sem=ss.at[2 + z], recv_sem=rs.at[2 + z], device_id=above, device_id_type=MESH))
        x_copies.append(pltpu.make_async_remote_copy(src_ref=species.at[:, pl.ds(0, 8), zs], dst_ref=hx.at[1, z], send_sem=ss.at[4 + z], recv_sem=rs.at[4 + z], device_id=below, device_id_type=MESH))
    for c in x_copies:
        c.start()
    for c in loads:
        c.wait()

    def lay(x, y):
        c = x * 8 + y
        for z in range(2):
            ext[x + 1, y + 1, :NS, z * 128:(z + 1) * 128] = sp_rows(z, c)

    def sp_rows(z, c):
        return sp.at[z].reshape(NS * 64, 128)[pl.ds(c, NS, stride=64), :]

    def lay_edge(x, _):
        lay(x, 0)
        lay(x, 7)
        return 0
    lax.fori_loop(0, 8, lay_edge, 0)
    y_up = pltpu.make_async_remote_copy(src_ref=ext.at[pl.ds(1, 8), 8], dst_ref=ext.at[pl.ds(1, 8), 0], send_sem=ss.at[0], recv_sem=rs.at[0], device_id=right, device_id_type=MESH)
    y_down = pltpu.make_async_remote_copy(src_ref=ext.at[pl.ds(1, 8), 1], dst_ref=ext.at[pl.ds(1, 8), 9], send_sem=ss.at[1], recv_sem=rs.at[1], device_id=left, device_id_type=MESH)
    y_up.start()
    y_down.start()

    def lay_inner(x, _):
        for y in range(1, 7):
            lay(x, y)
        return 0
    lax.fori_loop(0, 8, lay_inner, 0)

    own = lax.broadcasted_iota(jnp.int32, (SP, NS), 0) == lax.broadcasted_iota(jnp.int32, (SP, NS), 1)
    fifth = jnp.broadcast_to(0.2 * jnp.sum(jnp.where(own, diff_ref[...], 0.0), axis=1, keepdims=True), (SP, 256))
    lane = lax.broadcasted_iota(jnp.int32, (SP, 256), 1)
    row = lax.broadcasted_iota(jnp.int32, (SP, 256), 0)

    def move(x, y):
        c = x * 8 + y
        centre = ext[x + 1, y + 1]
        near = (ext[x, y + 1], ext[x + 2, y + 1], ext[x + 1, y], ext[x + 1, y + 2],
                jnp.where(lane == 0, centre, pltpu.roll(centre, 1, 1)), jnp.where(lane == 255, centre, pltpu.roll(centre, 255, 1)))
        speeds = [0.2 * vel_ref[d, pl.ds(c, 1), :] for d in range(3)]
        still = 1.0 - (jnp.abs(speeds[0]) + jnp.abs(speeds[1]) + jnp.abs(speeds[2]))
        total = centre * (still - 6.0 * fifth)
        for d in range(3):
            total = total + near[2 * d] * (fifth + jnp.maximum(speeds[d], 0.0))
            total = total + near[2 * d + 1] * (fifth - jnp.minimum(speeds[d], 0.0))
        total = jnp.where(row < NS, total, 2.0)
        mv[2 * c] = total[:, :128]
        mv[2 * c + 1] = total[:, 128:]

    def inner(x, _):
        def go(y, _):
            move(x, y)
            return 0
        return lax.fori_loop(1, 7, go, 0)
    lax.fori_loop(1, 7, inner, 0)
    for c in extra:
        c.wait()
    build_matrices(rates_ref, react_ref, prod_ref, react, prod, first_ref, second_ref)
    build_order(counts_ref, order_ref)
    y_up.wait()
    y_down.wait()

    @pl.when(me_c == 0)
    def _():
        ext[pl.ds(1, 8), 0] = ext[pl.ds(1, 8), 1]

    @pl.when(me_c == cols - 1)
    def _():
        ext[pl.ds(1, 8), 9] = ext[pl.ds(1, 8), 8]

    def sides(x, _):
        move(x, 0)
        move(x, 7)
        return 0
    lax.fori_loop(1, 7, sides, 0)
    middle = pltpu.make_async_copy(mv.at[pl.ds(16, 96)], mov_ref.at[pl.ds(16, 96)], sem_out.at[0])
    middle.start()
    for c in x_copies:
        c.wait()

    def lay_halo(y, _):
        for k, at in ((0, 0), (1, 9)):
            for z in range(2):
                ext[at, y + 1, :NS, z * 128:(z + 1) * 128] = hx_rows(k, z, y)
        return 0

    def hx_rows(k, z, y):
        return hx.at[k, z].reshape(NS * 8, 128)[pl.ds(y, NS, stride=8), :]
    lax.fori_loop(0, 8, lay_halo, 0)

    @pl.when(me_r == 0)
    def _():
        ext[0, pl.ds(1, 8)] = ext[1, pl.ds(1, 8)]

    @pl.when(me_r == rows - 1)
    def _():
        ext[9, pl.ds(1, 8)] = ext[8, pl.ds(1, 8)]

    def ends(y, _):
        move(0, y)
        move(7, y)
        return 0
    lax.fori_loop(0, 8, ends, 0)
    low = pltpu.make_async_copy(mv.at[pl.ds(0, 16)], mov_ref.at[pl.ds(0, 16)], sem_out.at[1])
    high = pltpu.make_async_copy(mv.at[pl.ds(112, 16)], mov_ref.at[pl.ds(112, 16)], sem_out.at[2])
    low.start()
    high.start()
    middle.wait()
    low.wait()
    high.wait()


def advance(species, velocity, diffusivity, log_rates, reactants, products, counts):
    vm = pl.BlockSpec(memory_space=pltpu.VMEM)
    hb = pl.BlockSpec(memory_space=pl.ANY)
    dma = pltpu.SemaphoreType.DMA
    shape = jax.ShapeDtypeStruct
    return pl.pallas_call(
        advance_kernel,
        out_shape=(shape((128, SP, 128), f32), shape((RP, 2 * SP), bf16), shape((2 * SP, 2 * RP), bf16), shape((2, 128), jnp.int32)),
        in_specs=[hb] * 7,
        out_specs=(hb, vm, vm, vm),
        scratch_shapes=[pltpu.VMEM((2, NS, 64, 128), f32), pltpu.VMEM((2, 2, NS, 8, 128), f32), pltpu.VMEM((10, 10, SP, 256), f32), pltpu.VMEM((128, SP, 128), f32),
                        pltpu.VMEM((3, 64, 256), f32), pltpu.VMEM((1, NS), f32), pltpu.VMEM((1, NR), f32), pltpu.VMEM((NR, NS), jnp.int32), pltpu.VMEM((NR, NS), jnp.int32),
                        pltpu.VMEM((1, 128), jnp.int32), pltpu.VMEM((RP, 128), f32), pltpu.VMEM((RP, 128), f32), dma((8,)), dma((6,)), dma((6,)), dma((3,))],
        compiler_params=pltpu.CompilerParams(collective_id=0, has_side_effects=True, vmem_limit_bytes=60 << 20),
        name="advance",
    )(species.reshape(NS, 64, 256), velocity.reshape(3, 64, 256), diffusivity[None, :], log_rates[None, :], reactants, products, counts[None, :])


def kinetics_kernel(G, order_ref, size_ref, mov_hbm, weight_hbm, s1_hbm, s2_hbm, out_ref, heat_ref, mov, cur, outs, weight_ref, s1_ref, s2_ref, sem, arrive):
    turns = 128 // G

    def fetch(t, slot):
        return [pltpu.make_async_copy(mov_hbm.at[order_ref[0, t * G + j]], mov.at[slot, j], arrive.at[slot]) for j in range(G)]
    for c in fetch(0, 0):
        c.start()
    constants = [pltpu.make_async_copy(a, b, sem.at[k]) for k, (a, b) in enumerate(((weight_hbm, weight_ref), (s1_hbm, s1_ref), (s2_hbm, s2_ref)))]
    for c in constants:
        c.start()
    for c in constants:
        c.wait()
    own = lax.broadcasted_iota(jnp.int32, (SP, NS), 0) == lax.broadcasted_iota(jnp.int32, (SP, NS), 1)
    weight = jnp.broadcast_to(jnp.sum(jnp.where(own, weight_ref[...], 0.0), axis=1, keepdims=True) / time_step, (SP, 128))
    W = G * 128

    def turn(t, _):
        slot = t % 2

        @pl.when(t + 1 < turns)
        def _():
            for c in fetch(t + 1, 1 - slot):
                c.start()
        ids = [order_ref[0, t * G + j] for j in range(G)]
        ns = [order_ref[1, t * G + j] for j in range(G)]
        for c in fetch(t, slot):
            c.wait()
        for j in range(G):
            cur[:, j * 128:(j + 1) * 128] = mov[slot, j]
        h = jnp.concatenate([jnp.full((SP, 128), size_ref[n], f32) for n in ns], axis=1)
        nb = jnp.concatenate([jnp.full((SP, 128), n, jnp.int32) for n in ns], axis=1)

        def level(k, _):
            conc = cur[...]
            lg = jnp.log2(conc)
            hi = lg.astype(bf16).astype(f32)
            xin = jnp.concatenate([hi, lg - hi], axis=0).astype(bf16)
            rates = jnp.exp2(jnp.dot(s1_ref[...], xin, preferred_element_type=f32))
            rhi = rates.astype(bf16)
            rlo = (rates - rhi.astype(f32)).astype(bf16)
            both = jnp.dot(s2_ref[...], jnp.concatenate([rhi, rlo], axis=0), preferred_element_type=f32)
            fresh = conc * (conc + h * both[:SP]) / (conc + h * both[SP:])
            cur[...] = jnp.where(nb > k, fresh, conc)
            return 0
        lax.fori_loop(0, ns[0], level, 0)
        for j in range(G):
            c, z = ids[j] // 2, ids[j] % 2
            res = cur[:, j * 128:(j + 1) * 128]
            outs[z, pl.ds(c, NS, stride=64), :] = res[:NS]
            heat_ref[z, pl.ds(c, 1), :] = jnp.sum(weight * (res - mov[slot, j]), axis=0, keepdims=True)
        return 0
    lax.fori_loop(0, turns, turn, 0)
    stores = [pltpu.make_async_copy(outs.at[z], out_ref.at[:, pl.ds(z * 128, 128)], sem.at[z]) for z in range(2)]
    for c in stores:
        c.start()
    for c in stores:
        c.wait()


def kinetics(G, moved, order, heat_weights, first, second):
    vm = pl.BlockSpec(memory_space=pltpu.VMEM)
    sm = pl.BlockSpec(memory_space=pltpu.SMEM)
    hb = pl.BlockSpec(memory_space=pl.ANY)
    sizes = np.array([0.0] + [time_step / n for n in range(1, 8)], np.float32)
    return pl.pallas_call(
        functools.partial(kinetics_kernel, G),
        out_shape=(jax.ShapeDtypeStruct((NS * 64, 256), f32), jax.ShapeDtypeStruct((2, 64, 128), f32)),
        in_specs=[sm, sm, hb, hb, hb, hb],
        out_specs=(hb, vm),
        scratch_shapes=[
            pltpu.VMEM((2, G, SP, 128), f32), pltpu.VMEM((SP, G * 128), f32), pltpu.VMEM((2, NS * 64, 128), f32), pltpu.VMEM((1, NS), f32),
            pltpu.VMEM((RP, 2 * SP), bf16), pltpu.VMEM((2 * SP, 2 * RP), bf16), pltpu.SemaphoreType.DMA((3,)), pltpu.SemaphoreType.DMA((2,))],
        compiler_params=pltpu.CompilerParams(vmem_limit_bytes=60 << 20),
        name="kinetics",
    )(order, jnp.asarray(sizes), moved, heat_weights[None, :], first, second)


def cosine_table(length):
    wave = np.arange(length)[:, None]
    sample = np.arange(length)[None, :] + 0.5
    weight = np.sqrt(np.where(wave == 0, 1.0, 2.0) / length)
    return (weight * np.cos(np.pi * wave * sample / length)).astype(np.float32)


def mode_values(length):
    return 2.0 - 2.0 * np.cos(np.pi * np.arange(length) / length)


def exact_dot(a, b, dims):
    return lax.dot_general(a, b, (dims, ((), ())), precision=highest, preferred_element_type=f32)


def solve_kernel(heat_hbm, div_hbm, tz_hbm, tx_hbm, ty_hbm, shift_hbm, ly_hbm, out_ref,
                 heat_ref, div_ref, tz_ref, tx_ref, ty_ref, shift_ref, ly_ref, sem_in,
                 f1, send1, recv1, yv, send2, recv2, recv3, yb, send4, recv4, fp,
                 ss1, rs1, ss2, rs2, ss3, rs3, ss4, rs4):
    rows, cols = 8, 16
    me_r, me_c = lax.axis_index("row"), lax.axis_index("col")
    pairs = ((heat_hbm, heat_ref), (div_hbm, div_ref), (tz_hbm, tz_ref), (tx_hbm, tx_ref), (ty_hbm, ty_ref), (shift_hbm, shift_ref), (ly_hbm, ly_ref))
    loads = [pltpu.make_async_copy(a, b, sem_in.at[k]) for k, (a, b) in enumerate(pairs)]
    for c in loads:
        c.start()
    barrier = pltpu.get_barrier_semaphore()
    for d in range(1, rows):
        pl.semaphore_signal(barrier, inc=1, device_id={"row": lax.rem(me_r + d, rows), "col": me_c}, device_id_type=pl.DeviceIdType.MESH)
    for d in range(1, cols):
        pl.semaphore_signal(barrier, inc=1, device_id={"row": me_r, "col": lax.rem(me_c + d, cols)}, device_id_type=pl.DeviceIdType.MESH)

    def row_copy(send, recv, ss, rs, d):
        to = lax.rem(me_r + d, rows)
        return pltpu.make_async_remote_copy(src_ref=send.at[to], dst_ref=recv.at[me_r], send_sem=ss.at[d], recv_sem=rs.at[me_r],
                                            device_id={"row": to, "col": me_c}, device_id_type=pl.DeviceIdType.MESH)

    def col_copy(send, recv, ss, rs, d):
        to = lax.rem(me_c + d, cols)
        return pltpu.make_async_remote_copy(src_ref=send.at[to], dst_ref=recv.at[me_c], send_sem=ss.at[d], recv_sem=rs.at[me_c],
                                            device_id={"row": me_r, "col": to}, device_id_type=pl.DeviceIdType.MESH)

    def row_arrival(send, recv, ss, rs, d):
        come = lax.rem(me_r + d, rows)
        return pltpu.make_async_remote_copy(src_ref=send.at[come], dst_ref=recv.at[come], send_sem=ss.at[d], recv_sem=rs.at[come],
                                            device_id={"row": come, "col": me_c}, device_id_type=pl.DeviceIdType.MESH)

    def col_arrival(send, recv, ss, rs, d):
        come = lax.rem(me_c + d, cols)
        return pltpu.make_async_remote_copy(src_ref=send.at[come], dst_ref=recv.at[come], send_sem=ss.at[d], recv_sem=rs.at[come],
                                            device_id={"row": me_r, "col": come}, device_id_type=pl.DeviceIdType.MESH)

    lane = lax.broadcasted_iota(jnp.int32, (8, 128), 1)
    part = lane // 32
    for c in loads:
        c.wait()
    source = div_ref[...] - jnp.concatenate([heat_ref[0], heat_ref[1]], axis=1)
    forward = exact_dot(source, tz_ref[...], ((1,), (1,)))
    f1[0] = forward[:, :128]
    f1[1] = forward[:, 128:]
    for kh in range(2):
        for h in range(2):
            v = [f1[kh, pl.ds(4 * h + p, 8, stride=8), :] for p in range(4)]
            for q in range(4):
                tile = jnp.zeros((8, 128), f32)
                for p in range(4):
                    s = (p - q) * 32 % 128
                    tile = jnp.where(part == p, pltpu.roll(v[p], s, 1) if s else v[p], tile)
                send1[kh * 4 + q, :, h * 128:(h + 1) * 128] = tile
    pl.semaphore_wait(barrier, rows - 1 + cols - 1)
    sent = [row_copy(send1, recv1, ss1, rs1, d) for d in range(1, rows)]
    for c in sent:
        c.start()
    recv1[me_r] = send1[me_r]
    for d in range(1, rows):
        row_arrival(send1, recv1, ss1, rs1, d).wait_recv()
    for c in sent:
        c.wait_send()
    block = recv1[...].reshape(64, 256)
    tx = tx_ref[...]
    yv[...] = exact_dot(jnp.transpose(block), jnp.concatenate([tx, tx], axis=0), ((1,), (1,)))
    for c in range(cols):
        send2[c] = jnp.where(lane < 64, yv[pl.ds(2 * c, 8, stride=32), :], yv[pl.ds(2 * c + 1, 8, stride=32), :])
    sent = [col_copy(send2, recv2, ss2, rs2, d) for d in range(1, cols)]
    for c in sent:
        c.start()
    recv2[me_c] = send2[me_c]
    for d in range(1, cols):
        col_arrival(send2, recv2, ss2, rs2, d).wait_recv()
    for c in sent:
        c.wait_send()
    ty = ty_ref[...]
    spectrum = exact_dot(ty, recv2[...].reshape(128, 128), ((1,), (0,)))
    shift = shift_ref[pl.ds(me_r * cols + me_c, 1), :]
    spectrum = spectrum / (ly_ref[...] + shift)
    send2[...] = exact_dot(ty, spectrum, ((0,), (0,))).reshape(cols, 8, 128)
    sent = [col_copy(send2, recv3, ss3, rs3, d) for d in range(1, cols)]
    for c in sent:
        c.start()
    recv3[me_c] = send2[me_c]
    for d in range(1, cols):
        col_arrival(send2, recv3, ss3, rs3, d).wait_recv()
    for c in sent:
        c.wait_send()
    for c in range(cols):
        tile = recv3[c]
        yb[pl.ds(2 * c, 8, stride=32), :] = jnp.where(lane < 64, tile, 0.0)
        yb[pl.ds(2 * c + 1, 8, stride=32), :] = jnp.where(lane < 64, 0.0, tile)
    txt = jnp.transpose(tx)
    send4[...] = exact_dot(jnp.concatenate([txt, txt], axis=1), yb[...], ((1,), (1,))).reshape(8, 8, 256)
    sent = [row_copy(send4, recv4, ss4, rs4, d) for d in range(1, rows)]
    for c in sent:
        c.start()
    recv4[me_r] = send4[me_r]
    for d in range(1, rows):
        row_arrival(send4, recv4, ss4, rs4, d).wait_recv()
    for c in sent:
        c.wait_send()
    for kh in range(2):
        for h in range(2):
            v = [recv4[kh * 4 + q, :, h * 128:(h + 1) * 128] for q in range(4)]
            for p in range(4):
                tile = jnp.zeros((8, 128), f32)
                for q in range(4):
                    s = (q - p) * 32 % 128
                    tile = jnp.where(part == q, pltpu.roll(v[q], s, 1) if s else v[q], tile)
                fp[kh, pl.ds(4 * h + p, 8, stride=8), :] = tile
    out_ref[...] = exact_dot(jnp.concatenate([fp[0], fp[1]], axis=1), tz_ref[...], ((1,), (0,)))


def solve(heat, divergence):
    lx, ly, lz = mode_values(64), mode_values(128), mode_values(256)
    device = np.arange(128)
    lanes = np.arange(128)
    shift = screen + lx[lanes % 64][None, :] + lz[(device // 16 * 32 + device % 16 * 2)[:, None] + (lanes // 64)[None, :]]
    vm = pl.BlockSpec(memory_space=pltpu.VMEM)
    hb = pl.BlockSpec(memory_space=pl.ANY)
    dma = pltpu.SemaphoreType.DMA
    out = pl.pallas_call(
        solve_kernel,
        out_shape=jax.ShapeDtypeStruct((64, 256), f32),
        in_specs=[hb] * 7,
        out_specs=vm,
        scratch_shapes=[
            pltpu.VMEM((2, 64, 128), f32), pltpu.VMEM((64, 256), f32), pltpu.VMEM((256, 256), f32), pltpu.VMEM((64, 64), f32), pltpu.VMEM((128, 128), f32),
            pltpu.VMEM((128, 128), f32), pltpu.VMEM((128, 128), f32), dma((7,)),
            pltpu.VMEM((2, 64, 128), f32), pltpu.VMEM((8, 8, 256), f32), pltpu.VMEM((8, 8, 256), f32), pltpu.VMEM((256, 128), f32),
            pltpu.VMEM((16, 8, 128), f32), pltpu.VMEM((16, 8, 128), f32), pltpu.VMEM((16, 8, 128), f32), pltpu.VMEM((256, 128), f32),
            pltpu.VMEM((8, 8, 256), f32), pltpu.VMEM((8, 8, 256), f32), pltpu.VMEM((2, 64, 128), f32),
            dma((8,)), dma((8,)), dma((16,)), dma((16,)), dma((16,)), dma((16,)), dma((8,)), dma((8,))],
        compiler_params=pltpu.CompilerParams(collective_id=1, has_side_effects=True, vmem_limit_bytes=60 << 20),
        name="screened_solve",
    )(heat, divergence.reshape(64, 256), jnp.asarray(cosine_table(256)), jnp.asarray(cosine_table(64)), jnp.asarray(cosine_table(128)),
      jnp.asarray(shift.astype(np.float32)), jnp.asarray(np.broadcast_to(ly[:, None], (128, 128)).astype(np.float32)))
    return out.reshape(8, 8, 256)


def local(species, velocity, diffusivity, divergence, log_rates, reactants, products, heat_weights, substeps):
    moved, first, second, order = advance(species, velocity, diffusivity, log_rates, reactants, products, substeps.reshape(-1))
    reacted, heat = kinetics(16, moved, order, heat_weights, first, second)
    pressure = solve(heat, divergence)
    return reacted.reshape(species.shape), pressure


def solution(mesh):
    cells = P("row", "col", None)
    fields = P(None, "row", "col", None)
    in_specs = (fields, fields, P(), cells, P(), P(), P(), P(), cells)
    return jax.shard_map(local, mesh=mesh, in_specs=in_specs, out_specs=(fields, cells), check_vma=False)
```

```python
import functools

import jax
import jax.numpy as jnp
import numpy as np
from jax import lax
from jax.experimental import pallas as pl
from jax.experimental.pallas import tpu as pltpu
from jax.sharding import PartitionSpec as P

f32, bf16 = jnp.float32, jnp.bfloat16
MESH = pl.DeviceIdType.MESH
NS, SP = 53, 56
NR, RP = 325, 336
LOG2E = 1.4426950408889634
time_step = 0.2
screen = 0.004
highest = lax.Precision.HIGHEST

def split3(x):
    hi = x.astype(bf16).astype(f32)
    mid = (x - hi).astype(bf16).astype(f32)
    return hi, mid, x - hi - mid


def build_matrices(log_rates, react_ref, prod_ref, react, prod, halves, first_ref, second_ref):
    react[...] = jnp.zeros_like(react)
    prod[...] = jnp.zeros_like(prod)
    react[:NS, :NR] = react_ref[...].astype(f32)
    prod[:NS, :NR] = prod_ref[...].astype(f32)
    rt, pt = react[...], prod[...]
    rp = jnp.transpose(rt)[:RP]
    own = lax.broadcasted_iota(jnp.int32, (RP, NR), 0) == lax.broadcasted_iota(jnp.int32, (RP, NR), 1)
    hi, mid, low = split3(jnp.sum(jnp.where(own, log_rates[...].reshape(1, NR), 0.0), axis=1, keepdims=True) * LOG2E)
    lane = lax.broadcasted_iota(jnp.int32, (RP, 128), 1)
    later = pltpu.roll(rp, SP, 1)
    both = jnp.where(lane == NS, hi, jnp.where(lane == NS + 1, mid, jnp.where(lane == NS + 2, low, rp + later)))
    first_ref[...] = both[:, :2 * SP].astype(bf16)
    outcome = jnp.concatenate([pt[:SP], rt[:SP]], axis=0)
    halves[:, :384] = outcome
    halves[:, RP:RP + 384] = outcome
    second_ref[...] = halves[:, :2 * RP].astype(bf16)


def build_order(counts, order_ref):
    row = lax.broadcasted_iota(jnp.int32, (128, 128), 0)
    lane = lax.broadcasted_iota(jnp.int32, (128, 128), 1)
    given = jnp.concatenate([counts[:, z, :] for z in range(2)], axis=0).astype(f32)
    tall = jnp.dot((lax.broadcasted_iota(jnp.int32, (128, 16), 0) // 8 == lax.broadcasted_iota(jnp.int32, (128, 16), 1)).astype(f32), given, preferred_element_type=f32)
    mine = lax.broadcasted_iota(jnp.int32, (128, 8), 0) % 8 == lax.broadcasted_iota(jnp.int32, (128, 8), 1)
    column = jnp.sum(jnp.where(mine, tall, 0.0), axis=1, keepdims=True)
    n = jnp.sum(jnp.where(row == lane, column, 0.0), axis=0, keepdims=True)
    ahead = jnp.where(n > column, 1.0, jnp.where(n == column, jnp.where(lane < row, 1.0, 0.0), 0.0))
    rank = jnp.sum(ahead, axis=1, keepdims=True).astype(jnp.int32)
    here = rank == lane
    order_ref[0:1, :] = jnp.sum(jnp.where(here, row.astype(f32), 0.0), axis=0, keepdims=True).astype(jnp.int32)
    order_ref[1:2, :] = jnp.sum(jnp.where(here, jnp.broadcast_to(column, (128, 128)), 0.0), axis=0, keepdims=True).astype(jnp.int32)


def advance_kernel(species, vel_hbm, diff_hbm, rates_hbm, react_hbm, prod_hbm, counts_hbm, mov_ref, first_ref, second_ref, order_ref,
                   sp, hx, ext, mv, vel_ref, diff_ref, rates_ref, react_ref, prod_ref, counts_ref, react, prod, halves, sem_in, ss, rs, sem_out):
    rows, cols = lax.axis_size("row"), lax.axis_size("col")
    me_r, me_c = lax.axis_index("row"), lax.axis_index("col")
    above = {"row": lax.rem(me_r + 1, rows), "col": me_c}
    below = {"row": lax.rem(me_r + rows - 1, rows), "col": me_c}
    right = {"row": me_r, "col": lax.rem(me_c + 1, cols)}
    left = {"row": me_r, "col": lax.rem(me_c + cols - 1, cols)}
    barrier = pltpu.get_barrier_semaphore()
    for peer in (above, below, right, left):
        pl.semaphore_signal(barrier, inc=1, device_id=peer, device_id_type=MESH)
    loads = [pltpu.make_async_copy(species.at[:, :, pl.ds(z * 128, 128)], sp.at[z], sem_in.at[z]) for z in range(2)]
    loads += [pltpu.make_async_copy(vel_hbm, vel_ref, sem_in.at[2]), pltpu.make_async_copy(diff_hbm, diff_ref, sem_in.at[3])]
    extra = [pltpu.make_async_copy(a, b, sem_in.at[4 + k]) for k, (a, b) in enumerate(((rates_hbm, rates_ref), (react_hbm, react_ref), (prod_hbm, prod_ref), (counts_hbm, counts_ref)))]
    for c in loads + extra:
        c.start()
    pl.semaphore_wait(barrier, 4)
    x_copies = []
    for z in range(2):
        zs = pl.ds(z * 128, 128)
        x_copies.append(pltpu.make_async_remote_copy(src_ref=species.at[:, pl.ds(56, 8), zs], dst_ref=hx.at[0, z], send_sem=ss.at[2 + z], recv_sem=rs.at[2 + z], device_id=above, device_id_type=MESH))
        x_copies.append(pltpu.make_async_remote_copy(src_ref=species.at[:, pl.ds(0, 8), zs], dst_ref=hx.at[1, z], send_sem=ss.at[4 + z], recv_sem=rs.at[4 + z], device_id=below, device_id_type=MESH))
    for c in x_copies:
        c.start()
    for c in loads:
        c.wait()

    def lay(x, y):
        c = x * 8 + y
        for z in range(2):
            ext[x + 1, y + 1, :NS, z * 128:(z + 1) * 128] = sp_rows(z, c)

    def sp_rows(z, c):
        return sp.at[z].reshape(NS * 64, 128)[pl.ds(c, NS, stride=64), :]

    def lay_edge(x, _):
        lay(x, 0)
        lay(x, 7)
        return 0
    lax.fori_loop(0, 8, lay_edge, 0)
    y_up = pltpu.make_async_remote_copy(src_ref=ext.at[pl.ds(1, 8), 8], dst_ref=ext.at[pl.ds(1, 8), 0], send_sem=ss.at[0], recv_sem=rs.at[0], device_id=right, device_id_type=MESH)
    y_down = pltpu.make_async_remote_copy(src_ref=ext.at[pl.ds(1, 8), 1], dst_ref=ext.at[pl.ds(1, 8), 9], send_sem=ss.at[1], recv_sem=rs.at[1], device_id=left, device_id_type=MESH)
    y_up.start()
    y_down.start()

    def lay_inner(x, _):
        for y in range(1, 7):
            lay(x, y)
        return 0
    lax.fori_loop(0, 8, lay_inner, 0)

    own = lax.broadcasted_iota(jnp.int32, (SP, NS), 0) == lax.broadcasted_iota(jnp.int32, (SP, NS), 1)
    fifth = jnp.broadcast_to(0.2 * jnp.sum(jnp.where(own, diff_ref[...], 0.0), axis=1, keepdims=True), (SP, 256))
    lane = lax.broadcasted_iota(jnp.int32, (SP, 256), 1)
    row = lax.broadcasted_iota(jnp.int32, (SP, 256), 0)

    def move(x, y):
        c = x * 8 + y
        centre = ext[x + 1, y + 1]
        near = (ext[x, y + 1], ext[x + 2, y + 1], ext[x + 1, y], ext[x + 1, y + 2],
                jnp.where(lane == 0, centre, pltpu.roll(centre, 1, 1)), jnp.where(lane == 255, centre, pltpu.roll(centre, 255, 1)))
        speeds = [0.2 * vel_ref[d, pl.ds(c, 1), :] for d in range(3)]
        still = 1.0 - (jnp.abs(speeds[0]) + jnp.abs(speeds[1]) + jnp.abs(speeds[2]))
        total = centre * (still - 6.0 * fifth)
        for d in range(3):
            total = total + near[2 * d] * (fifth + jnp.maximum(speeds[d], 0.0))
            total = total + near[2 * d + 1] * (fifth - jnp.minimum(speeds[d], 0.0))
        total = jnp.where(row < NS, total, 2.0)
        mv[c] = total[:, :128]
        mv[64 + c] = total[:, 128:]

    def inner(x, _):
        def go(y, _):
            move(x, y)
            return 0
        return lax.fori_loop(1, 7, go, 0)
    lax.fori_loop(1, 7, inner, 0)
    for c in extra:
        c.wait()
    build_matrices(rates_ref, react_ref, prod_ref, react, prod, halves, first_ref, second_ref)
    build_order(counts_ref, order_ref)
    y_up.wait()
    y_down.wait()

    @pl.when(me_c == 0)
    def _():
        ext[pl.ds(1, 8), 0] = ext[pl.ds(1, 8), 1]

    @pl.when(me_c == cols - 1)
    def _():
        ext[pl.ds(1, 8), 9] = ext[pl.ds(1, 8), 8]

    def sides(x, _):
        move(x, 0)
        move(x, 7)
        return 0
    lax.fori_loop(1, 7, sides, 0)
    middle = [pltpu.make_async_copy(mv.at[pl.ds(64 * z + 8, 48)], mov_ref.at[pl.ds(64 * z + 8, 48)], sem_out.at[z]) for z in range(2)]
    for c in middle:
        c.start()
    for c in x_copies:
        c.wait()

    def lay_halo(y, _):
        for k, at in ((0, 0), (1, 9)):
            for z in range(2):
                ext[at, y + 1, :NS, z * 128:(z + 1) * 128] = hx_rows(k, z, y)
        return 0

    def hx_rows(k, z, y):
        return hx.at[k, z].reshape(NS * 8, 128)[pl.ds(y, NS, stride=8), :]
    lax.fori_loop(0, 8, lay_halo, 0)

    @pl.when(me_r == 0)
    def _():
        ext[0, pl.ds(1, 8)] = ext[1, pl.ds(1, 8)]

    @pl.when(me_r == rows - 1)
    def _():
        ext[9, pl.ds(1, 8)] = ext[8, pl.ds(1, 8)]

    def ends(y, _):
        move(0, y)
        move(7, y)
        return 0
    lax.fori_loop(0, 8, ends, 0)
    outer = [pltpu.make_async_copy(mv.at[pl.ds(at, 8)], mov_ref.at[pl.ds(at, 8)], sem_out.at[2 + k]) for k, at in enumerate((0, 56, 64, 120))]
    for c in outer:
        c.start()
    for c in middle + outer:
        c.wait()


def advance(species, velocity, diffusivity, log_rates, reactants, products, substeps):
    vm = pl.BlockSpec(memory_space=pltpu.VMEM)
    hb = pl.BlockSpec(memory_space=pl.ANY)
    dma = pltpu.SemaphoreType.DMA
    shape = jax.ShapeDtypeStruct
    return pl.pallas_call(
        advance_kernel,
        out_shape=(shape((128, SP, 128), f32), shape((RP, 2 * SP), bf16), shape((2 * SP, 2 * RP), bf16), shape((2, 128), jnp.int32)),
        in_specs=[hb] * 7,
        out_specs=(hb, vm, vm, vm),
        scratch_shapes=[pltpu.VMEM((2, NS, 64, 128), f32), pltpu.VMEM((2, 2, NS, 8, 128), f32), pltpu.VMEM((10, 10, SP, 256), f32), pltpu.VMEM((128, SP, 128), f32),
                        pltpu.VMEM((3, 64, 256), f32), pltpu.VMEM((1, NS), f32), pltpu.VMEM((NR,), f32), pltpu.VMEM((NS, NR), jnp.int32), pltpu.VMEM((NS, NR), jnp.int32),
                        pltpu.VMEM((8, 2, 8), jnp.int32), pltpu.VMEM((128, 384), f32), pltpu.VMEM((128, 384), f32), pltpu.VMEM((2 * SP, RP + 384), f32), dma((8,)), dma((6,)), dma((6,)), dma((6,))],
        compiler_params=pltpu.CompilerParams(collective_id=0, has_side_effects=True, vmem_limit_bytes=60 << 20),
        name="advance",
    )(species.reshape(NS, 64, 256), velocity.reshape(3, 64, 256), diffusivity[None, :], log_rates, reactants.T, products.T, jnp.transpose(substeps, (0, 2, 1)))


def kinetics_kernel(G, order_ref, size_ref, mov_hbm, weight_hbm, s1_hbm, s2_hbm, out_ref, heat_ref, mov, cur, outs, weight_ref, s1_ref, s2_ref, sem, arrive):
    turns = 128 // G

    def fetch(t, slot):
        return [pltpu.make_async_copy(mov_hbm.at[order_ref[0, t * G + j]], mov.at[slot, j], arrive.at[slot]) for j in range(G)]
    for c in fetch(0, 0):
        c.start()
    constants = [pltpu.make_async_copy(a, b, sem.at[k]) for k, (a, b) in enumerate(((weight_hbm, weight_ref), (s1_hbm, s1_ref), (s2_hbm, s2_ref)))]
    for c in constants:
        c.start()
    for c in constants:
        c.wait()
    own = lax.broadcasted_iota(jnp.int32, (SP, NS), 0) == lax.broadcasted_iota(jnp.int32, (SP, NS), 1)
    weight = jnp.broadcast_to(jnp.sum(jnp.where(own, weight_ref[...], 0.0), axis=1, keepdims=True) / time_step, (SP, 128))
    W = G * 128

    def turn(t, _):
        slot = t % 2

        @pl.when(t + 1 < turns)
        def _():
            for c in fetch(t + 1, 1 - slot):
                c.start()
        ids = [order_ref[0, t * G + j] for j in range(G)]
        ns = [order_ref[1, t * G + j] for j in range(G)]
        for c in fetch(t, slot):
            c.wait()
        for j in range(G):
            cur[:, j * 128:(j + 1) * 128] = mov[slot, j]
        h = jnp.concatenate([jnp.full((SP, 128), size_ref[n], f32) for n in ns], axis=1)
        nb = jnp.concatenate([jnp.full((SP, 128), n, jnp.int32) for n in ns], axis=1)

        def level(k, _):
            conc = cur[...]
            lg = jnp.log2(conc)
            hi = lg.astype(bf16).astype(f32)
            xin = jnp.concatenate([hi, lg - hi], axis=0).astype(bf16)
            rates = jnp.exp2(jnp.dot(s1_ref[...], xin, preferred_element_type=f32))
            rhi = rates.astype(bf16)
            rlo = (rates - rhi.astype(f32)).astype(bf16)
            both = jnp.dot(s2_ref[...], jnp.concatenate([rhi, rlo], axis=0), preferred_element_type=f32)
            fresh = conc * (conc + h * both[:SP]) / (conc + h * both[SP:])
            cur[...] = jnp.where(nb > k, fresh, conc)
            return 0
        lax.fori_loop(0, ns[0], level, 0)
        for j in range(G):
            c, z = ids[j] % 64, ids[j] // 64
            res = cur[:, j * 128:(j + 1) * 128]
            outs[z, pl.ds(c, NS, stride=64), :] = res[:NS]
            heat_ref[z, pl.ds(c, 1), :] = jnp.sum(weight * (res - mov[slot, j]), axis=0, keepdims=True)
        return 0
    lax.fori_loop(0, turns, turn, 0)
    stores = [pltpu.make_async_copy(outs.at[z], out_ref.at[:, pl.ds(z * 128, 128)], sem.at[z]) for z in range(2)]
    for c in stores:
        c.start()
    for c in stores:
        c.wait()


def kinetics(G, moved, order, heat_weights, first, second):
    vm = pl.BlockSpec(memory_space=pltpu.VMEM)
    sm = pl.BlockSpec(memory_space=pltpu.SMEM)
    hb = pl.BlockSpec(memory_space=pl.ANY)
    sizes = np.array([0.0] + [time_step / n for n in range(1, 8)], np.float32)
    return pl.pallas_call(
        functools.partial(kinetics_kernel, G),
        out_shape=(jax.ShapeDtypeStruct((NS * 64, 256), f32), jax.ShapeDtypeStruct((2, 64, 128), f32)),
        in_specs=[sm, sm, hb, hb, hb, hb],
        out_specs=(hb, vm),
        scratch_shapes=[
            pltpu.VMEM((2, G, SP, 128), f32), pltpu.VMEM((SP, G * 128), f32), pltpu.VMEM((2, NS * 64, 128), f32), pltpu.VMEM((1, NS), f32),
            pltpu.VMEM((RP, 2 * SP), bf16), pltpu.VMEM((2 * SP, 2 * RP), bf16), pltpu.SemaphoreType.DMA((3,)), pltpu.SemaphoreType.DMA((2,))],
        compiler_params=pltpu.CompilerParams(vmem_limit_bytes=60 << 20),
        name="kinetics",
    )(order, jnp.asarray(sizes), moved, heat_weights[None, :], first, second)


def cosine_table(length):
    wave = np.arange(length)[:, None]
    sample = np.arange(length)[None, :] + 0.5
    weight = np.sqrt(np.where(wave == 0, 1.0, 2.0) / length)
    return (weight * np.cos(np.pi * wave * sample / length)).astype(np.float32)


def mode_values(length):
    return 2.0 - 2.0 * np.cos(np.pi * np.arange(length) / length)


def exact_dot(a, b, dims):
    return lax.dot_general(a, b, (dims, ((), ())), precision=highest, preferred_element_type=f32)


def solve_kernel(heat_hbm, div_hbm, tz_hbm, tx_hbm, ty_hbm, shift_hbm, ly_hbm, out_ref,
                 heat_ref, div_ref, tz_ref, tx_ref, ty_ref, shift_ref, ly_ref, sem_in,
                 f1, send1, recv1, yv, send2, recv2, recv3, yb, send4, recv4, fp,
                 ss1, rs1, ss2, rs2, ss3, rs3, ss4, rs4):
    rows, cols = 8, 16
    me_r, me_c = lax.axis_index("row"), lax.axis_index("col")
    pairs = ((heat_hbm, heat_ref), (div_hbm, div_ref), (tz_hbm, tz_ref), (tx_hbm, tx_ref), (ty_hbm, ty_ref), (shift_hbm, shift_ref), (ly_hbm, ly_ref))
    loads = [pltpu.make_async_copy(a, b, sem_in.at[k]) for k, (a, b) in enumerate(pairs)]
    for c in loads:
        c.start()
    barrier = pltpu.get_barrier_semaphore()
    for d in range(1, rows):
        pl.semaphore_signal(barrier, inc=1, device_id={"row": lax.rem(me_r + d, rows), "col": me_c}, device_id_type=pl.DeviceIdType.MESH)
    for d in range(1, cols):
        pl.semaphore_signal(barrier, inc=1, device_id={"row": me_r, "col": lax.rem(me_c + d, cols)}, device_id_type=pl.DeviceIdType.MESH)

    def row_copy(send, recv, ss, rs, d):
        to = lax.rem(me_r + d, rows)
        return pltpu.make_async_remote_copy(src_ref=send.at[to], dst_ref=recv.at[me_r], send_sem=ss.at[d], recv_sem=rs.at[me_r],
                                            device_id={"row": to, "col": me_c}, device_id_type=pl.DeviceIdType.MESH)

    def col_copy(send, recv, ss, rs, d):
        to = lax.rem(me_c + d, cols)
        return pltpu.make_async_remote_copy(src_ref=send.at[to], dst_ref=recv.at[me_c], send_sem=ss.at[d], recv_sem=rs.at[me_c],
                                            device_id={"row": me_r, "col": to}, device_id_type=pl.DeviceIdType.MESH)

    def row_arrival(send, recv, ss, rs, d):
        come = lax.rem(me_r + d, rows)
        return pltpu.make_async_remote_copy(src_ref=send.at[come], dst_ref=recv.at[come], send_sem=ss.at[d], recv_sem=rs.at[come],
                                            device_id={"row": come, "col": me_c}, device_id_type=pl.DeviceIdType.MESH)

    def col_arrival(send, recv, ss, rs, d):
        come = lax.rem(me_c + d, cols)
        return pltpu.make_async_remote_copy(src_ref=send.at[come], dst_ref=recv.at[come], send_sem=ss.at[d], recv_sem=rs.at[come],
                                            device_id={"row": me_r, "col": come}, device_id_type=pl.DeviceIdType.MESH)

    lane = lax.broadcasted_iota(jnp.int32, (8, 128), 1)
    part = lane // 32
    for c in loads:
        c.wait()
    source = div_ref[...] - jnp.concatenate([heat_ref[0], heat_ref[1]], axis=1)
    forward = exact_dot(source, tz_ref[...], ((1,), (1,)))
    f1[0] = forward[:, :128]
    f1[1] = forward[:, 128:]
    for kh in range(2):
        for h in range(2):
            v = [f1[kh, pl.ds(4 * h + p, 8, stride=8), :] for p in range(4)]
            for q in range(4):
                tile = jnp.zeros((8, 128), f32)
                for p in range(4):
                    s = (p - q) * 32 % 128
                    tile = jnp.where(part == p, pltpu.roll(v[p], s, 1) if s else v[p], tile)
                send1[kh * 4 + q, :, h * 128:(h + 1) * 128] = tile
    pl.semaphore_wait(barrier, rows - 1 + cols - 1)
    sent = [row_copy(send1, recv1, ss1, rs1, d) for d in range(1, rows)]
    for c in sent:
        c.start()
    recv1[me_r] = send1[me_r]
    for d in range(1, rows):
        row_arrival(send1, recv1, ss1, rs1, d).wait_recv()
    for c in sent:
        c.wait_send()
    block = recv1[...].reshape(64, 256)
    tx = tx_ref[...]
    yv[...] = exact_dot(jnp.transpose(block), jnp.concatenate([tx, tx], axis=0), ((1,), (1,)))
    for c in range(cols):
        send2[c] = jnp.where(lane < 64, yv[pl.ds(2 * c, 8, stride=32), :], yv[pl.ds(2 * c + 1, 8, stride=32), :])
    sent = [col_copy(send2, recv2, ss2, rs2, d) for d in range(1, cols)]
    for c in sent:
        c.start()
    recv2[me_c] = send2[me_c]
    for d in range(1, cols):
        col_arrival(send2, recv2, ss2, rs2, d).wait_recv()
    for c in sent:
        c.wait_send()
    ty = ty_ref[...]
    spectrum = exact_dot(ty, recv2[...].reshape(128, 128), ((1,), (0,)))
    shift = shift_ref[pl.ds(me_r * cols + me_c, 1), :]
    spectrum = spectrum / (ly_ref[...] + shift)
    send2[...] = exact_dot(ty, spectrum, ((0,), (0,))).reshape(cols, 8, 128)
    sent = [col_copy(send2, recv3, ss3, rs3, d) for d in range(1, cols)]
    for c in sent:
        c.start()
    recv3[me_c] = send2[me_c]
    for d in range(1, cols):
        col_arrival(send2, recv3, ss3, rs3, d).wait_recv()
    for c in sent:
        c.wait_send()
    for c in range(cols):
        tile = recv3[c]
        yb[pl.ds(2 * c, 8, stride=32), :] = jnp.where(lane < 64, tile, 0.0)
        yb[pl.ds(2 * c + 1, 8, stride=32), :] = jnp.where(lane < 64, 0.0, tile)
    txt = jnp.transpose(tx)
    send4[...] = exact_dot(jnp.concatenate([txt, txt], axis=1), yb[...], ((1,), (1,))).reshape(8, 8, 256)
    sent = [row_copy(send4, recv4, ss4, rs4, d) for d in range(1, rows)]
    for c in sent:
        c.start()
    recv4[me_r] = send4[me_r]
    for d in range(1, rows):
        row_arrival(send4, recv4, ss4, rs4, d).wait_recv()
    for c in sent:
        c.wait_send()
    for kh in range(2):
        for h in range(2):
            v = [recv4[kh * 4 + q, :, h * 128:(h + 1) * 128] for q in range(4)]
            for p in range(4):
                tile = jnp.zeros((8, 128), f32)
                for q in range(4):
                    s = (q - p) * 32 % 128
                    tile = jnp.where(part == q, pltpu.roll(v[q], s, 1) if s else v[q], tile)
                fp[kh, pl.ds(4 * h + p, 8, stride=8), :] = tile
    out_ref[...] = exact_dot(jnp.concatenate([fp[0], fp[1]], axis=1), tz_ref[...], ((1,), (0,)))


def solve(heat, divergence):
    lx, ly, lz = mode_values(64), mode_values(128), mode_values(256)
    device = np.arange(128)
    lanes = np.arange(128)
    shift = screen + lx[lanes % 64][None, :] + lz[(device // 16 * 32 + device % 16 * 2)[:, None] + (lanes // 64)[None, :]]
    vm = pl.BlockSpec(memory_space=pltpu.VMEM)
    hb = pl.BlockSpec(memory_space=pl.ANY)
    dma = pltpu.SemaphoreType.DMA
    out = pl.pallas_call(
        solve_kernel,
        out_shape=jax.ShapeDtypeStruct((64, 256), f32),
        in_specs=[hb] * 7,
        out_specs=vm,
        scratch_shapes=[
            pltpu.VMEM((2, 64, 128), f32), pltpu.VMEM((64, 256), f32), pltpu.VMEM((256, 256), f32), pltpu.VMEM((64, 64), f32), pltpu.VMEM((128, 128), f32),
            pltpu.VMEM((128, 128), f32), pltpu.VMEM((128, 128), f32), dma((7,)),
            pltpu.VMEM((2, 64, 128), f32), pltpu.VMEM((8, 8, 256), f32), pltpu.VMEM((8, 8, 256), f32), pltpu.VMEM((256, 128), f32),
            pltpu.VMEM((16, 8, 128), f32), pltpu.VMEM((16, 8, 128), f32), pltpu.VMEM((16, 8, 128), f32), pltpu.VMEM((256, 128), f32),
            pltpu.VMEM((8, 8, 256), f32), pltpu.VMEM((8, 8, 256), f32), pltpu.VMEM((2, 64, 128), f32),
            dma((8,)), dma((8,)), dma((16,)), dma((16,)), dma((16,)), dma((16,)), dma((8,)), dma((8,))],
        compiler_params=pltpu.CompilerParams(collective_id=1, has_side_effects=True, vmem_limit_bytes=60 << 20),
        name="screened_solve",
    )(heat, divergence.reshape(64, 256), jnp.asarray(cosine_table(256)), jnp.asarray(cosine_table(64)), jnp.asarray(cosine_table(128)),
      jnp.asarray(shift.astype(np.float32)), jnp.asarray(np.broadcast_to(ly[:, None], (128, 128)).astype(np.float32)))
    return out.reshape(8, 8, 256)


def local(species, velocity, diffusivity, divergence, log_rates, reactants, products, heat_weights, substeps):
    moved, first, second, order = advance(species, velocity, diffusivity, log_rates, reactants, products, substeps)
    reacted, heat = kinetics(16, moved, order, heat_weights, first, second)
    pressure = solve(heat, divergence)
    return reacted.reshape(species.shape), pressure


def solution(mesh):
    cells = P("row", "col", None)
    fields = P(None, "row", "col", None)
    in_specs = (fields, fields, P(), cells, P(), P(), P(), P(), cells)
    return jax.shard_map(local, mesh=mesh, in_specs=in_specs, out_specs=(fields, cells), check_vma=False)
```

```python
import functools

import jax
import jax.numpy as jnp
import numpy as np
from jax import lax
from jax.experimental import pallas as pl
from jax.experimental.pallas import tpu as pltpu
from jax.sharding import PartitionSpec as P

f32, bf16 = jnp.float32, jnp.bfloat16
MESH = pl.DeviceIdType.MESH
NS, SP = 53, 56
NR, RP = 325, 336
LOG2E = 1.4426950408889634
time_step = 0.2
screen = 0.004
highest = lax.Precision.HIGHEST

def split3(x):
    hi = x.astype(bf16).astype(f32)
    mid = (x - hi).astype(bf16).astype(f32)
    return hi, mid, x - hi - mid


def build_matrices(log_rates, react_ref, prod_ref, react, prod, halves, first_ref, second_ref):
    react[...] = jnp.zeros_like(react)
    prod[...] = jnp.zeros_like(prod)
    react[:NS, :NR] = react_ref[...].astype(f32)
    prod[:NS, :NR] = prod_ref[...].astype(f32)
    rt, pt = react[...], prod[...]
    rp = jnp.transpose(rt)[:RP]
    own = lax.broadcasted_iota(jnp.int32, (RP, NR), 0) == lax.broadcasted_iota(jnp.int32, (RP, NR), 1)
    hi, mid, low = split3(jnp.sum(jnp.where(own, log_rates[...].reshape(1, NR), 0.0), axis=1, keepdims=True) * LOG2E)
    lane = lax.broadcasted_iota(jnp.int32, (RP, 128), 1)
    later = pltpu.roll(rp, SP, 1)
    both = jnp.where(lane == NS, hi, jnp.where(lane == NS + 1, mid, jnp.where(lane == NS + 2, low, rp + later)))
    first_ref[...] = both[:, :2 * SP].astype(bf16)
    outcome = jnp.concatenate([pt[:SP], rt[:SP]], axis=0)
    halves[:, :384] = outcome
    halves[:, RP:RP + 384] = outcome
    second_ref[...] = halves[:, :2 * RP].astype(bf16)


def build_order(counts, order_ref):
    row = lax.broadcasted_iota(jnp.int32, (128, 128), 0)
    lane = lax.broadcasted_iota(jnp.int32, (128, 128), 1)
    given = jnp.concatenate([counts[:, z, :] for z in range(2)], axis=0).astype(f32)
    tall = jnp.dot((lax.broadcasted_iota(jnp.int32, (128, 16), 0) // 8 == lax.broadcasted_iota(jnp.int32, (128, 16), 1)).astype(f32), given, preferred_element_type=f32)
    mine = lax.broadcasted_iota(jnp.int32, (128, 8), 0) % 8 == lax.broadcasted_iota(jnp.int32, (128, 8), 1)
    column = jnp.sum(jnp.where(mine, tall, 0.0), axis=1, keepdims=True)
    n = jnp.sum(jnp.where(row == lane, column, 0.0), axis=0, keepdims=True)
    ahead = jnp.where(n > column, 1.0, jnp.where(n == column, jnp.where(lane < row, 1.0, 0.0), 0.0))
    rank = jnp.sum(ahead, axis=1, keepdims=True).astype(jnp.int32)
    here = rank == lane
    order_ref[0:1, :] = jnp.sum(jnp.where(here, row.astype(f32), 0.0), axis=0, keepdims=True).astype(jnp.int32)
    order_ref[1:2, :] = jnp.sum(jnp.where(here, jnp.broadcast_to(column, (128, 128)), 0.0), axis=0, keepdims=True).astype(jnp.int32)


def advance_kernel(species, vel_hbm, diff_hbm, rates_hbm, react_hbm, prod_hbm, counts_hbm, mov_ref, first_ref, second_ref, order_ref,
                   hx, ext, mv, vel_ref, diff_ref, rates_ref, react_ref, prod_ref, counts_ref, react, prod, halves, sem_in, ss, rs, sem_out):
    rows, cols = lax.axis_size("row"), lax.axis_size("col")
    me_r, me_c = lax.axis_index("row"), lax.axis_index("col")
    above = {"row": lax.rem(me_r + 1, rows), "col": me_c}
    below = {"row": lax.rem(me_r + rows - 1, rows), "col": me_c}
    right = {"row": me_r, "col": lax.rem(me_c + 1, cols)}
    left = {"row": me_r, "col": lax.rem(me_c + cols - 1, cols)}
    barrier = pltpu.get_barrier_semaphore()
    for peer in (above, below, right, left):
        pl.semaphore_signal(barrier, inc=1, device_id=peer, device_id_type=MESH)
    def column(x, y, z, sem):
        zs = pl.ds(z * 128, 128)
        return pltpu.make_async_copy(species.at[:, x * 8 + y, zs], ext.at[x + 1, y + 1, z, pl.ds(0, NS)], sem)

    def arrived(count, sem):
        whole = mv.at[pl.ds(0, count), pl.ds(0, NS)]
        pltpu.make_async_copy(whole, whole, sem).wait()

    def edge_columns(x, _):
        for y in (0, 7):
            for z in range(2):
                column(x, y, z, sem_in.at[0]).start()
        return 0
    lax.fori_loop(0, 8, edge_columns, 0)
    extra = [pltpu.make_async_copy(a, b, sem_in.at[9 + k]) for k, (a, b) in enumerate(((vel_hbm, vel_ref), (diff_hbm, diff_ref), (rates_hbm, rates_ref), (react_hbm, react_ref), (prod_hbm, prod_ref), (counts_hbm, counts_ref)))]
    for c in extra:
        c.start()
    pl.semaphore_wait(barrier, 4)
    x_copies = []
    for z in range(2):
        zs = pl.ds(z * 128, 128)
        x_copies.append(pltpu.make_async_remote_copy(src_ref=species.at[:, pl.ds(56, 8), zs], dst_ref=hx.at[0, z], send_sem=ss.at[2 + z], recv_sem=rs.at[2 + z], device_id=above, device_id_type=MESH))
        x_copies.append(pltpu.make_async_remote_copy(src_ref=species.at[:, pl.ds(0, 8), zs], dst_ref=hx.at[1, z], send_sem=ss.at[4 + z], recv_sem=rs.at[4 + z], device_id=below, device_id_type=MESH))
    for c in x_copies:
        c.start()
    def inner_columns(x, _):
        for y in range(1, 7):
            for z in range(2):
                column(x, y, z, sem_in.at[1 + x]).start()
        return 0
    lax.fori_loop(0, 8, inner_columns, 0)
    arrived(32, sem_in.at[0])
    y_up = pltpu.make_async_remote_copy(src_ref=ext.at[pl.ds(1, 8), 8], dst_ref=ext.at[pl.ds(1, 8), 0], send_sem=ss.at[0], recv_sem=rs.at[0], device_id=right, device_id_type=MESH)
    y_down = pltpu.make_async_remote_copy(src_ref=ext.at[pl.ds(1, 8), 1], dst_ref=ext.at[pl.ds(1, 8), 9], send_sem=ss.at[1], recv_sem=rs.at[1], device_id=left, device_id_type=MESH)
    y_up.start()
    y_down.start()

    for c in extra:
        c.wait()
    own = lax.broadcasted_iota(jnp.int32, (SP, NS), 0) == lax.broadcasted_iota(jnp.int32, (SP, NS), 1)
    fifth = jnp.broadcast_to(0.2 * jnp.sum(jnp.where(own, diff_ref[...], 0.0), axis=1, keepdims=True), (SP, 256))
    lane = lax.broadcasted_iota(jnp.int32, (SP, 256), 1)
    row = lax.broadcasted_iota(jnp.int32, (SP, 256), 0)

    def move(x, y):
        c = x * 8 + y
        def cells(at, to):
            return jnp.concatenate([ext[at, to, 0], ext[at, to, 1]], axis=1)
        centre = cells(x + 1, y + 1)
        near = (cells(x, y + 1), cells(x + 2, y + 1), cells(x + 1, y), cells(x + 1, y + 2),
                jnp.where(lane == 0, centre, pltpu.roll(centre, 1, 1)), jnp.where(lane == 255, centre, pltpu.roll(centre, 255, 1)))
        speeds = [0.2 * vel_ref[d, pl.ds(c, 1), :] for d in range(3)]
        still = 1.0 - (jnp.abs(speeds[0]) + jnp.abs(speeds[1]) + jnp.abs(speeds[2]))
        total = centre * (still - 6.0 * fifth)
        for d in range(3):
            total = total + near[2 * d] * (fifth + jnp.maximum(speeds[d], 0.0))
            total = total + near[2 * d + 1] * (fifth - jnp.minimum(speeds[d], 0.0))
        total = jnp.where(row < NS, total, 2.0)
        mv[c] = total[:, :128]
        mv[64 + c] = total[:, 128:]

    arrived(12, sem_in.at[1])
    arrived(12, sem_in.at[2])

    def inner(x, _):
        arrived(12, sem_in.at[2 + x])

        def go(y, _):
            move(x, y)
            return 0
        return lax.fori_loop(1, 7, go, 0)
    lax.fori_loop(1, 7, inner, 0)
    build_matrices(rates_ref, react_ref, prod_ref, react, prod, halves, first_ref, second_ref)
    build_order(counts_ref, order_ref)
    y_up.wait()
    y_down.wait()

    @pl.when(me_c == 0)
    def _():
        ext[pl.ds(1, 8), 0] = ext[pl.ds(1, 8), 1]

    @pl.when(me_c == cols - 1)
    def _():
        ext[pl.ds(1, 8), 9] = ext[pl.ds(1, 8), 8]

    def sides(x, _):
        move(x, 0)
        move(x, 7)
        return 0
    lax.fori_loop(1, 7, sides, 0)
    middle = [pltpu.make_async_copy(mv.at[pl.ds(64 * z + 8, 48)], mov_ref.at[pl.ds(64 * z + 8, 48)], sem_out.at[z]) for z in range(2)]
    for c in middle:
        c.start()
    for c in x_copies:
        c.wait()

    def lay_halo(y, _):
        for k, at in ((0, 0), (1, 9)):
            for z in range(2):
                ext[at, y + 1, z, :NS, :] = hx_rows(k, z, y)
        return 0

    def hx_rows(k, z, y):
        return hx.at[k, z].reshape(NS * 8, 128)[pl.ds(y, NS, stride=8), :]
    lax.fori_loop(0, 8, lay_halo, 0)

    @pl.when(me_r == 0)
    def _():
        ext[0, pl.ds(1, 8)] = ext[1, pl.ds(1, 8)]

    @pl.when(me_r == rows - 1)
    def _():
        ext[9, pl.ds(1, 8)] = ext[8, pl.ds(1, 8)]

    def ends(y, _):
        move(0, y)
        move(7, y)
        return 0
    lax.fori_loop(0, 8, ends, 0)
    outer = [pltpu.make_async_copy(mv.at[pl.ds(at, 8)], mov_ref.at[pl.ds(at, 8)], sem_out.at[2 + k]) for k, at in enumerate((0, 56, 64, 120))]
    for c in outer:
        c.start()
    for c in middle + outer:
        c.wait()


def advance(species, velocity, diffusivity, log_rates, reactants, products, substeps):
    vm = pl.BlockSpec(memory_space=pltpu.VMEM)
    hb = pl.BlockSpec(memory_space=pl.ANY)
    dma = pltpu.SemaphoreType.DMA
    shape = jax.ShapeDtypeStruct
    return pl.pallas_call(
        advance_kernel,
        out_shape=(shape((128, SP, 128), f32), shape((RP, 2 * SP), bf16), shape((2 * SP, 2 * RP), bf16), shape((2, 128), jnp.int32)),
        in_specs=[hb] * 7,
        out_specs=(hb, vm, vm, vm),
        scratch_shapes=[pltpu.VMEM((2, 2, NS, 8, 128), f32), pltpu.VMEM((10, 10, 2, SP, 128), f32), pltpu.VMEM((128, SP, 128), f32),
                        pltpu.VMEM((3, 64, 256), f32), pltpu.VMEM((1, NS), f32), pltpu.VMEM((NR,), f32), pltpu.VMEM((NS, NR), jnp.int32), pltpu.VMEM((NS, NR), jnp.int32),
                        pltpu.VMEM((8, 2, 8), jnp.int32), pltpu.VMEM((128, 384), f32), pltpu.VMEM((128, 384), f32), pltpu.VMEM((2 * SP, RP + 384), f32), dma((15,)), dma((6,)), dma((6,)), dma((6,))],
        compiler_params=pltpu.CompilerParams(collective_id=0, has_side_effects=True, vmem_limit_bytes=60 << 20),
        name="advance",
    )(species.reshape(NS, 64, 256), velocity.reshape(3, 64, 256), diffusivity[None, :], log_rates, reactants.T, products.T, jnp.transpose(substeps, (0, 2, 1)))


def kinetics_kernel(G, order_ref, size_ref, mov_hbm, weight_hbm, s1_hbm, s2_hbm, out_ref, heat_ref, mov, cur, stage, depart, weight_ref, s1_ref, s2_ref, sem, arrive):
    turns = 128 // G

    def fetch(t, slot):
        return [pltpu.make_async_copy(mov_hbm.at[order_ref[0, t * G + j]], mov.at[slot, j], arrive.at[slot]) for j in range(G)]
    def leave(t, slot):
        made = []
        for j in range(G):
            i = order_ref[0, t * G + j]
            made.append(pltpu.make_async_copy(stage.at[slot, j, pl.ds(0, NS)], out_ref.at[:, i % 64, pl.ds(pl.multiple_of(i // 64 * 128, 128), 128)], depart.at[slot]))
        return made

    for c in fetch(0, 0):
        c.start()
    constants = [pltpu.make_async_copy(a, b, sem.at[k]) for k, (a, b) in enumerate(((weight_hbm, weight_ref), (s1_hbm, s1_ref), (s2_hbm, s2_ref)))]
    for c in constants:
        c.start()
    for c in constants:
        c.wait()
    own = lax.broadcasted_iota(jnp.int32, (SP, NS), 0) == lax.broadcasted_iota(jnp.int32, (SP, NS), 1)
    weight = jnp.broadcast_to(jnp.sum(jnp.where(own, weight_ref[...], 0.0), axis=1, keepdims=True) / time_step, (SP, 128))
    W = G * 128

    def turn(t, _):
        slot = t % 2

        @pl.when(t + 1 < turns)
        def _():
            for c in fetch(t + 1, 1 - slot):
                c.start()
        ids = [order_ref[0, t * G + j] for j in range(G)]
        ns = [order_ref[1, t * G + j] for j in range(G)]
        for c in fetch(t, slot):
            c.wait()
        for j in range(G):
            cur[:, j * 128:(j + 1) * 128] = mov[slot, j]
        h = jnp.concatenate([jnp.full((SP, 128), size_ref[n], f32) for n in ns], axis=1)
        nb = jnp.concatenate([jnp.full((SP, 128), n, jnp.int32) for n in ns], axis=1)

        def level(k, _):
            conc = cur[...]
            lg = jnp.log2(conc)
            hi = lg.astype(bf16).astype(f32)
            xin = jnp.concatenate([hi, lg - hi], axis=0).astype(bf16)
            rates = jnp.exp2(jnp.dot(s1_ref[...], xin, preferred_element_type=f32))
            rhi = rates.astype(bf16)
            rlo = (rates - rhi.astype(f32)).astype(bf16)
            both = jnp.dot(s2_ref[...], jnp.concatenate([rhi, rlo], axis=0), preferred_element_type=f32)
            fresh = conc * (conc + h * both[:SP]) / (conc + h * both[SP:])
            cur[...] = jnp.where(nb > k, fresh, conc)
            return 0
        lax.fori_loop(0, ns[0], level, 0)
        @pl.when(t >= 2)
        def _():
            for c in leave(t, slot):
                c.wait()
        for j in range(G):
            c, z = ids[j] % 64, ids[j] // 64
            res = cur[:, j * 128:(j + 1) * 128]
            stage[slot, j] = res
            heat_ref[z, pl.ds(c, 1), :] = jnp.sum(weight * (res - mov[slot, j]), axis=0, keepdims=True)
        for c in leave(t, slot):
            c.start()
        return 0
    lax.fori_loop(0, turns, turn, 0)
    for slot in range(2):
        for c in leave(slot, slot):
            c.wait()


def kinetics(G, moved, order, heat_weights, first, second):
    vm = pl.BlockSpec(memory_space=pltpu.VMEM)
    sm = pl.BlockSpec(memory_space=pltpu.SMEM)
    hb = pl.BlockSpec(memory_space=pl.ANY)
    sizes = np.array([0.0] + [time_step / n for n in range(1, 8)], np.float32)
    return pl.pallas_call(
        functools.partial(kinetics_kernel, G),
        out_shape=(jax.ShapeDtypeStruct((NS, 64, 256), f32), jax.ShapeDtypeStruct((2, 64, 128), f32)),
        in_specs=[sm, sm, hb, hb, hb, hb],
        out_specs=(hb, vm),
        scratch_shapes=[
            pltpu.VMEM((2, G, SP, 128), f32), pltpu.VMEM((SP, G * 128), f32), pltpu.VMEM((2, G, SP, 128), f32), pltpu.SemaphoreType.DMA((2,)), pltpu.VMEM((1, NS), f32),
            pltpu.VMEM((RP, 2 * SP), bf16), pltpu.VMEM((2 * SP, 2 * RP), bf16), pltpu.SemaphoreType.DMA((3,)), pltpu.SemaphoreType.DMA((2,))],
        compiler_params=pltpu.CompilerParams(vmem_limit_bytes=60 << 20),
        name="kinetics",
    )(order, jnp.asarray(sizes), moved, heat_weights[None, :], first, second)


def cosine_table(length):
    wave = np.arange(length)[:, None]
    sample = np.arange(length)[None, :] + 0.5
    weight = np.sqrt(np.where(wave == 0, 1.0, 2.0) / length)
    return (weight * np.cos(np.pi * wave * sample / length)).astype(np.float32)


def mode_values(length):
    return 2.0 - 2.0 * np.cos(np.pi * np.arange(length) / length)


def exact_dot(a, b, dims):
    return lax.dot_general(a, b, (dims, ((), ())), precision=highest, preferred_element_type=f32)


def solve_kernel(heat_hbm, div_hbm, tz_hbm, tx_hbm, ty_hbm, shift_hbm, ly_hbm, out_ref,
                 heat_ref, div_ref, tz_ref, tx_ref, ty_ref, shift_ref, ly_ref, sem_in,
                 f1, send1, recv1, yv, send2, recv2, recv3, yb, send4, recv4, fp,
                 ss1, rs1, ss2, rs2, ss3, rs3, ss4, rs4):
    rows, cols = 8, 16
    me_r, me_c = lax.axis_index("row"), lax.axis_index("col")
    pairs = ((heat_hbm, heat_ref), (div_hbm, div_ref), (tz_hbm, tz_ref), (tx_hbm, tx_ref), (ty_hbm, ty_ref), (shift_hbm, shift_ref), (ly_hbm, ly_ref))
    loads = [pltpu.make_async_copy(a, b, sem_in.at[k]) for k, (a, b) in enumerate(pairs)]
    for c in loads:
        c.start()
    barrier = pltpu.get_barrier_semaphore()
    for d in range(1, rows):
        pl.semaphore_signal(barrier, inc=1, device_id={"row": lax.rem(me_r + d, rows), "col": me_c}, device_id_type=pl.DeviceIdType.MESH)
    for d in range(1, cols):
        pl.semaphore_signal(barrier, inc=1, device_id={"row": me_r, "col": lax.rem(me_c + d, cols)}, device_id_type=pl.DeviceIdType.MESH)

    def row_copy(send, recv, ss, rs, d):
        to = lax.rem(me_r + d, rows)
        return pltpu.make_async_remote_copy(src_ref=send.at[to], dst_ref=recv.at[me_r], send_sem=ss.at[d], recv_sem=rs.at[me_r],
                                            device_id={"row": to, "col": me_c}, device_id_type=pl.DeviceIdType.MESH)

    def col_copy(send, recv, ss, rs, d):
        to = lax.rem(me_c + d, cols)
        return pltpu.make_async_remote_copy(src_ref=send.at[to], dst_ref=recv.at[me_c], send_sem=ss.at[d], recv_sem=rs.at[me_c],
                                            device_id={"row": me_r, "col": to}, device_id_type=pl.DeviceIdType.MESH)

    def row_arrival(send, recv, ss, rs, d):
        come = lax.rem(me_r + d, rows)
        return pltpu.make_async_remote_copy(src_ref=send.at[come], dst_ref=recv.at[come], send_sem=ss.at[d], recv_sem=rs.at[come],
                                            device_id={"row": come, "col": me_c}, device_id_type=pl.DeviceIdType.MESH)

    def col_arrival(send, recv, ss, rs, d):
        come = lax.rem(me_c + d, cols)
        return pltpu.make_async_remote_copy(src_ref=send.at[come], dst_ref=recv.at[come], send_sem=ss.at[d], recv_sem=rs.at[come],
                                            device_id={"row": me_r, "col": come}, device_id_type=pl.DeviceIdType.MESH)

    lane = lax.broadcasted_iota(jnp.int32, (8, 128), 1)
    part = lane // 32
    for c in loads:
        c.wait()
    source = div_ref[...] - jnp.concatenate([heat_ref[0], heat_ref[1]], axis=1)
    forward = exact_dot(source, tz_ref[...], ((1,), (1,)))
    f1[0] = forward[:, :128]
    f1[1] = forward[:, 128:]
    for kh in range(2):
        for h in range(2):
            v = [f1[kh, pl.ds(4 * h + p, 8, stride=8), :] for p in range(4)]
            for q in range(4):
                tile = jnp.zeros((8, 128), f32)
                for p in range(4):
                    s = (p - q) * 32 % 128
                    tile = jnp.where(part == p, pltpu.roll(v[p], s, 1) if s else v[p], tile)
                send1[kh * 4 + q, :, h * 128:(h + 1) * 128] = tile
    pl.semaphore_wait(barrier, rows - 1 + cols - 1)
    sent = [row_copy(send1, recv1, ss1, rs1, d) for d in range(1, rows)]
    for c in sent:
        c.start()
    recv1[me_r] = send1[me_r]
    for d in range(1, rows):
        row_arrival(send1, recv1, ss1, rs1, d).wait_recv()
    for c in sent:
        c.wait_send()
    block = recv1[...].reshape(64, 256)
    tx = tx_ref[...]
    yv[...] = exact_dot(jnp.transpose(block), jnp.concatenate([tx, tx], axis=0), ((1,), (1,)))
    for c in range(cols):
        send2[c] = jnp.where(lane < 64, yv[pl.ds(2 * c, 8, stride=32), :], yv[pl.ds(2 * c + 1, 8, stride=32), :])
    sent = [col_copy(send2, recv2, ss2, rs2, d) for d in range(1, cols)]
    for c in sent:
        c.start()
    recv2[me_c] = send2[me_c]
    for d in range(1, cols):
        col_arrival(send2, recv2, ss2, rs2, d).wait_recv()
    for c in sent:
        c.wait_send()
    ty = ty_ref[...]
    spectrum = exact_dot(ty, recv2[...].reshape(128, 128), ((1,), (0,)))
    shift = shift_ref[pl.ds(me_r * cols + me_c, 1), :]
    spectrum = spectrum / (ly_ref[...] + shift)
    send2[...] = exact_dot(ty, spectrum, ((0,), (0,))).reshape(cols, 8, 128)
    sent = [col_copy(send2, recv3, ss3, rs3, d) for d in range(1, cols)]
    for c in sent:
        c.start()
    recv3[me_c] = send2[me_c]
    for d in range(1, cols):
        col_arrival(send2, recv3, ss3, rs3, d).wait_recv()
    for c in sent:
        c.wait_send()
    for c in range(cols):
        tile = recv3[c]
        yb[pl.ds(2 * c, 8, stride=32), :] = jnp.where(lane < 64, tile, 0.0)
        yb[pl.ds(2 * c + 1, 8, stride=32), :] = jnp.where(lane < 64, 0.0, tile)
    txt = jnp.transpose(tx)
    send4[...] = exact_dot(jnp.concatenate([txt, txt], axis=1), yb[...], ((1,), (1,))).reshape(8, 8, 256)
    sent = [row_copy(send4, recv4, ss4, rs4, d) for d in range(1, rows)]
    for c in sent:
        c.start()
    recv4[me_r] = send4[me_r]
    for d in range(1, rows):
        row_arrival(send4, recv4, ss4, rs4, d).wait_recv()
    for c in sent:
        c.wait_send()
    for kh in range(2):
        for h in range(2):
            v = [recv4[kh * 4 + q, :, h * 128:(h + 1) * 128] for q in range(4)]
            for p in range(4):
                tile = jnp.zeros((8, 128), f32)
                for q in range(4):
                    s = (q - p) * 32 % 128
                    tile = jnp.where(part == q, pltpu.roll(v[q], s, 1) if s else v[q], tile)
                fp[kh, pl.ds(4 * h + p, 8, stride=8), :] = tile
    out_ref[...] = exact_dot(jnp.concatenate([fp[0], fp[1]], axis=1), tz_ref[...], ((1,), (0,)))


def solve(heat, divergence):
    lx, ly, lz = mode_values(64), mode_values(128), mode_values(256)
    device = np.arange(128)
    lanes = np.arange(128)
    shift = screen + lx[lanes % 64][None, :] + lz[(device // 16 * 32 + device % 16 * 2)[:, None] + (lanes // 64)[None, :]]
    vm = pl.BlockSpec(memory_space=pltpu.VMEM)
    hb = pl.BlockSpec(memory_space=pl.ANY)
    dma = pltpu.SemaphoreType.DMA
    out = pl.pallas_call(
        solve_kernel,
        out_shape=jax.ShapeDtypeStruct((64, 256), f32),
        in_specs=[hb] * 7,
        out_specs=vm,
        scratch_shapes=[
            pltpu.VMEM((2, 64, 128), f32), pltpu.VMEM((64, 256), f32), pltpu.VMEM((256, 256), f32), pltpu.VMEM((64, 64), f32), pltpu.VMEM((128, 128), f32),
            pltpu.VMEM((128, 128), f32), pltpu.VMEM((128, 128), f32), dma((7,)),
            pltpu.VMEM((2, 64, 128), f32), pltpu.VMEM((8, 8, 256), f32), pltpu.VMEM((8, 8, 256), f32), pltpu.VMEM((256, 128), f32),
            pltpu.VMEM((16, 8, 128), f32), pltpu.VMEM((16, 8, 128), f32), pltpu.VMEM((16, 8, 128), f32), pltpu.VMEM((256, 128), f32),
            pltpu.VMEM((8, 8, 256), f32), pltpu.VMEM((8, 8, 256), f32), pltpu.VMEM((2, 64, 128), f32),
            dma((8,)), dma((8,)), dma((16,)), dma((16,)), dma((16,)), dma((16,)), dma((8,)), dma((8,))],
        compiler_params=pltpu.CompilerParams(collective_id=1, has_side_effects=True, vmem_limit_bytes=60 << 20),
        name="screened_solve",
    )(heat, divergence.reshape(64, 256), jnp.asarray(cosine_table(256)), jnp.asarray(cosine_table(64)), jnp.asarray(cosine_table(128)),
      jnp.asarray(shift.astype(np.float32)), jnp.asarray(np.broadcast_to(ly[:, None], (128, 128)).astype(np.float32)))
    return out.reshape(8, 8, 256)


def local(species, velocity, diffusivity, divergence, log_rates, reactants, products, heat_weights, substeps):
    moved, first, second, order = advance(species, velocity, diffusivity, log_rates, reactants, products, substeps)
    reacted, heat = kinetics(16, moved, order, heat_weights, first, second)
    pressure = solve(heat, divergence)
    return reacted.reshape(species.shape), pressure


def solution(mesh):
    cells = P("row", "col", None)
    fields = P(None, "row", "col", None)
    in_specs = (fields, fields, P(), cells, P(), P(), P(), P(), cells)
    return jax.shard_map(local, mesh=mesh, in_specs=in_specs, out_specs=(fields, cells), check_vma=False)
```

```python
import functools

import jax
import jax.numpy as jnp
import numpy as np
from jax import lax
from jax.experimental import pallas as pl
from jax.experimental.pallas import tpu as pltpu
from jax.sharding import PartitionSpec as P

f32, bf16 = jnp.float32, jnp.bfloat16
MESH = pl.DeviceIdType.MESH
NS, SP = 53, 56
NR, RP = 325, 336
LOG2E = 1.4426950408889634
time_step = 0.2
screen = 0.004
highest = lax.Precision.HIGHEST
FAR_ROW = (6, 2, 5, 3, 4, 7, 1)
FAR_COL = (12, 10, 14, 8, 11, 13, 9, 15, 4, 6, 2, 5, 3, 7, 1)

def split3(x):
    hi = x.astype(bf16).astype(f32)
    mid = (x - hi).astype(bf16).astype(f32)
    return hi, mid, x - hi - mid


def build_matrices(log_rates, react_ref, prod_ref, react, prod, halves, first_ref, second_ref):
    react[...] = jnp.zeros_like(react)
    prod[...] = jnp.zeros_like(prod)
    react[:NS, :NR] = react_ref[...].astype(f32)
    prod[:NS, :NR] = prod_ref[...].astype(f32)
    rt, pt = react[...], prod[...]
    rp = jnp.transpose(rt)[:RP]
    own = lax.broadcasted_iota(jnp.int32, (RP, NR), 0) == lax.broadcasted_iota(jnp.int32, (RP, NR), 1)
    hi, mid, low = split3(jnp.sum(jnp.where(own, log_rates[...].reshape(1, NR), 0.0), axis=1, keepdims=True) * LOG2E)
    lane = lax.broadcasted_iota(jnp.int32, (RP, 128), 1)
    later = pltpu.roll(rp, SP, 1)
    both = jnp.where(lane == NS, hi, jnp.where(lane == NS + 1, mid, jnp.where(lane == NS + 2, low, rp + later)))
    first_ref[...] = both[:, :2 * SP].astype(bf16)
    outcome = jnp.concatenate([pt[:SP], rt[:SP]], axis=0)
    halves[:, :384] = outcome
    halves[:, RP:RP + 384] = outcome
    second_ref[...] = halves[:, :2 * RP].astype(bf16)


def build_order(counts, order_ref):
    row = lax.broadcasted_iota(jnp.int32, (128, 128), 0)
    lane = lax.broadcasted_iota(jnp.int32, (128, 128), 1)
    given = jnp.concatenate([counts[:, z, :] for z in range(2)], axis=0).astype(f32)
    tall = jnp.dot((lax.broadcasted_iota(jnp.int32, (128, 16), 0) // 8 == lax.broadcasted_iota(jnp.int32, (128, 16), 1)).astype(f32), given, preferred_element_type=f32)
    mine = lax.broadcasted_iota(jnp.int32, (128, 8), 0) % 8 == lax.broadcasted_iota(jnp.int32, (128, 8), 1)
    column = jnp.sum(jnp.where(mine, tall, 0.0), axis=1, keepdims=True)
    n = jnp.sum(jnp.where(row == lane, column, 0.0), axis=0, keepdims=True)
    ahead = jnp.where(n > column, 1.0, jnp.where(n == column, jnp.where(lane < row, 1.0, 0.0), 0.0))
    rank = jnp.sum(ahead, axis=1, keepdims=True).astype(jnp.int32)
    here = rank == lane
    order_ref[0:1, :] = jnp.sum(jnp.where(here, row.astype(f32), 0.0), axis=0, keepdims=True).astype(jnp.int32)
    order_ref[1:2, :] = jnp.sum(jnp.where(here, jnp.broadcast_to(column, (128, 128)), 0.0), axis=0, keepdims=True).astype(jnp.int32)


def advance_kernel(species, vel_hbm, diff_hbm, rates_hbm, react_hbm, prod_hbm, counts_hbm, mov_ref, first_ref, second_ref, order_ref,
                   hx, ext, mv, vel_ref, diff_ref, rates_ref, react_ref, prod_ref, counts_ref, react, prod, halves, sem_in, ss, rs, sem_out):
    rows, cols = lax.axis_size("row"), lax.axis_size("col")
    me_r, me_c = lax.axis_index("row"), lax.axis_index("col")
    above = {"row": lax.rem(me_r + 1, rows), "col": me_c}
    below = {"row": lax.rem(me_r + rows - 1, rows), "col": me_c}
    right = {"row": me_r, "col": lax.rem(me_c + 1, cols)}
    left = {"row": me_r, "col": lax.rem(me_c + cols - 1, cols)}
    barrier = pltpu.get_barrier_semaphore()
    for peer in (above, below, right, left):
        pl.semaphore_signal(barrier, inc=1, device_id=peer, device_id_type=MESH)
    def column(x, y, z, sem):
        zs = pl.ds(z * 128, 128)
        return pltpu.make_async_copy(species.at[:, x * 8 + y, zs], ext.at[x + 1, y + 1, z, pl.ds(0, NS)], sem)

    def arrived(count, sem):
        whole = mv.at[pl.ds(0, count), pl.ds(0, NS)]
        pltpu.make_async_copy(whole, whole, sem).wait()

    def edge_columns(x, _):
        for y in (0, 7):
            for z in range(2):
                column(x, y, z, sem_in.at[0]).start()
        return 0
    lax.fori_loop(0, 8, edge_columns, 0)
    extra = [pltpu.make_async_copy(a, b, sem_in.at[9 + k]) for k, (a, b) in enumerate(((vel_hbm, vel_ref), (diff_hbm, diff_ref), (rates_hbm, rates_ref), (react_hbm, react_ref), (prod_hbm, prod_ref), (counts_hbm, counts_ref)))]
    for c in extra:
        c.start()
    pl.semaphore_wait(barrier, 4)
    x_copies = []
    for z in range(2):
        zs = pl.ds(z * 128, 128)
        x_copies.append(pltpu.make_async_remote_copy(src_ref=species.at[:, pl.ds(56, 8), zs], dst_ref=hx.at[0, z], send_sem=ss.at[2 + z], recv_sem=rs.at[2 + z], device_id=above, device_id_type=MESH))
        x_copies.append(pltpu.make_async_remote_copy(src_ref=species.at[:, pl.ds(0, 8), zs], dst_ref=hx.at[1, z], send_sem=ss.at[4 + z], recv_sem=rs.at[4 + z], device_id=below, device_id_type=MESH))
    for c in x_copies:
        c.start()
    def inner_columns(x, _):
        for y in range(1, 7):
            for z in range(2):
                column(x, y, z, sem_in.at[1 + x]).start()
        return 0
    lax.fori_loop(0, 8, inner_columns, 0)
    arrived(32, sem_in.at[0])
    y_up = pltpu.make_async_remote_copy(src_ref=ext.at[pl.ds(1, 8), 8], dst_ref=ext.at[pl.ds(1, 8), 0], send_sem=ss.at[0], recv_sem=rs.at[0], device_id=right, device_id_type=MESH)
    y_down = pltpu.make_async_remote_copy(src_ref=ext.at[pl.ds(1, 8), 1], dst_ref=ext.at[pl.ds(1, 8), 9], send_sem=ss.at[1], recv_sem=rs.at[1], device_id=left, device_id_type=MESH)
    y_up.start()
    y_down.start()

    for c in extra:
        c.wait()
    own = lax.broadcasted_iota(jnp.int32, (SP, NS), 0) == lax.broadcasted_iota(jnp.int32, (SP, NS), 1)
    fifth = jnp.broadcast_to(0.2 * jnp.sum(jnp.where(own, diff_ref[...], 0.0), axis=1, keepdims=True), (SP, 256))
    lane = lax.broadcasted_iota(jnp.int32, (SP, 256), 1)
    row = lax.broadcasted_iota(jnp.int32, (SP, 256), 0)

    def move(x, y, halves=slice(0, 256)):
        c = x * 8 + y
        low, high = halves.start // 128, halves.stop // 128

        def cells(at, to):
            return jnp.concatenate([ext[at, to, z] for z in range(low, high)], axis=1)
        whole = jnp.concatenate([ext[x + 1, y + 1, 0], ext[x + 1, y + 1, 1]], axis=1)
        centre = whole[:, halves]
        diffused, lanes, rows_here = fifth[:, halves], lane[:, halves], row[:, halves]
        near = (cells(x, y + 1), cells(x + 2, y + 1), cells(x + 1, y), cells(x + 1, y + 2),
                jnp.where(lanes == 0, centre, pltpu.roll(whole, 1, 1)[:, halves]), jnp.where(lanes == 255, centre, pltpu.roll(whole, 255, 1)[:, halves]))
        speeds = [0.2 * vel_ref[d, pl.ds(c, 1), :][:, halves] for d in range(3)]
        still = 1.0 - (jnp.abs(speeds[0]) + jnp.abs(speeds[1]) + jnp.abs(speeds[2]))
        total = centre * (still - 6.0 * diffused)
        for d in range(3):
            total = total + near[2 * d] * (diffused + jnp.maximum(speeds[d], 0.0))
            total = total + near[2 * d + 1] * (diffused - jnp.minimum(speeds[d], 0.0))
        total = jnp.where(rows_here < NS, total, 2.0)
        for z in range(low, high):
            mv[64 * z + c] = total[:, (z - low) * 128:(z - low + 1) * 128]

    arrived(12, sem_in.at[1])
    arrived(12, sem_in.at[2])

    def inner(x, _):
        arrived(12, sem_in.at[2 + x])

        def go(y, _):
            move(x, y)
            return 0
        return lax.fori_loop(1, 7, go, 0)
    lax.fori_loop(1, 7, inner, 0)
    build_matrices(rates_ref, react_ref, prod_ref, react, prod, halves, first_ref, second_ref)
    build_order(counts_ref, order_ref)
    y_up.wait()
    y_down.wait()

    @pl.when(me_c == 0)
    def _():
        ext[pl.ds(1, 8), 0] = ext[pl.ds(1, 8), 1]

    @pl.when(me_c == cols - 1)
    def _():
        ext[pl.ds(1, 8), 9] = ext[pl.ds(1, 8), 8]

    def sides(x, _):
        move(x, 0)
        move(x, 7)
        return 0
    lax.fori_loop(1, 7, sides, 0)
    middle = [pltpu.make_async_copy(mv.at[pl.ds(64 * z + 8, 48)], mov_ref.at[pl.ds(64 * z + 8, 48)], sem_out.at[z]) for z in range(2)]
    for c in middle:
        c.start()
    outer = []
    for z in range(2):
        for c in x_copies[2 * z:2 * z + 2]:
            c.wait()

        def lay_halo(y, _):
            for k, at in ((0, 0), (1, 9)):
                ext[at, y + 1, z, :NS, :] = hx.at[k, z].reshape(NS * 8, 128)[pl.ds(y, NS, stride=8), :]
            return 0
        lax.fori_loop(0, 8, lay_halo, 0)

        @pl.when(me_r == 0)
        def _():
            ext[0, pl.ds(1, 8), z] = ext[1, pl.ds(1, 8), z]

        @pl.when(me_r == rows - 1)
        def _():
            ext[9, pl.ds(1, 8), z] = ext[8, pl.ds(1, 8), z]

        def ends(y, _):
            move(0, y, slice(z * 128, (z + 1) * 128))
            move(7, y, slice(z * 128, (z + 1) * 128))
            return 0
        lax.fori_loop(0, 8, ends, 0)
        for k, at in ((0, 64 * z), (1, 64 * z + 56)):
            outer.append(pltpu.make_async_copy(mv.at[pl.ds(at, 8)], mov_ref.at[pl.ds(at, 8)], sem_out.at[2 + 2 * z + k]))
            outer[-1].start()
    for c in middle + outer:
        c.wait()


def advance(species, velocity, diffusivity, log_rates, reactants, products, substeps):
    vm = pl.BlockSpec(memory_space=pltpu.VMEM)
    hb = pl.BlockSpec(memory_space=pl.ANY)
    dma = pltpu.SemaphoreType.DMA
    shape = jax.ShapeDtypeStruct
    return pl.pallas_call(
        advance_kernel,
        out_shape=(shape((128, SP, 128), f32), shape((RP, 2 * SP), bf16), shape((2 * SP, 2 * RP), bf16), shape((2, 128), jnp.int32)),
        in_specs=[hb] * 7,
        out_specs=(hb, vm, vm, vm),
        scratch_shapes=[pltpu.VMEM((2, 2, NS, 8, 128), f32), pltpu.VMEM((10, 10, 2, SP, 128), f32), pltpu.VMEM((128, SP, 128), f32),
                        pltpu.VMEM((3, 64, 256), f32), pltpu.VMEM((1, NS), f32), pltpu.VMEM((NR,), f32), pltpu.VMEM((NS, NR), jnp.int32), pltpu.VMEM((NS, NR), jnp.int32),
                        pltpu.VMEM((8, 2, 8), jnp.int32), pltpu.VMEM((128, 384), f32), pltpu.VMEM((128, 384), f32), pltpu.VMEM((2 * SP, RP + 384), f32), dma((15,)), dma((6,)), dma((6,)), dma((6,))],
        compiler_params=pltpu.CompilerParams(collective_id=0, has_side_effects=True, vmem_limit_bytes=60 << 20),
        name="advance",
    )(species.reshape(NS, 64, 256), velocity.reshape(3, 64, 256), diffusivity[None, :], log_rates, reactants.T, products.T, jnp.transpose(substeps, (0, 2, 1)))


def kinetics_kernel(G, order_ref, size_ref, mov_hbm, weight_hbm, s1_hbm, s2_hbm, out_ref, heat_ref, mov, cur, stage, depart, weight_ref, s1_ref, s2_ref, sem, arrive):
    turns = 128 // G

    def fetch(t, slot):
        return [pltpu.make_async_copy(mov_hbm.at[order_ref[0, t * G + j]], mov.at[slot, j], arrive.at[slot]) for j in range(G)]
    def leave(t, slot):
        made = []
        for j in range(G):
            i = order_ref[0, t * G + j]
            made.append(pltpu.make_async_copy(stage.at[slot, j, pl.ds(0, NS)], out_ref.at[:, i % 64, pl.ds(pl.multiple_of(i // 64 * 128, 128), 128)], depart.at[slot]))
        return made

    def left(slot):
        whole = stage.at[slot, :, pl.ds(0, NS)]
        pltpu.make_async_copy(whole, whole, depart.at[slot]).wait()

    for c in fetch(0, 0):
        c.start()
    constants = [pltpu.make_async_copy(a, b, sem.at[k]) for k, (a, b) in enumerate(((weight_hbm, weight_ref), (s1_hbm, s1_ref), (s2_hbm, s2_ref)))]
    for c in constants:
        c.start()
    for c in constants:
        c.wait()
    own = lax.broadcasted_iota(jnp.int32, (SP, NS), 0) == lax.broadcasted_iota(jnp.int32, (SP, NS), 1)
    weight = jnp.broadcast_to(jnp.sum(jnp.where(own, weight_ref[...], 0.0), axis=1, keepdims=True) / time_step, (SP, 128))
    W = G * 128

    def turn(t, _):
        slot = t % 2

        @pl.when(t + 1 < turns)
        def _():
            for c in fetch(t + 1, 1 - slot):
                c.start()
        ids = [order_ref[0, t * G + j] for j in range(G)]
        ns = [order_ref[1, t * G + j] for j in range(G)]
        pltpu.make_async_copy(mov.at[slot], mov.at[slot], arrive.at[slot]).wait()
        for j in range(G):
            cur[:, j * 128:(j + 1) * 128] = mov[slot, j]
        h = jnp.concatenate([jnp.full((SP, 128), size_ref[n], f32) for n in ns], axis=1)
        nb = jnp.concatenate([jnp.full((SP, 128), n, jnp.int32) for n in ns], axis=1)

        def level(k, _):
            conc = cur[...]
            lg = jnp.log2(conc)
            hi = lg.astype(bf16).astype(f32)
            xin = jnp.concatenate([hi, lg - hi], axis=0).astype(bf16)
            rates = jnp.exp2(jnp.dot(s1_ref[...], xin, preferred_element_type=f32))
            rhi = rates.astype(bf16)
            rlo = (rates - rhi.astype(f32)).astype(bf16)
            both = jnp.dot(s2_ref[...], jnp.concatenate([rhi, rlo], axis=0), preferred_element_type=f32)
            fresh = conc * (conc + h * both[:SP]) / (conc + h * both[SP:])
            cur[...] = jnp.where(nb > k, fresh, conc)
            return 0
        lax.fori_loop(0, ns[0], level, 0)
        @pl.when(t >= 2)
        def _():
            left(slot)
        for j in range(G):
            stage[slot, j] = cur[:, j * 128:(j + 1) * 128]
        for c in leave(t, slot):
            c.start()
        for j in range(G):
            term = weight * (cur[:, j * 128:(j + 1) * 128] - mov[slot, j])
            heat_ref[ids[j] // 64, pl.ds(ids[j] % 64, 1), :] = jnp.sum(term, axis=0, keepdims=True)
        return 0
    lax.fori_loop(0, turns, turn, 0)
    left(0)
    left(1)


def kinetics(G, moved, order, heat_weights, first, second):
    vm = pl.BlockSpec(memory_space=pltpu.VMEM)
    sm = pl.BlockSpec(memory_space=pltpu.SMEM)
    hb = pl.BlockSpec(memory_space=pl.ANY)
    sizes = np.array([0.0] + [time_step / n for n in range(1, 8)], np.float32)
    return pl.pallas_call(
        functools.partial(kinetics_kernel, G),
        out_shape=(jax.ShapeDtypeStruct((NS, 64, 256), f32), jax.ShapeDtypeStruct((2, 64, 128), f32)),
        in_specs=[sm, sm, hb, hb, hb, hb],
        out_specs=(hb, vm),
        scratch_shapes=[
            pltpu.VMEM((2, G, SP, 128), f32), pltpu.VMEM((SP, G * 128), f32), pltpu.VMEM((2, G, SP, 128), f32), pltpu.SemaphoreType.DMA((2,)), pltpu.VMEM((1, NS), f32),
            pltpu.VMEM((RP, 2 * SP), bf16), pltpu.VMEM((2 * SP, 2 * RP), bf16), pltpu.SemaphoreType.DMA((3,)), pltpu.SemaphoreType.DMA((2,))],
        compiler_params=pltpu.CompilerParams(vmem_limit_bytes=60 << 20),
        name="kinetics",
    )(order, jnp.asarray(sizes), moved, heat_weights[None, :], first, second)


def cosine_table(length):
    wave = np.arange(length)[:, None]
    sample = np.arange(length)[None, :] + 0.5
    weight = np.sqrt(np.where(wave == 0, 1.0, 2.0) / length)
    return (weight * np.cos(np.pi * wave * sample / length)).astype(np.float32)


def mode_values(length):
    return 2.0 - 2.0 * np.cos(np.pi * np.arange(length) / length)


def exact_dot(a, b, dims):
    return lax.dot_general(a, b, (dims, ((), ())), precision=highest, preferred_element_type=f32)


def solve_kernel(heat_hbm, div_hbm, tz_hbm, tx_hbm, ty_hbm, shift_hbm, ly_hbm, out_ref,
                 heat_ref, div_ref, tz_ref, tx_ref, ty_ref, shift_ref, ly_ref, sem_in,
                 f1, send1, recv1, yv, send2, recv2, recv3, yb, send4, recv4, fp,
                 ss1, rs1, ss2, rs2, ss3, rs3, ss4, rs4):
    rows, cols = 8, 16
    me_r, me_c = lax.axis_index("row"), lax.axis_index("col")
    pairs = ((heat_hbm, heat_ref), (div_hbm, div_ref), (tz_hbm, tz_ref), (tx_hbm, tx_ref), (ty_hbm, ty_ref), (shift_hbm, shift_ref), (ly_hbm, ly_ref))
    loads = [pltpu.make_async_copy(a, b, sem_in.at[k]) for k, (a, b) in enumerate(pairs)]
    for c in loads:
        c.start()
    barrier = pltpu.get_barrier_semaphore()
    for d in range(1, rows):
        pl.semaphore_signal(barrier, inc=1, device_id={"row": lax.rem(me_r + d, rows), "col": me_c}, device_id_type=pl.DeviceIdType.MESH)
    for d in range(1, cols):
        pl.semaphore_signal(barrier, inc=1, device_id={"row": me_r, "col": lax.rem(me_c + d, cols)}, device_id_type=pl.DeviceIdType.MESH)

    def row_copy(send, recv, ss, rs, d):
        to = lax.rem(me_r + d, rows)
        return pltpu.make_async_remote_copy(src_ref=send.at[to], dst_ref=recv.at[me_r], send_sem=ss.at[d], recv_sem=rs.at[me_r],
                                            device_id={"row": to, "col": me_c}, device_id_type=pl.DeviceIdType.MESH)

    def col_copy(send, recv, ss, rs, d):
        to = lax.rem(me_c + d, cols)
        return pltpu.make_async_remote_copy(src_ref=send.at[to], dst_ref=recv.at[me_c], send_sem=ss.at[d], recv_sem=rs.at[me_c],
                                            device_id={"row": me_r, "col": to}, device_id_type=pl.DeviceIdType.MESH)

    def row_arrival(send, recv, ss, rs, d):
        come = lax.rem(me_r + d, rows)
        return pltpu.make_async_remote_copy(src_ref=send.at[come], dst_ref=recv.at[come], send_sem=ss.at[d], recv_sem=rs.at[come],
                                            device_id={"row": come, "col": me_c}, device_id_type=pl.DeviceIdType.MESH)

    def col_arrival(send, recv, ss, rs, d):
        come = lax.rem(me_c + d, cols)
        return pltpu.make_async_remote_copy(src_ref=send.at[come], dst_ref=recv.at[come], send_sem=ss.at[d], recv_sem=rs.at[come],
                                            device_id={"row": me_r, "col": come}, device_id_type=pl.DeviceIdType.MESH)

    lane = lax.broadcasted_iota(jnp.int32, (8, 128), 1)
    part = lane // 32
    for c in loads:
        c.wait()
    source = div_ref[...] - jnp.concatenate([heat_ref[0], heat_ref[1]], axis=1)
    forward = exact_dot(source, tz_ref[...], ((1,), (1,)))
    f1[0] = forward[:, :128]
    f1[1] = forward[:, 128:]
    for kh in range(2):
        for h in range(2):
            v = [f1[kh, pl.ds(4 * h + p, 8, stride=8), :] for p in range(4)]
            for q in range(4):
                tile = jnp.zeros((8, 128), f32)
                for p in range(4):
                    s = (p - q) * 32 % 128
                    tile = jnp.where(part == p, pltpu.roll(v[p], s, 1) if s else v[p], tile)
                send1[kh * 4 + q, :, h * 128:(h + 1) * 128] = tile
    pl.semaphore_wait(barrier, rows - 1 + cols - 1)
    sent = [row_copy(send1, recv1, ss1, rs1, d) for d in FAR_ROW]
    for c in sent:
        c.start()
    recv1[me_r] = send1[me_r]
    for d in range(1, rows):
        row_arrival(send1, recv1, ss1, rs1, d).wait_recv()
    for c in sent:
        c.wait_send()
    block = recv1[...].reshape(64, 256)
    tx = tx_ref[...]
    yv[...] = exact_dot(jnp.transpose(block), jnp.concatenate([tx, tx], axis=0), ((1,), (1,)))
    for c in range(cols):
        send2[c] = jnp.where(lane < 64, yv[pl.ds(2 * c, 8, stride=32), :], yv[pl.ds(2 * c + 1, 8, stride=32), :])
    sent = [col_copy(send2, recv2, ss2, rs2, d) for d in FAR_COL]
    for c in sent:
        c.start()
    recv2[me_c] = send2[me_c]
    for d in range(1, cols):
        col_arrival(send2, recv2, ss2, rs2, d).wait_recv()
    for c in sent:
        c.wait_send()
    ty = ty_ref[...]
    spectrum = exact_dot(ty, recv2[...].reshape(128, 128), ((1,), (0,)))
    shift = shift_ref[pl.ds(me_r * cols + me_c, 1), :]
    spectrum = spectrum / (ly_ref[...] + shift)
    send2[...] = exact_dot(ty, spectrum, ((0,), (0,))).reshape(cols, 8, 128)
    sent = [col_copy(send2, recv3, ss3, rs3, d) for d in FAR_COL]
    for c in sent:
        c.start()
    recv3[me_c] = send2[me_c]
    for d in range(1, cols):
        col_arrival(send2, recv3, ss3, rs3, d).wait_recv()
    for c in sent:
        c.wait_send()
    for c in range(cols):
        tile = recv3[c]
        yb[pl.ds(2 * c, 8, stride=32), :] = jnp.where(lane < 64, tile, 0.0)
        yb[pl.ds(2 * c + 1, 8, stride=32), :] = jnp.where(lane < 64, 0.0, tile)
    txt = jnp.transpose(tx)
    send4[...] = exact_dot(jnp.concatenate([txt, txt], axis=1), yb[...], ((1,), (1,))).reshape(8, 8, 256)
    sent = [row_copy(send4, recv4, ss4, rs4, d) for d in FAR_ROW]
    for c in sent:
        c.start()
    recv4[me_r] = send4[me_r]
    for d in range(1, rows):
        row_arrival(send4, recv4, ss4, rs4, d).wait_recv()
    for c in sent:
        c.wait_send()
    for kh in range(2):
        for h in range(2):
            v = [recv4[kh * 4 + q, :, h * 128:(h + 1) * 128] for q in range(4)]
            for p in range(4):
                tile = jnp.zeros((8, 128), f32)
                for q in range(4):
                    s = (q - p) * 32 % 128
                    tile = jnp.where(part == q, pltpu.roll(v[q], s, 1) if s else v[q], tile)
                fp[kh, pl.ds(4 * h + p, 8, stride=8), :] = tile
    out_ref[...] = exact_dot(jnp.concatenate([fp[0], fp[1]], axis=1), tz_ref[...], ((1,), (0,)))


def solve(heat, divergence):
    lx, ly, lz = mode_values(64), mode_values(128), mode_values(256)
    device = np.arange(128)
    lanes = np.arange(128)
    shift = screen + lx[lanes % 64][None, :] + lz[(device // 16 * 32 + device % 16 * 2)[:, None] + (lanes // 64)[None, :]]
    vm = pl.BlockSpec(memory_space=pltpu.VMEM)
    hb = pl.BlockSpec(memory_space=pl.ANY)
    dma = pltpu.SemaphoreType.DMA
    out = pl.pallas_call(
        solve_kernel,
        out_shape=jax.ShapeDtypeStruct((64, 256), f32),
        in_specs=[hb] * 7,
        out_specs=vm,
        scratch_shapes=[
            pltpu.VMEM((2, 64, 128), f32), pltpu.VMEM((64, 256), f32), pltpu.VMEM((256, 256), f32), pltpu.VMEM((64, 64), f32), pltpu.VMEM((128, 128), f32),
            pltpu.VMEM((128, 128), f32), pltpu.VMEM((128, 128), f32), dma((7,)),
            pltpu.VMEM((2, 64, 128), f32), pltpu.VMEM((8, 8, 256), f32), pltpu.VMEM((8, 8, 256), f32), pltpu.VMEM((256, 128), f32),
            pltpu.VMEM((16, 8, 128), f32), pltpu.VMEM((16, 8, 128), f32), pltpu.VMEM((16, 8, 128), f32), pltpu.VMEM((256, 128), f32),
            pltpu.VMEM((8, 8, 256), f32), pltpu.VMEM((8, 8, 256), f32), pltpu.VMEM((2, 64, 128), f32),
            dma((8,)), dma((8,)), dma((16,)), dma((16,)), dma((16,)), dma((16,)), dma((8,)), dma((8,))],
        compiler_params=pltpu.CompilerParams(collective_id=1, has_side_effects=True, vmem_limit_bytes=60 << 20),
        name="screened_solve",
    )(heat, divergence.reshape(64, 256), jnp.asarray(cosine_table(256)), jnp.asarray(cosine_table(64)), jnp.asarray(cosine_table(128)),
      jnp.asarray(shift.astype(np.float32)), jnp.asarray(np.broadcast_to(ly[:, None], (128, 128)).astype(np.float32)))
    return out.reshape(8, 8, 256)


def local(species, velocity, diffusivity, divergence, log_rates, reactants, products, heat_weights, substeps):
    moved, first, second, order = advance(species, velocity, diffusivity, log_rates, reactants, products, substeps)
    reacted, heat = kinetics(16, moved, order, heat_weights, first, second)
    pressure = solve(heat, divergence)
    return reacted.reshape(species.shape), pressure


def solution(mesh):
    cells = P("row", "col", None)
    fields = P(None, "row", "col", None)
    in_specs = (fields, fields, P(), cells, P(), P(), P(), P(), cells)
    return jax.shard_map(local, mesh=mesh, in_specs=in_specs, out_specs=(fields, cells), check_vma=False)
```

```python
import functools

import jax
import jax.numpy as jnp
import numpy as np
from jax import lax
from jax.experimental import pallas as pl
from jax.experimental.pallas import tpu as pltpu
from jax.sharding import PartitionSpec as P

f32, bf16 = jnp.float32, jnp.bfloat16
MESH = pl.DeviceIdType.MESH
NS, SP = 53, 56
NR, RP = 325, 336
LOG2E = 1.4426950408889634
time_step = 0.2
screen = 0.004
highest = lax.Precision.HIGHEST
FAR_ROW = (6, 2, 5, 3, 4, 7, 1)
FAR_COL = (12, 10, 14, 8, 11, 13, 9, 15, 4, 6, 2, 5, 3, 7, 1)

def split3(x):
    hi = x.astype(bf16).astype(f32)
    mid = (x - hi).astype(bf16).astype(f32)
    return hi, mid, x - hi - mid


def build_matrices(log_rates, react_ref, prod_ref, react, prod, halves, first_ref, second_ref):
    react[...] = jnp.zeros_like(react)
    prod[...] = jnp.zeros_like(prod)
    react[:NS, :NR] = react_ref[...].astype(f32)
    prod[:NS, :NR] = prod_ref[...].astype(f32)
    rt, pt = react[...], prod[...]
    rp = jnp.transpose(rt)[:RP]
    own = lax.broadcasted_iota(jnp.int32, (RP, NR), 0) == lax.broadcasted_iota(jnp.int32, (RP, NR), 1)
    hi, mid, low = split3(jnp.sum(jnp.where(own, log_rates[...].reshape(1, NR), 0.0), axis=1, keepdims=True) * LOG2E)
    lane = lax.broadcasted_iota(jnp.int32, (RP, 128), 1)
    later = pltpu.roll(rp, SP, 1)
    both = jnp.where(lane == NS, hi, jnp.where(lane == NS + 1, mid, jnp.where(lane == NS + 2, low, rp + later)))
    first_ref[...] = both[:, :2 * SP].astype(bf16)
    outcome = jnp.concatenate([pt[:SP], rt[:SP]], axis=0)
    halves[:, :384] = outcome
    halves[:, RP:RP + 384] = outcome
    second_ref[...] = halves[:, :2 * RP].astype(bf16)


def build_order(counts, order_ref):
    row = lax.broadcasted_iota(jnp.int32, (128, 128), 0)
    lane = lax.broadcasted_iota(jnp.int32, (128, 128), 1)
    given = jnp.concatenate([counts[:, z, :] for z in range(2)], axis=0).astype(f32)
    tall = jnp.dot((lax.broadcasted_iota(jnp.int32, (128, 16), 0) // 8 == lax.broadcasted_iota(jnp.int32, (128, 16), 1)).astype(f32), given, preferred_element_type=f32)
    mine = lax.broadcasted_iota(jnp.int32, (128, 8), 0) % 8 == lax.broadcasted_iota(jnp.int32, (128, 8), 1)
    column = jnp.sum(jnp.where(mine, tall, 0.0), axis=1, keepdims=True)
    n = jnp.sum(jnp.where(row == lane, column, 0.0), axis=0, keepdims=True)
    ahead = jnp.where(n > column, 1.0, jnp.where(n == column, jnp.where(lane < row, 1.0, 0.0), 0.0))
    rank = jnp.sum(ahead, axis=1, keepdims=True).astype(jnp.int32)
    here = rank == lane
    order_ref[0:1, :] = jnp.sum(jnp.where(here, row.astype(f32), 0.0), axis=0, keepdims=True).astype(jnp.int32)
    order_ref[1:2, :] = jnp.sum(jnp.where(here, jnp.broadcast_to(column, (128, 128)), 0.0), axis=0, keepdims=True).astype(jnp.int32)


def advance_kernel(species, vel_hbm, diff_hbm, rates_hbm, react_hbm, prod_hbm, counts_hbm, mov_ref, first_ref, second_ref, order_ref,
                   hx, ext, mv, vel_ref, diff_ref, rates_ref, react_ref, prod_ref, counts_ref, react, prod, halves, sem_in, ss, rs, sem_out):
    rows, cols = lax.axis_size("row"), lax.axis_size("col")
    me_r, me_c = lax.axis_index("row"), lax.axis_index("col")
    above = {"row": lax.rem(me_r + 1, rows), "col": me_c}
    below = {"row": lax.rem(me_r + rows - 1, rows), "col": me_c}
    right = {"row": me_r, "col": lax.rem(me_c + 1, cols)}
    left = {"row": me_r, "col": lax.rem(me_c + cols - 1, cols)}
    barrier = pltpu.get_barrier_semaphore()
    for peer in (above, below, right, left):
        pl.semaphore_signal(barrier, inc=1, device_id=peer, device_id_type=MESH)
    def column(x, y, z, sem):
        zs = pl.ds(z * 128, 128)
        return pltpu.make_async_copy(species.at[:, x * 8 + y, zs], ext.at[x + 1, y + 1, z, pl.ds(0, NS)], sem)

    def arrived(count, sem):
        whole = mv.at[pl.ds(0, count), pl.ds(0, NS)]
        pltpu.make_async_copy(whole, whole, sem).wait()

    def edge_columns(x, _):
        for y in (0, 7):
            for z in range(2):
                column(x, y, z, sem_in.at[0]).start()
        return 0
    lax.fori_loop(0, 8, edge_columns, 0)
    extra = [pltpu.make_async_copy(a, b, sem_in.at[9 + k]) for k, (a, b) in enumerate(((vel_hbm, vel_ref), (diff_hbm, diff_ref), (rates_hbm, rates_ref), (react_hbm, react_ref), (prod_hbm, prod_ref), (counts_hbm, counts_ref)))]
    for c in extra:
        c.start()
    pl.semaphore_wait(barrier, 4)
    x_copies = []
    for z in range(2):
        zs = pl.ds(z * 128, 128)
        x_copies.append(pltpu.make_async_remote_copy(src_ref=species.at[:, pl.ds(56, 8), zs], dst_ref=hx.at[0, z], send_sem=ss.at[2 + z], recv_sem=rs.at[2 + z], device_id=above, device_id_type=MESH))
        x_copies.append(pltpu.make_async_remote_copy(src_ref=species.at[:, pl.ds(0, 8), zs], dst_ref=hx.at[1, z], send_sem=ss.at[4 + z], recv_sem=rs.at[4 + z], device_id=below, device_id_type=MESH))
    for c in x_copies:
        c.start()
    def inner_columns(x, _):
        for y in range(1, 7):
            for z in range(2):
                column(x, y, z, sem_in.at[1 + x]).start()
        return 0
    lax.fori_loop(0, 8, inner_columns, 0)
    arrived(32, sem_in.at[0])
    y_up = pltpu.make_async_remote_copy(src_ref=ext.at[pl.ds(1, 8), 8], dst_ref=ext.at[pl.ds(1, 8), 0], send_sem=ss.at[0], recv_sem=rs.at[0], device_id=right, device_id_type=MESH)
    y_down = pltpu.make_async_remote_copy(src_ref=ext.at[pl.ds(1, 8), 1], dst_ref=ext.at[pl.ds(1, 8), 9], send_sem=ss.at[1], recv_sem=rs.at[1], device_id=left, device_id_type=MESH)
    y_up.start()
    y_down.start()

    for c in extra:
        c.wait()
    own = lax.broadcasted_iota(jnp.int32, (SP, NS), 0) == lax.broadcasted_iota(jnp.int32, (SP, NS), 1)
    fifth = jnp.broadcast_to(0.2 * jnp.sum(jnp.where(own, diff_ref[...], 0.0), axis=1, keepdims=True), (SP, 256))
    lane = lax.broadcasted_iota(jnp.int32, (SP, 256), 1)
    row = lax.broadcasted_iota(jnp.int32, (SP, 256), 0)

    def move(x, y, halves=slice(0, 256)):
        c = x * 8 + y
        low, high = halves.start // 128, halves.stop // 128

        def cells(at, to):
            return jnp.concatenate([ext[at, to, z] for z in range(low, high)], axis=1)
        whole = jnp.concatenate([ext[x + 1, y + 1, 0], ext[x + 1, y + 1, 1]], axis=1)
        centre = whole[:, halves]
        diffused, lanes, rows_here = fifth[:, halves], lane[:, halves], row[:, halves]
        near = (cells(x, y + 1), cells(x + 2, y + 1), cells(x + 1, y), cells(x + 1, y + 2),
                jnp.where(lanes == 0, centre, pltpu.roll(whole, 1, 1)[:, halves]), jnp.where(lanes == 255, centre, pltpu.roll(whole, 255, 1)[:, halves]))
        speeds = [0.2 * vel_ref[d, pl.ds(c, 1), :][:, halves] for d in range(3)]
        still = 1.0 - (jnp.abs(speeds[0]) + jnp.abs(speeds[1]) + jnp.abs(speeds[2]))
        total = centre * (still - 6.0 * diffused)
        for d in range(3):
            total = total + near[2 * d] * (diffused + jnp.maximum(speeds[d], 0.0))
            total = total + near[2 * d + 1] * (diffused - jnp.minimum(speeds[d], 0.0))
        total = jnp.where(rows_here < NS, total, 2.0)
        for z in range(low, high):
            mv[64 * z + c] = total[:, (z - low) * 128:(z - low + 1) * 128]

    arrived(12, sem_in.at[1])
    arrived(12, sem_in.at[2])

    def inner(x, _):
        arrived(12, sem_in.at[2 + x])

        def go(y, _):
            move(x, y)
            return 0
        return lax.fori_loop(1, 7, go, 0)
    lax.fori_loop(1, 7, inner, 0)
    build_matrices(rates_ref, react_ref, prod_ref, react, prod, halves, first_ref, second_ref)
    build_order(counts_ref, order_ref)
    y_up.wait()
    y_down.wait()

    @pl.when(me_c == 0)
    def _():
        ext[pl.ds(1, 8), 0] = ext[pl.ds(1, 8), 1]

    @pl.when(me_c == cols - 1)
    def _():
        ext[pl.ds(1, 8), 9] = ext[pl.ds(1, 8), 8]

    def sides(x, _):
        move(x, 0)
        move(x, 7)
        return 0
    lax.fori_loop(1, 7, sides, 0)
    middle = [pltpu.make_async_copy(mv.at[pl.ds(64 * z + 8, 48)], mov_ref.at[pl.ds(64 * z + 8, 48)], sem_out.at[z]) for z in range(2)]
    for c in middle:
        c.start()
    outer = []
    for z in range(2):
        for c in x_copies[2 * z:2 * z + 2]:
            c.wait()

        def lay_halo(y, _):
            for k, at in ((0, 0), (1, 9)):
                ext[at, y + 1, z, :NS, :] = hx.at[k, z].reshape(NS * 8, 128)[pl.ds(y, NS, stride=8), :]
            return 0
        lax.fori_loop(0, 8, lay_halo, 0)

        @pl.when(me_r == 0)
        def _():
            ext[0, pl.ds(1, 8), z] = ext[1, pl.ds(1, 8), z]

        @pl.when(me_r == rows - 1)
        def _():
            ext[9, pl.ds(1, 8), z] = ext[8, pl.ds(1, 8), z]

        def ends(y, _):
            move(0, y, slice(z * 128, (z + 1) * 128))
            move(7, y, slice(z * 128, (z + 1) * 128))
            return 0
        lax.fori_loop(0, 8, ends, 0)
        for k, at in ((0, 64 * z), (1, 64 * z + 56)):
            outer.append(pltpu.make_async_copy(mv.at[pl.ds(at, 8)], mov_ref.at[pl.ds(at, 8)], sem_out.at[2 + 2 * z + k]))
            outer[-1].start()
    for c in middle + outer:
        c.wait()


def advance(species, velocity, diffusivity, log_rates, reactants, products, substeps):
    vm = pl.BlockSpec(memory_space=pltpu.VMEM)
    hb = pl.BlockSpec(memory_space=pl.ANY)
    dma = pltpu.SemaphoreType.DMA
    shape = jax.ShapeDtypeStruct
    return pl.pallas_call(
        advance_kernel,
        out_shape=(shape((128, SP, 128), f32), shape((RP, 2 * SP), bf16), shape((2 * SP, 2 * RP), bf16), shape((2, 128), jnp.int32)),
        in_specs=[hb] * 7,
        out_specs=(hb, vm, vm, vm),
        scratch_shapes=[pltpu.VMEM((2, 2, NS, 8, 128), f32), pltpu.VMEM((10, 10, 2, SP, 128), f32), pltpu.VMEM((128, SP, 128), f32),
                        pltpu.VMEM((3, 64, 256), f32), pltpu.VMEM((1, NS), f32), pltpu.VMEM((NR,), f32), pltpu.VMEM((NS, NR), jnp.int32), pltpu.VMEM((NS, NR), jnp.int32),
                        pltpu.VMEM((8, 2, 8), jnp.int32), pltpu.VMEM((128, 384), f32), pltpu.VMEM((128, 384), f32), pltpu.VMEM((2 * SP, RP + 384), f32), dma((15,)), dma((6,)), dma((6,)), dma((6,))],
        compiler_params=pltpu.CompilerParams(collective_id=0, has_side_effects=True, vmem_limit_bytes=60 << 20),
        name="advance",
    )(species.reshape(NS, 64, 256), velocity.reshape(3, 64, 256), diffusivity[None, :], log_rates, reactants.T, products.T, jnp.transpose(substeps, (0, 2, 1)))


def kinetics_kernel(G, order_ref, size_ref, mov_hbm, weight_hbm, s1_hbm, s2_hbm, out_ref, heat_ref, mov, cur, stage, depart, weight_ref, s1_ref, s2_ref, sem, arrive):
    turns = 128 // G

    def fetch(t, slot):
        return [pltpu.make_async_copy(mov_hbm.at[order_ref[0, t * G + j]], mov.at[slot, j], arrive.at[slot]) for j in range(G)]
    def leave(t, slot):
        made = []
        for j in range(G):
            i = order_ref[0, t * G + j]
            made.append(pltpu.make_async_copy(stage.at[slot, j, pl.ds(0, NS)], out_ref.at[:, i % 64, pl.ds(pl.multiple_of(i // 64 * 128, 128), 128)], depart.at[slot]))
        return made

    def left(slot):
        whole = stage.at[slot, :, pl.ds(0, NS)]
        pltpu.make_async_copy(whole, whole, depart.at[slot]).wait()

    for c in fetch(0, 0):
        c.start()
    constants = [pltpu.make_async_copy(a, b, sem.at[k]) for k, (a, b) in enumerate(((weight_hbm, weight_ref), (s1_hbm, s1_ref), (s2_hbm, s2_ref)))]
    for c in constants:
        c.start()
    for c in constants:
        c.wait()
    own = lax.broadcasted_iota(jnp.int32, (SP, NS), 0) == lax.broadcasted_iota(jnp.int32, (SP, NS), 1)
    weight = jnp.broadcast_to(jnp.sum(jnp.where(own, weight_ref[...], 0.0), axis=1, keepdims=True) / time_step, (SP, 128))
    W = G * 128

    def turn(t, _):
        slot = t % 2

        @pl.when(t + 1 < turns)
        def _():
            for c in fetch(t + 1, 1 - slot):
                c.start()
        ids = [order_ref[0, t * G + j] for j in range(G)]
        ns = [order_ref[1, t * G + j] for j in range(G)]
        pltpu.make_async_copy(mov.at[slot], mov.at[slot], arrive.at[slot]).wait()
        for j in range(G):
            cur[:, j * 128:(j + 1) * 128] = mov[slot, j]
        h = jnp.concatenate([jnp.full((SP, 128), size_ref[n], f32) for n in ns], axis=1)
        nb = jnp.concatenate([jnp.full((SP, 128), n, jnp.int32) for n in ns], axis=1)

        def level(k, _):
            conc = cur[...]
            lg = jnp.log2(conc)
            hi = lg.astype(bf16).astype(f32)
            xin = jnp.concatenate([hi, lg - hi], axis=0).astype(bf16)
            rates = jnp.exp2(jnp.dot(s1_ref[...], xin, preferred_element_type=f32))
            rhi = rates.astype(bf16)
            rlo = (rates - rhi.astype(f32)).astype(bf16)
            both = jnp.dot(s2_ref[...], jnp.concatenate([rhi, rlo], axis=0), preferred_element_type=f32)
            fresh = conc * (conc + h * both[:SP]) / (conc + h * both[SP:])
            cur[...] = jnp.where(nb > k, fresh, conc)
            return 0
        lax.fori_loop(0, ns[0], level, 0)
        @pl.when(t >= 2)
        def _():
            left(slot)
        for j in range(G):
            stage[slot, j] = cur[:, j * 128:(j + 1) * 128]
        for c in leave(t, slot):
            c.start()
        for j in range(G):
            term = weight * (cur[:, j * 128:(j + 1) * 128] - mov[slot, j])
            heat_ref[ids[j] // 64, pl.ds(ids[j] % 64, 1), :] = jnp.sum(term, axis=0, keepdims=True)
        return 0
    lax.fori_loop(0, turns, turn, 0)
    left(0)
    left(1)


def kinetics(G, moved, order, heat_weights, first, second):
    vm = pl.BlockSpec(memory_space=pltpu.VMEM)
    sm = pl.BlockSpec(memory_space=pltpu.SMEM)
    hb = pl.BlockSpec(memory_space=pl.ANY)
    sizes = np.array([0.0] + [time_step / n for n in range(1, 8)], np.float32)
    return pl.pallas_call(
        functools.partial(kinetics_kernel, G),
        out_shape=(jax.ShapeDtypeStruct((NS, 64, 256), f32), jax.ShapeDtypeStruct((2, 64, 128), f32)),
        in_specs=[sm, sm, hb, hb, hb, hb],
        out_specs=(hb, vm),
        scratch_shapes=[
            pltpu.VMEM((2, G, SP, 128), f32), pltpu.VMEM((SP, G * 128), f32), pltpu.VMEM((2, G, SP, 128), f32), pltpu.SemaphoreType.DMA((2,)), pltpu.VMEM((1, NS), f32),
            pltpu.VMEM((RP, 2 * SP), bf16), pltpu.VMEM((2 * SP, 2 * RP), bf16), pltpu.SemaphoreType.DMA((3,)), pltpu.SemaphoreType.DMA((2,))],
        compiler_params=pltpu.CompilerParams(vmem_limit_bytes=60 << 20),
        name="kinetics",
    )(order, jnp.asarray(sizes), moved, heat_weights[None, :], first, second)


def cosine_table(length):
    wave = np.arange(length)[:, None]
    sample = np.arange(length)[None, :] + 0.5
    weight = np.sqrt(np.where(wave == 0, 1.0, 2.0) / length)
    return (weight * np.cos(np.pi * wave * sample / length)).astype(np.float32)


def mode_values(length):
    return 2.0 - 2.0 * np.cos(np.pi * np.arange(length) / length)


def exact_dot(a, b, dims):
    return lax.dot_general(a, b, (dims, ((), ())), precision=highest, preferred_element_type=f32)


def solve_kernel(heat_hbm, div_hbm, tz_hbm, tx_hbm, ty_hbm, shift_hbm, ly_hbm, out_ref,
                 heat_ref, div_ref, tz_ref, tx_ref, ty_ref, shift_ref, ly_ref, sem_in,
                 f1, send1, recv1, yv, send2, recv2, send3, recv3, yb, send4, recv4, fp,
                 ss, rs):
    rows, cols = 8, 16
    me_r, me_c = lax.axis_index("row"), lax.axis_index("col")
    pairs = ((heat_hbm, heat_ref), (div_hbm, div_ref), (tz_hbm, tz_ref), (tx_hbm, tx_ref), (ty_hbm, ty_ref), (shift_hbm, shift_ref), (ly_hbm, ly_ref))
    loads = [pltpu.make_async_copy(a, b, sem_in.at[k]) for k, (a, b) in enumerate(pairs)]
    for c in loads:
        c.start()
    barrier = pltpu.get_barrier_semaphore()
    for d in range(1, rows):
        pl.semaphore_signal(barrier, inc=1, device_id={"row": lax.rem(me_r + d, rows), "col": me_c}, device_id_type=pl.DeviceIdType.MESH)
    for d in range(1, cols):
        pl.semaphore_signal(barrier, inc=1, device_id={"row": me_r, "col": lax.rem(me_c + d, cols)}, device_id_type=pl.DeviceIdType.MESH)

    def row_copy(send, recv, k, d):
        to = lax.rem(me_r + d, rows)
        return pltpu.make_async_remote_copy(src_ref=send.at[to], dst_ref=recv.at[me_r], send_sem=ss.at[k], recv_sem=rs.at[k],
                                            device_id={"row": to, "col": me_c}, device_id_type=pl.DeviceIdType.MESH)

    def col_copy(send, recv, k, d):
        to = lax.rem(me_c + d, cols)
        return pltpu.make_async_remote_copy(src_ref=send.at[to], dst_ref=recv.at[me_c], send_sem=ss.at[k], recv_sem=rs.at[k],
                                            device_id={"row": me_r, "col": to}, device_id_type=pl.DeviceIdType.MESH)

    def others(buffer, sem):
        most = buffer.at[pl.ds(0, buffer.shape[0] - 1)]
        pltpu.make_async_copy(most, most, sem).wait()

    lane = lax.broadcasted_iota(jnp.int32, (8, 128), 1)
    part = lane // 32
    for c in loads:
        c.wait()
    source = div_ref[...] - jnp.concatenate([heat_ref[0], heat_ref[1]], axis=1)
    forward = exact_dot(source, tz_ref[...], ((1,), (1,)))
    f1[0] = forward[:, :128]
    f1[1] = forward[:, 128:]
    for kh in range(2):
        for h in range(2):
            v = [f1[kh, pl.ds(4 * h + p, 8, stride=8), :] for p in range(4)]
            for q in range(4):
                tile = jnp.zeros((8, 128), f32)
                for p in range(4):
                    s = (p - q) * 32 % 128
                    tile = jnp.where(part == p, pltpu.roll(v[p], s, 1) if s else v[p], tile)
                send1[kh * 4 + q, :, h * 128:(h + 1) * 128] = tile
    pl.semaphore_wait(barrier, rows - 1 + cols - 1)
    for d in FAR_ROW:
        row_copy(send1, recv1, 0, d).start()
    recv1[me_r] = send1[me_r]
    others(recv1, rs.at[0])
    block = recv1[...].reshape(64, 256)
    tx = tx_ref[...]
    yv[...] = exact_dot(jnp.transpose(block), jnp.concatenate([tx, tx], axis=0), ((1,), (1,)))
    for c in range(cols):
        send2[c] = jnp.where(lane < 64, yv[pl.ds(2 * c, 8, stride=32), :], yv[pl.ds(2 * c + 1, 8, stride=32), :])
    for d in FAR_COL:
        col_copy(send2, recv2, 1, d).start()
    recv2[me_c] = send2[me_c]
    others(recv2, rs.at[1])
    ty = ty_ref[...]
    spectrum = exact_dot(ty, recv2[...].reshape(128, 128), ((1,), (0,)))
    shift = shift_ref[pl.ds(me_r * cols + me_c, 1), :]
    spectrum = spectrum / (ly_ref[...] + shift)
    send3[...] = exact_dot(ty, spectrum, ((0,), (0,))).reshape(cols, 8, 128)
    for d in FAR_COL:
        col_copy(send3, recv3, 2, d).start()
    recv3[me_c] = send3[me_c]
    others(recv3, rs.at[2])
    for c in range(cols):
        tile = recv3[c]
        yb[pl.ds(2 * c, 8, stride=32), :] = jnp.where(lane < 64, tile, 0.0)
        yb[pl.ds(2 * c + 1, 8, stride=32), :] = jnp.where(lane < 64, 0.0, tile)
    txt = jnp.transpose(tx)
    send4[...] = exact_dot(jnp.concatenate([txt, txt], axis=1), yb[...], ((1,), (1,))).reshape(8, 8, 256)
    for d in FAR_ROW:
        row_copy(send4, recv4, 3, d).start()
    recv4[me_r] = send4[me_r]
    others(recv4, rs.at[3])
    for kh in range(2):
        for h in range(2):
            v = [recv4[kh * 4 + q, :, h * 128:(h + 1) * 128] for q in range(4)]
            for p in range(4):
                tile = jnp.zeros((8, 128), f32)
                for q in range(4):
                    s = (q - p) * 32 % 128
                    tile = jnp.where(part == q, pltpu.roll(v[q], s, 1) if s else v[q], tile)
                fp[kh, pl.ds(4 * h + p, 8, stride=8), :] = tile
    out_ref[...] = exact_dot(jnp.concatenate([fp[0], fp[1]], axis=1), tz_ref[...], ((1,), (0,)))
    for k, buffer in enumerate((send1, send2, send3, send4)):
        others(buffer, ss.at[k])


def solve(heat, divergence):
    lx, ly, lz = mode_values(64), mode_values(128), mode_values(256)
    device = np.arange(128)
    lanes = np.arange(128)
    shift = screen + lx[lanes % 64][None, :] + lz[(device // 16 * 32 + device % 16 * 2)[:, None] + (lanes // 64)[None, :]]
    vm = pl.BlockSpec(memory_space=pltpu.VMEM)
    hb = pl.BlockSpec(memory_space=pl.ANY)
    dma = pltpu.SemaphoreType.DMA
    out = pl.pallas_call(
        solve_kernel,
        out_shape=jax.ShapeDtypeStruct((64, 256), f32),
        in_specs=[hb] * 7,
        out_specs=vm,
        scratch_shapes=[
            pltpu.VMEM((2, 64, 128), f32), pltpu.VMEM((64, 256), f32), pltpu.VMEM((256, 256), f32), pltpu.VMEM((64, 64), f32), pltpu.VMEM((128, 128), f32),
            pltpu.VMEM((128, 128), f32), pltpu.VMEM((128, 128), f32), dma((7,)),
            pltpu.VMEM((2, 64, 128), f32), pltpu.VMEM((8, 8, 256), f32), pltpu.VMEM((8, 8, 256), f32), pltpu.VMEM((256, 128), f32),
            pltpu.VMEM((16, 8, 128), f32), pltpu.VMEM((16, 8, 128), f32), pltpu.VMEM((16, 8, 128), f32), pltpu.VMEM((16, 8, 128), f32), pltpu.VMEM((256, 128), f32),
            pltpu.VMEM((8, 8, 256), f32), pltpu.VMEM((8, 8, 256), f32), pltpu.VMEM((2, 64, 128), f32),
            dma((4,)), dma((4,))],
        compiler_params=pltpu.CompilerParams(collective_id=1, has_side_effects=True, vmem_limit_bytes=60 << 20),
        name="screened_solve",
    )(heat, divergence.reshape(64, 256), jnp.asarray(cosine_table(256)), jnp.asarray(cosine_table(64)), jnp.asarray(cosine_table(128)),
      jnp.asarray(shift.astype(np.float32)), jnp.asarray(np.broadcast_to(ly[:, None], (128, 128)).astype(np.float32)))
    return out.reshape(8, 8, 256)


def local(species, velocity, diffusivity, divergence, log_rates, reactants, products, heat_weights, substeps):
    moved, first, second, order = advance(species, velocity, diffusivity, log_rates, reactants, products, substeps)
    reacted, heat = kinetics(16, moved, order, heat_weights, first, second)
    pressure = solve(heat, divergence)
    return reacted.reshape(species.shape), pressure


def solution(mesh):
    cells = P("row", "col", None)
    fields = P(None, "row", "col", None)
    in_specs = (fields, fields, P(), cells, P(), P(), P(), P(), cells)
    return jax.shard_map(local, mesh=mesh, in_specs=in_specs, out_specs=(fields, cells), check_vma=False)
```

```python
import functools

import jax
import jax.numpy as jnp
import numpy as np
from jax import lax
from jax.experimental import pallas as pl
from jax.experimental.pallas import tpu as pltpu
from jax.sharding import PartitionSpec as P

f32, bf16 = jnp.float32, jnp.bfloat16
MESH = pl.DeviceIdType.MESH
NS, SP = 53, 56
NR, RP = 325, 336
LOG2E = 1.4426950408889634
time_step = 0.2
screen = 0.004
highest = lax.Precision.HIGHEST
FAR_ROW = (6, 2, 5, 3, 4, 7, 1)
FAR_COL = (12, 10, 14, 8, 11, 13, 9, 15, 4, 6, 2, 5, 3, 7, 1)

def split3(x):
    hi = x.astype(bf16).astype(f32)
    mid = (x - hi).astype(bf16).astype(f32)
    return hi, mid, x - hi - mid


def build_matrices(log_rates, react_ref, prod_ref, react, prod, halves, first_ref, second_ref):
    react[...] = jnp.zeros_like(react)
    prod[...] = jnp.zeros_like(prod)
    react[:NS, :NR] = react_ref[...].astype(f32)
    prod[:NS, :NR] = prod_ref[...].astype(f32)
    rt, pt = react[...], prod[...]
    rp = jnp.transpose(rt)[:RP]
    own = lax.broadcasted_iota(jnp.int32, (RP, NR), 0) == lax.broadcasted_iota(jnp.int32, (RP, NR), 1)
    hi, mid, low = split3(jnp.sum(jnp.where(own, log_rates[...].reshape(1, NR), 0.0), axis=1, keepdims=True) * LOG2E)
    lane = lax.broadcasted_iota(jnp.int32, (RP, 128), 1)
    later = pltpu.roll(rp, SP, 1)
    both = jnp.where(lane == NS, hi, jnp.where(lane == NS + 1, mid, jnp.where(lane == NS + 2, low, rp + later)))
    first_ref[...] = both[:, :2 * SP].astype(bf16)
    outcome = jnp.concatenate([pt[:SP], rt[:SP]], axis=0)
    halves[:, :384] = outcome
    halves[:, RP:RP + 384] = outcome
    second_ref[...] = halves[:, :2 * RP].astype(bf16)


def build_order(counts, order_ref):
    row = lax.broadcasted_iota(jnp.int32, (128, 128), 0)
    lane = lax.broadcasted_iota(jnp.int32, (128, 128), 1)
    given = jnp.concatenate([counts[:, z, :] for z in range(2)], axis=0).astype(f32)
    tall = jnp.dot((lax.broadcasted_iota(jnp.int32, (128, 16), 0) // 8 == lax.broadcasted_iota(jnp.int32, (128, 16), 1)).astype(f32), given, preferred_element_type=f32)
    mine = lax.broadcasted_iota(jnp.int32, (128, 8), 0) % 8 == lax.broadcasted_iota(jnp.int32, (128, 8), 1)
    column = jnp.sum(jnp.where(mine, tall, 0.0), axis=1, keepdims=True)
    n = jnp.sum(jnp.where(row == lane, column, 0.0), axis=0, keepdims=True)
    ahead = jnp.where(n > column, 1.0, jnp.where(n == column, jnp.where(lane < row, 1.0, 0.0), 0.0))
    rank = jnp.sum(ahead, axis=1, keepdims=True).astype(jnp.int32)
    here = rank == lane
    order_ref[0:1, :] = jnp.sum(jnp.where(here, row.astype(f32), 0.0), axis=0, keepdims=True).astype(jnp.int32)
    order_ref[1:2, :] = jnp.sum(jnp.where(here, jnp.broadcast_to(column, (128, 128)), 0.0), axis=0, keepdims=True).astype(jnp.int32)


def advance_kernel(species, vel_hbm, diff_hbm, rates_hbm, react_hbm, prod_hbm, counts_hbm, mov_ref, first_ref, second_ref, order_ref,
                   hx, ext, mv, vel_ref, diff_ref, rates_ref, react_ref, prod_ref, counts_ref, react, prod, halves, sem_in, ss, rs, sem_out):
    rows, cols = lax.axis_size("row"), lax.axis_size("col")
    me_r, me_c = lax.axis_index("row"), lax.axis_index("col")
    above = {"row": lax.rem(me_r + 1, rows), "col": me_c}
    below = {"row": lax.rem(me_r + rows - 1, rows), "col": me_c}
    right = {"row": me_r, "col": lax.rem(me_c + 1, cols)}
    left = {"row": me_r, "col": lax.rem(me_c + cols - 1, cols)}
    barrier = pltpu.get_barrier_semaphore()
    for peer in (above, below, right, left):
        pl.semaphore_signal(barrier, inc=1, device_id=peer, device_id_type=MESH)
    def column(x, y, z, sem):
        zs = pl.ds(z * 128, 128)
        return pltpu.make_async_copy(species.at[:, x * 8 + y, zs], ext.at[x + 1, y + 1, z, pl.ds(0, NS)], sem)

    def arrived(count, sem):
        whole = mv.at[pl.ds(0, count), pl.ds(0, NS)]
        pltpu.make_async_copy(whole, whole, sem).wait()

    def edge_columns(x, _):
        for y in (0, 7):
            for z in range(2):
                column(x, y, z, sem_in.at[0]).start()
        return 0
    pl.semaphore_wait(barrier, 4)
    x_copies = []
    for z in range(2):
        zs = pl.ds(z * 128, 128)
        x_copies.append(pltpu.make_async_remote_copy(src_ref=species.at[:, pl.ds(56, 8), zs], dst_ref=hx.at[0, z], send_sem=ss.at[2 + z], recv_sem=rs.at[2 + z], device_id=above, device_id_type=MESH))
        x_copies.append(pltpu.make_async_remote_copy(src_ref=species.at[:, pl.ds(0, 8), zs], dst_ref=hx.at[1, z], send_sem=ss.at[4 + z], recv_sem=rs.at[4 + z], device_id=below, device_id_type=MESH))
    for c in x_copies:
        c.start()
    lax.fori_loop(0, 8, edge_columns, 0)
    extra = [pltpu.make_async_copy(a, b, sem_in.at[9 + k]) for k, (a, b) in enumerate(((vel_hbm, vel_ref), (diff_hbm, diff_ref), (rates_hbm, rates_ref), (react_hbm, react_ref), (prod_hbm, prod_ref), (counts_hbm, counts_ref)))]
    for c in extra:
        c.start()
    def inner_columns(x, _):
        for y in range(1, 7):
            for z in range(2):
                column(x, y, z, sem_in.at[1 + x]).start()
        return 0
    lax.fori_loop(0, 8, inner_columns, 0)
    arrived(32, sem_in.at[0])
    y_up = pltpu.make_async_remote_copy(src_ref=ext.at[pl.ds(1, 8), 8], dst_ref=ext.at[pl.ds(1, 8), 0], send_sem=ss.at[0], recv_sem=rs.at[0], device_id=right, device_id_type=MESH)
    y_down = pltpu.make_async_remote_copy(src_ref=ext.at[pl.ds(1, 8), 1], dst_ref=ext.at[pl.ds(1, 8), 9], send_sem=ss.at[1], recv_sem=rs.at[1], device_id=left, device_id_type=MESH)
    y_up.start()
    y_down.start()

    for c in extra:
        c.wait()
    own = lax.broadcasted_iota(jnp.int32, (SP, NS), 0) == lax.broadcasted_iota(jnp.int32, (SP, NS), 1)
    fifth = jnp.broadcast_to(0.2 * jnp.sum(jnp.where(own, diff_ref[...], 0.0), axis=1, keepdims=True), (SP, 256))
    lane = lax.broadcasted_iota(jnp.int32, (SP, 256), 1)
    row = lax.broadcasted_iota(jnp.int32, (SP, 256), 0)

    def move(x, y, halves=slice(0, 256)):
        c = x * 8 + y
        low, high = halves.start // 128, halves.stop // 128

        def cells(at, to):
            return jnp.concatenate([ext[at, to, z] for z in range(low, high)], axis=1)
        whole = jnp.concatenate([ext[x + 1, y + 1, 0], ext[x + 1, y + 1, 1]], axis=1)
        centre = whole[:, halves]
        diffused, lanes, rows_here = fifth[:, halves], lane[:, halves], row[:, halves]
        near = (cells(x, y + 1), cells(x + 2, y + 1), cells(x + 1, y), cells(x + 1, y + 2),
                jnp.where(lanes == 0, centre, pltpu.roll(whole, 1, 1)[:, halves]), jnp.where(lanes == 255, centre, pltpu.roll(whole, 255, 1)[:, halves]))
        speeds = [0.2 * vel_ref[d, pl.ds(c, 1), :][:, halves] for d in range(3)]
        still = 1.0 - (jnp.abs(speeds[0]) + jnp.abs(speeds[1]) + jnp.abs(speeds[2]))
        total = centre * (still - 6.0 * diffused)
        for d in range(3):
            total = total + near[2 * d] * (diffused + jnp.maximum(speeds[d], 0.0))
            total = total + near[2 * d + 1] * (diffused - jnp.minimum(speeds[d], 0.0))
        total = jnp.where(rows_here < NS, total, 2.0)
        for z in range(low, high):
            mv[64 * z + c] = total[:, (z - low) * 128:(z - low + 1) * 128]

    arrived(12, sem_in.at[1])
    arrived(12, sem_in.at[2])

    def inner(x, _):
        arrived(12, sem_in.at[2 + x])

        def go(y, _):
            move(x, y)
            return 0
        return lax.fori_loop(1, 7, go, 0)
    lax.fori_loop(1, 7, inner, 0)
    build_matrices(rates_ref, react_ref, prod_ref, react, prod, halves, first_ref, second_ref)
    build_order(counts_ref, order_ref)
    y_up.wait()
    y_down.wait()

    @pl.when(me_c == 0)
    def _():
        ext[pl.ds(1, 8), 0] = ext[pl.ds(1, 8), 1]

    @pl.when(me_c == cols - 1)
    def _():
        ext[pl.ds(1, 8), 9] = ext[pl.ds(1, 8), 8]

    def sides(x, _):
        move(x, 0)
        move(x, 7)
        return 0
    lax.fori_loop(1, 7, sides, 0)
    middle = [pltpu.make_async_copy(mv.at[pl.ds(64 * z + 8, 48)], mov_ref.at[pl.ds(64 * z + 8, 48)], sem_out.at[z]) for z in range(2)]
    for c in middle:
        c.start()
    outer = []
    for z in range(2):
        for c in x_copies[2 * z:2 * z + 2]:
            c.wait()

        def lay_halo(y, _):
            for k, at in ((0, 0), (1, 9)):
                ext[at, y + 1, z, :NS, :] = hx.at[k, z].reshape(NS * 8, 128)[pl.ds(y, NS, stride=8), :]
            return 0
        lax.fori_loop(0, 8, lay_halo, 0)

        @pl.when(me_r == 0)
        def _():
            ext[0, pl.ds(1, 8), z] = ext[1, pl.ds(1, 8), z]

        @pl.when(me_r == rows - 1)
        def _():
            ext[9, pl.ds(1, 8), z] = ext[8, pl.ds(1, 8), z]

        def ends(y, _):
            move(0, y, slice(z * 128, (z + 1) * 128))
            move(7, y, slice(z * 128, (z + 1) * 128))
            return 0
        lax.fori_loop(0, 8, ends, 0)
        for k, at in ((0, 64 * z), (1, 64 * z + 56)):
            outer.append(pltpu.make_async_copy(mv.at[pl.ds(at, 8)], mov_ref.at[pl.ds(at, 8)], sem_out.at[2 + 2 * z + k]))
            outer[-1].start()
    for c in middle + outer:
        c.wait()


def advance(species, velocity, diffusivity, log_rates, reactants, products, substeps):
    vm = pl.BlockSpec(memory_space=pltpu.VMEM)
    hb = pl.BlockSpec(memory_space=pl.ANY)
    dma = pltpu.SemaphoreType.DMA
    shape = jax.ShapeDtypeStruct
    return pl.pallas_call(
        advance_kernel,
        out_shape=(shape((128, SP, 128), f32), shape((RP, 2 * SP), bf16), shape((2 * SP, 2 * RP), bf16), shape((2, 128), jnp.int32)),
        in_specs=[hb] * 7,
        out_specs=(hb, vm, vm, vm),
        scratch_shapes=[pltpu.VMEM((2, 2, NS, 8, 128), f32), pltpu.VMEM((10, 10, 2, SP, 128), f32), pltpu.VMEM((128, SP, 128), f32),
                        pltpu.VMEM((3, 64, 256), f32), pltpu.VMEM((1, NS), f32), pltpu.VMEM((NR,), f32), pltpu.VMEM((NS, NR), jnp.int32), pltpu.VMEM((NS, NR), jnp.int32),
                        pltpu.VMEM((8, 2, 8), jnp.int32), pltpu.VMEM((128, 384), f32), pltpu.VMEM((128, 384), f32), pltpu.VMEM((2 * SP, RP + 384), f32), dma((15,)), dma((6,)), dma((6,)), dma((6,))],
        compiler_params=pltpu.CompilerParams(collective_id=0, has_side_effects=True, vmem_limit_bytes=60 << 20),
        name="advance",
    )(species.reshape(NS, 64, 256), velocity.reshape(3, 64, 256), diffusivity[None, :], log_rates, reactants.T, products.T, jnp.transpose(substeps, (0, 2, 1)))


def kinetics_kernel(G, order_ref, size_ref, mov_hbm, weight_hbm, s1_hbm, s2_hbm, out_ref, heat_ref, mov, cur, stage, depart, weight_ref, s1_ref, s2_ref, sem, arrive):
    turns = 128 // G

    def fetch(t, slot):
        return [pltpu.make_async_copy(mov_hbm.at[order_ref[0, t * G + j]], mov.at[slot, j], arrive.at[slot]) for j in range(G)]
    def leave(t, slot):
        made = []
        for j in range(G):
            i = order_ref[0, t * G + j]
            made.append(pltpu.make_async_copy(stage.at[slot, j, pl.ds(0, NS)], out_ref.at[:, i % 64, pl.ds(pl.multiple_of(i // 64 * 128, 128), 128)], depart.at[slot]))
        return made

    def left(slot):
        whole = stage.at[slot, :, pl.ds(0, NS)]
        pltpu.make_async_copy(whole, whole, depart.at[slot]).wait()

    for c in fetch(0, 0):
        c.start()
    constants = [pltpu.make_async_copy(a, b, sem.at[k]) for k, (a, b) in enumerate(((weight_hbm, weight_ref), (s1_hbm, s1_ref), (s2_hbm, s2_ref)))]
    for c in constants:
        c.start()
    for c in constants:
        c.wait()
    own = lax.broadcasted_iota(jnp.int32, (SP, NS), 0) == lax.broadcasted_iota(jnp.int32, (SP, NS), 1)
    weight = jnp.broadcast_to(jnp.sum(jnp.where(own, weight_ref[...], 0.0), axis=1, keepdims=True) / time_step, (SP, 128))
    W = G * 128

    def turn(t, _):
        slot = t % 2

        @pl.when(t + 1 < turns)
        def _():
            for c in fetch(t + 1, 1 - slot):
                c.start()
        ids = [order_ref[0, t * G + j] for j in range(G)]
        ns = [order_ref[1, t * G + j] for j in range(G)]
        pltpu.make_async_copy(mov.at[slot], mov.at[slot], arrive.at[slot]).wait()
        for j in range(G):
            cur[:, j * 128:(j + 1) * 128] = mov[slot, j]
        h = jnp.concatenate([jnp.full((SP, 128), size_ref[n], f32) for n in ns], axis=1)
        nb = jnp.concatenate([jnp.full((SP, 128), n, jnp.int32) for n in ns], axis=1)

        def level(k, _):
            conc = cur[...]
            lg = jnp.log2(conc)
            hi = lg.astype(bf16).astype(f32)
            xin = jnp.concatenate([hi, lg - hi], axis=0).astype(bf16)
            rates = jnp.exp2(jnp.dot(s1_ref[...], xin, preferred_element_type=f32))
            rhi = rates.astype(bf16)
            rlo = (rates - rhi.astype(f32)).astype(bf16)
            both = jnp.dot(s2_ref[...], jnp.concatenate([rhi, rlo], axis=0), preferred_element_type=f32)
            fresh = conc * (conc + h * both[:SP]) / (conc + h * both[SP:])
            cur[...] = jnp.where(nb > k, fresh, conc)
            return 0
        lax.fori_loop(0, ns[0], level, 0)
        @pl.when(t >= 2)
        def _():
            left(slot)
        for j in range(G):
            stage[slot, j] = cur[:, j * 128:(j + 1) * 128]
        for c in leave(t, slot):
            c.start()
        for j in range(G):
            term = weight * (cur[:, j * 128:(j + 1) * 128] - mov[slot, j])
            heat_ref[ids[j] // 64, pl.ds(ids[j] % 64, 1), :] = jnp.sum(term, axis=0, keepdims=True)
        return 0
    lax.fori_loop(0, turns, turn, 0)
    left(0)
    left(1)


def kinetics(G, moved, order, heat_weights, first, second):
    vm = pl.BlockSpec(memory_space=pltpu.VMEM)
    sm = pl.BlockSpec(memory_space=pltpu.SMEM)
    hb = pl.BlockSpec(memory_space=pl.ANY)
    sizes = np.array([0.0] + [time_step / n for n in range(1, 8)], np.float32)
    return pl.pallas_call(
        functools.partial(kinetics_kernel, G),
        out_shape=(jax.ShapeDtypeStruct((NS, 64, 256), f32), jax.ShapeDtypeStruct((2, 64, 128), f32)),
        in_specs=[sm, sm, hb, hb, hb, hb],
        out_specs=(hb, vm),
        scratch_shapes=[
            pltpu.VMEM((2, G, SP, 128), f32), pltpu.VMEM((SP, G * 128), f32), pltpu.VMEM((2, G, SP, 128), f32), pltpu.SemaphoreType.DMA((2,)), pltpu.VMEM((1, NS), f32),
            pltpu.VMEM((RP, 2 * SP), bf16), pltpu.VMEM((2 * SP, 2 * RP), bf16), pltpu.SemaphoreType.DMA((3,)), pltpu.SemaphoreType.DMA((2,))],
        compiler_params=pltpu.CompilerParams(vmem_limit_bytes=60 << 20),
        name="kinetics",
    )(order, jnp.asarray(sizes), moved, heat_weights[None, :], first, second)


def cosine_table(length):
    wave = np.arange(length)[:, None]
    sample = np.arange(length)[None, :] + 0.5
    weight = np.sqrt(np.where(wave == 0, 1.0, 2.0) / length)
    return (weight * np.cos(np.pi * wave * sample / length)).astype(np.float32)


def mode_values(length):
    return 2.0 - 2.0 * np.cos(np.pi * np.arange(length) / length)


def exact_dot(a, b, dims):
    return lax.dot_general(a, b, (dims, ((), ())), precision=highest, preferred_element_type=f32)


def solve_kernel(heat_hbm, div_hbm, tz_hbm, tx_hbm, ty_hbm, shift_hbm, ly_hbm, out_ref,
                 heat_ref, div_ref, tz_ref, tx_ref, ty_ref, shift_ref, ly_ref, sem_in,
                 f1, send1, recv1, yv, send2, recv2, send3, recv3, yb, send4, recv4, fp,
                 ss, rs):
    rows, cols = 8, 16
    me_r, me_c = lax.axis_index("row"), lax.axis_index("col")
    barrier = pltpu.get_barrier_semaphore()
    for d in range(1, rows):
        pl.semaphore_signal(barrier, inc=1, device_id={"row": lax.rem(me_r + d, rows), "col": me_c}, device_id_type=pl.DeviceIdType.MESH)
    for d in range(1, cols):
        pl.semaphore_signal(barrier, inc=1, device_id={"row": me_r, "col": lax.rem(me_c + d, cols)}, device_id_type=pl.DeviceIdType.MESH)

    pairs = ((heat_hbm, heat_ref), (div_hbm, div_ref), (tz_hbm, tz_ref), (tx_hbm, tx_ref), (ty_hbm, ty_ref), (shift_hbm, shift_ref), (ly_hbm, ly_ref))
    loads = [pltpu.make_async_copy(a, b, sem_in.at[k]) for k, (a, b) in enumerate(pairs)]
    for c in loads:
        c.start()

    def row_copy(send, recv, k, d):
        to = lax.rem(me_r + d, rows)
        return pltpu.make_async_remote_copy(src_ref=send.at[to], dst_ref=recv.at[me_r], send_sem=ss.at[k], recv_sem=rs.at[k],
                                            device_id={"row": to, "col": me_c}, device_id_type=pl.DeviceIdType.MESH)

    def col_copy(send, recv, k, d):
        to = lax.rem(me_c + d, cols)
        return pltpu.make_async_remote_copy(src_ref=send.at[to], dst_ref=recv.at[me_c], send_sem=ss.at[k], recv_sem=rs.at[k],
                                            device_id={"row": me_r, "col": to}, device_id_type=pl.DeviceIdType.MESH)

    def others(buffer, sem):
        most = buffer.at[pl.ds(0, buffer.shape[0] - 1)]
        pltpu.make_async_copy(most, most, sem).wait()

    lane = lax.broadcasted_iota(jnp.int32, (8, 128), 1)
    part = lane // 32
    for c in loads[:3]:
        c.wait()
    source = div_ref[...] - jnp.concatenate([heat_ref[0], heat_ref[1]], axis=1)
    forward = exact_dot(source, tz_ref[...], ((1,), (1,)))
    f1[0] = forward[:, :128]
    f1[1] = forward[:, 128:]
    for kh in range(2):
        for h in range(2):
            v = [f1[kh, pl.ds(4 * h + p, 8, stride=8), :] for p in range(4)]
            for q in range(4):
                tile = jnp.zeros((8, 128), f32)
                for p in range(4):
                    s = (p - q) * 32 % 128
                    tile = jnp.where(part == p, pltpu.roll(v[p], s, 1) if s else v[p], tile)
                send1[kh * 4 + q, :, h * 128:(h + 1) * 128] = tile
    pl.semaphore_wait(barrier, rows - 1 + cols - 1)
    for d in FAR_ROW:
        row_copy(send1, recv1, 0, d).start()
    recv1[me_r] = send1[me_r]
    for c in loads[3:]:
        c.wait()
    tx = tx_ref[...]
    txt = jnp.transpose(tx)
    twice, twice_back = jnp.concatenate([tx, tx], axis=0), jnp.concatenate([txt, txt], axis=1)
    others(recv1, rs.at[0])
    block = recv1[...].reshape(64, 256)
    yv[...] = exact_dot(jnp.transpose(block), twice, ((1,), (1,)))
    for c in range(cols):
        send2[c] = jnp.where(lane < 64, yv[pl.ds(2 * c, 8, stride=32), :], yv[pl.ds(2 * c + 1, 8, stride=32), :])
    for d in FAR_COL:
        col_copy(send2, recv2, 1, d).start()
    recv2[me_c] = send2[me_c]
    others(recv2, rs.at[1])
    ty = ty_ref[...]
    spectrum = exact_dot(ty, recv2[...].reshape(128, 128), ((1,), (0,)))
    shift = shift_ref[pl.ds(me_r * cols + me_c, 1), :]
    spectrum = spectrum / (ly_ref[...] + shift)
    send3[...] = exact_dot(ty, spectrum, ((0,), (0,))).reshape(cols, 8, 128)
    for d in FAR_COL:
        col_copy(send3, recv3, 2, d).start()
    recv3[me_c] = send3[me_c]
    others(recv3, rs.at[2])
    for c in range(cols):
        tile = recv3[c]
        yb[pl.ds(2 * c, 8, stride=32), :] = jnp.where(lane < 64, tile, 0.0)
        yb[pl.ds(2 * c + 1, 8, stride=32), :] = jnp.where(lane < 64, 0.0, tile)
    send4[...] = exact_dot(twice_back, yb[...], ((1,), (1,))).reshape(8, 8, 256)
    for d in FAR_ROW:
        row_copy(send4, recv4, 3, d).start()
    recv4[me_r] = send4[me_r]
    others(recv4, rs.at[3])
    for kh in range(2):
        for h in range(2):
            v = [recv4[kh * 4 + q, :, h * 128:(h + 1) * 128] for q in range(4)]
            for p in range(4):
                tile = jnp.zeros((8, 128), f32)
                for q in range(4):
                    s = (q - p) * 32 % 128
                    tile = jnp.where(part == q, pltpu.roll(v[q], s, 1) if s else v[q], tile)
                fp[kh, pl.ds(4 * h + p, 8, stride=8), :] = tile
    out_ref[...] = exact_dot(jnp.concatenate([fp[0], fp[1]], axis=1), tz_ref[...], ((1,), (0,)))
    for k, buffer in enumerate((send1, send2, send3, send4)):
        others(buffer, ss.at[k])


def solve(heat, divergence):
    lx, ly, lz = mode_values(64), mode_values(128), mode_values(256)
    device = np.arange(128)
    lanes = np.arange(128)
    shift = screen + lx[lanes % 64][None, :] + lz[(device // 16 * 32 + device % 16 * 2)[:, None] + (lanes // 64)[None, :]]
    vm = pl.BlockSpec(memory_space=pltpu.VMEM)
    hb = pl.BlockSpec(memory_space=pl.ANY)
    dma = pltpu.SemaphoreType.DMA
    out = pl.pallas_call(
        solve_kernel,
        out_shape=jax.ShapeDtypeStruct((64, 256), f32),
        in_specs=[hb] * 7,
        out_specs=vm,
        scratch_shapes=[
            pltpu.VMEM((2, 64, 128), f32), pltpu.VMEM((64, 256), f32), pltpu.VMEM((256, 256), f32), pltpu.VMEM((64, 64), f32), pltpu.VMEM((128, 128), f32),
            pltpu.VMEM((128, 128), f32), pltpu.VMEM((128, 128), f32), dma((7,)),
            pltpu.VMEM((2, 64, 128), f32), pltpu.VMEM((8, 8, 256), f32), pltpu.VMEM((8, 8, 256), f32), pltpu.VMEM((256, 128), f32),
            pltpu.VMEM((16, 8, 128), f32), pltpu.VMEM((16, 8, 128), f32), pltpu.VMEM((16, 8, 128), f32), pltpu.VMEM((16, 8, 128), f32), pltpu.VMEM((256, 128), f32),
            pltpu.VMEM((8, 8, 256), f32), pltpu.VMEM((8, 8, 256), f32), pltpu.VMEM((2, 64, 128), f32),
            dma((4,)), dma((4,))],
        compiler_params=pltpu.CompilerParams(collective_id=1, has_side_effects=True, vmem_limit_bytes=60 << 20),
        name="screened_solve",
    )(heat, divergence.reshape(64, 256), jnp.asarray(cosine_table(256)), jnp.asarray(cosine_table(64)), jnp.asarray(cosine_table(128)),
      jnp.asarray(shift.astype(np.float32)), jnp.asarray(np.broadcast_to(ly[:, None], (128, 128)).astype(np.float32)))
    return out.reshape(8, 8, 256)


def local(species, velocity, diffusivity, divergence, log_rates, reactants, products, heat_weights, substeps):
    moved, first, second, order = advance(species, velocity, diffusivity, log_rates, reactants, products, substeps)
    reacted, heat = kinetics(16, moved, order, heat_weights, first, second)
    pressure = solve(heat, divergence)
    return reacted.reshape(species.shape), pressure


def solution(mesh):
    cells = P("row", "col", None)
    fields = P(None, "row", "col", None)
    in_specs = (fields, fields, P(), cells, P(), P(), P(), P(), cells)
    return jax.shard_map(local, mesh=mesh, in_specs=in_specs, out_specs=(fields, cells), check_vma=False)
```
